512 devices in a mesh: refl: 8 (over y), slab: 64 (over z, x, core).
Axes of the slice: x: 4, y: 8, z: 8, core: 2. Of those that a mesh axis runs over, the one named last changes fastest.
Arguments:
- detector: bfloat16 [8, 65536, 2, 128], P('refl', 'slab'), may hold values from -6 to 6
- owners: int32 [8, 65536, 1], P('refl', 'slab'), may hold values from 0 to 63; in each aligned block of 1024 rows (0 to 1023, 1024 to 2047, ..., all dimensions but the last counted through in order) at most 32 rows name the same one
- block_ids: int32 [8, 65536], P('refl', 'slab'), may hold values from 0 to 63
- kernel_ids: int32 [8, 65536], P('refl', 'slab'), may hold values from 0 to 7
- kernels: bfloat16 [8, 128, 128], replicated, may hold values from -0.5 to 0.5
- bragg_vectors: float32 [8, 3], replicated, may hold values from -3 to 3
- object_field: float32 [8, 128, 32, 2, 128], P('refl', 'slab'), may hold values from -6 to 6
Outputs:
- updated: float32 [8, 128, 32, 2, 128], P('refl', 'slab')
The draws below stay inside these ranges and needn't reach their ends.
Inputs may be any that keep to these rules, and one draw needn't show every extreme that they name: `owners`: among the tiles of one device and one reflection, at most 32 name the same owner, a bound that some block reaches.
All inputs are finite; a program needn't handle non-finite values.
Results may differ from the reference program's by a relative error of at most 0.0003.
Values may be sent and summed in bfloat16 or wider, within the bound.
A program may use at most 64 MiB of HBM per device.

```python
import math
import jax
import jax.numpy as jnp
import numpy as np
from jax import lax

TILE_W = 128
NKER = 8
TILE_DEV = 1024
CX = 2
BY = 32
NREFL = 8
TILES = 65536
CAP = 32
NX = 128
N_SLAB = 64


def plant(result, own_key, least, high):
    dims = result.shape
    index_at = [jax.random.randint(jax.random.fold_in(own_key, axis), (), 0, dims[axis]) for axis in range(len(dims))]
    result = result.at[tuple(index_at)].set(least)
    longest = dims.index(max(dims))
    index_at[longest] = (index_at[longest] + 1) % dims[longest]
    return result.at[tuple(index_at)].set(high)


def block_scale(own_key, shape, cuts, smallest, largest):
    factor_of = 1.0
    for axis_at, blocks in cuts:
        heights = jax.random.uniform(jax.random.fold_in(jax.random.fold_in(own_key, 6), axis_at), (blocks,), jnp.float32, smallest / len(cuts), largest / len(cuts))
        factor_of = factor_of * jnp.repeat(jnp.exp(heights), shape[axis_at] // blocks).reshape((-1,) + (1,) * (len(shape) - 1 - axis_at))
    return factor_of


def deal_out(rng, own, number, rows, count, top, limit, skew):
    ranking = jax.random.permutation(rng, count)
    heavy_load, ordinary = shares(count, rows * top, limit, skew, True), shares(count, rows * top, limit, skew, False)
    places = jnp.arange(count)

    def named(tallies, rotation):
        used = int((tallies > 0).sum())
        fixed = max(1, used // 4)
        moved = fixed + (places - fixed + rotation * (used - fixed)) % max(1, count - fixed)
        return jnp.zeros((count,), jnp.int32).at[ranking[jnp.where(places < fixed, places, moved)]].set(jnp.asarray(tallies, jnp.int32))

    tallies = jnp.where(number % 4 == 0, named(heavy_load, number // 4), named(ordinary, number - number // 4 - 1))
    mixed = jax.random.permutation(jax.random.fold_in(own, 3), count)
    source_of, taker = mixed[0:count // 2 * 2:2], mixed[1:count // 2 * 2:2]
    margin = jnp.minimum(tallies[source_of] - 1, limit - tallies[taker]) // 2
    margin = jnp.where((source_of == ranking[0]) | (taker == ranking[0]) | (tallies[taker] == 0), 0, jnp.maximum(margin, 0))
    moved = jax.random.randint(jax.random.fold_in(own, 4), (count // 2,), 0, 1 << 20) % (margin + 1)
    tallies = tallies.at[source_of].add(-moved).at[taker].add(moved)
    labels = jnp.searchsorted(jnp.cumsum(tallies), jnp.arange(rows * top), side="right").astype(jnp.int32)
    table = labels.reshape(top, rows).T
    table = table[jax.random.permutation(jax.random.fold_in(own, 1), rows)]
    rotation = jax.random.randint(jax.random.fold_in(own, 2), (rows, 1), 0, top)
    return jnp.take_along_axis(table, (jnp.arange(top)[None, :] + rotation) % top, axis=1)


def shares(count, total, reach, skew, full):
    portions = [(1 << 20) // math.isqrt(grade ** skew) + 1 for grade in range(1, count + 1)]
    largest = reach if full else min(reach, max(-(-total // count), total * portions[0] // sum(portions)))
    least = 1 if total - largest >= count - 1 else 0
    holding, surplus = [largest] + [least] * (count - 1), total - largest - least * (count - 1)
    while surplus > 0:
        free = [i for i in range(1, count) if holding[i] < largest] or [i for i in range(1, count) if holding[i] < reach]
        pool, remaining = sum([portions[i] for i in free]), surplus
        for i in free:
            extra = min(reach - holding[i], max(1, remaining * portions[i] // pool), surplus)
            holding[i] = holding[i] + extra
            surplus = surplus - extra
    return np.array(holding)


def scatter_about(rng, dims, width, limit, split=(), held_as=jnp.bfloat16):
    entries = jax.random.normal(rng, dims, jnp.float32) * width
    if len(split) > 0:
        entries = block_scale(rng, dims, split, -0.22, 0.18) * entries
    return jnp.clip(entries, min=-limit, max=limit).astype(held_as)


def setup_inputs(seed: int = 0) -> dict:
    keys = jax.random.split(jax.random.key(seed), 8)
    detector = scatter_about(keys[0], (NREFL, TILES, 2, TILE_W), 1.0, 6.0, ((0, 8), (1, 64)))
    owners_keys = jax.random.split(jax.random.fold_in(keys[1], 1), NREFL * TILES // TILE_DEV)
    owners_turns = jax.random.permutation(jax.random.fold_in(keys[1], 3), NREFL * TILES // TILE_DEV)
    owners = jax.vmap(lambda own, number: deal_out(jax.random.fold_in(keys[1], 2), own, number, TILE_DEV, N_SLAB, 1, CAP, 2))(owners_keys, owners_turns).reshape((NREFL, TILES, 1))
    block_ids = plant(jax.random.randint(keys[2], (NREFL, TILES), 0, CX * BY), jax.random.fold_in(keys[2], 1), 0, (CX * BY) - 1).astype(jnp.int32)
    kernel_ids = plant(jax.random.randint(keys[3], (NREFL, TILES), 0, NKER), jax.random.fold_in(keys[3], 1), 0, NKER - 1).astype(jnp.int32)
    kernels = scatter_about(keys[4], (NKER, TILE_W, TILE_W), TILE_W ** -0.5, 0.5)
    bragg_vectors = scatter_about(keys[5], (NREFL, 3), 0.5, 3.0, (), jnp.float32)
    object_field = scatter_about(keys[6], (NREFL, NX, BY, 2, TILE_W), 1.0, 6.0, ((0, 8), (1, 64)), jnp.float32)
    return {"detector": detector, "owners": owners, "block_ids": block_ids, "kernel_ids": kernel_ids, "kernels": kernels, "bragg_vectors": bragg_vectors, "object_field": object_field}


def central(field, dimension):
    widths = [(0, 0)] * field.ndim
    widths[dimension] = (1, 1)
    padded = jnp.pad(field, widths)
    length = field.shape[dimension]
    return 0.5 * (lax.slice_in_dim(padded, 2, length + 2, axis=dimension) - lax.slice_in_dim(padded, 0, length, axis=dimension))


def phase_term(obj_real, obj_imag, grad_x, grad_y, grad_z, qrow):
    term_x = obj_real * grad_x[:, :, 1] - obj_imag * grad_x[:, :, 0]
    term_y = obj_real * grad_y[:, :, 1] - obj_imag * grad_y[:, :, 0]
    term_z = obj_real * grad_z[:, :, 1] - obj_imag * grad_z[:, :, 0]
    return qrow[0] * term_x + qrow[1] * term_y + qrow[2] * term_z


def reference(detector, owners, block_ids, kernel_ids, kernels, bragg_vectors, object_field):
    refl_count = detector.shape[0]
    tile_total = detector.shape[1]
    kernel_wide = kernels.astype(jnp.float32)
    grids = []
    phases = []
    for reflection in range(refl_count):
        codes = ((owners[reflection, :, 0] * (CX * BY) + block_ids[reflection]) * NKER + kernel_ids[reflection]).astype(jnp.int32)
        values = detector[reflection].reshape(tile_total, 2 * TILE_W).astype(jnp.float32)
        summed = jax.ops.segment_sum(values, codes, num_segments=NX * BY * NKER).reshape(NX * BY, NKER, 2, TILE_W)
        gridded = jnp.einsum("bkcz,kzw->bcw", summed, kernel_wide, precision=lax.Precision.HIGHEST).reshape(NX, BY, 2, TILE_W)
        obj = object_field[reflection]
        phase = phase_term(obj[:, :, 0], obj[:, :, 1], central(gridded, 0), central(gridded, 1), central(gridded, 3), bragg_vectors[reflection])
        grids.append(gridded)
        phases.append(phase)
    total = jnp.zeros((3,) + phases[0].shape, jnp.float32)
    for reflection in range(refl_count):
        total = total + bragg_vectors[reflection][:, None, None, None] * phases[reflection][None]
    results = []
    for reflection in range(refl_count):
        matched = reflection + 1 - 2 * (reflection % 2)
        diff = bragg_vectors[reflection] - bragg_vectors[matched]
        shift = diff[0] * total[0] + diff[1] * total[1] + diff[2] * total[2]
        obj = object_field[reflection]
        gridded = grids[reflection]
        new_real = obj[:, :, 0] - 0.5 * (gridded[:, :, 0] - obj[:, :, 1] * shift)
        new_imag = obj[:, :, 1] - 0.5 * (gridded[:, :, 1] + obj[:, :, 0] * shift)
        results.append(jnp.stack([new_real, new_imag], axis=2))
    return jnp.stack(results, axis=0)
```

```python
import jax
import jax.numpy as jnp
from jax import lax
from jax.sharding import PartitionSpec as P


def extended(block, sides, width):
    for axis, dim in sides:
        count = lax.axis_size(axis)
        forward = [(i, i + 1) for i in range(count - 1)]
        backward = [(target, source) for source, target in forward]
        low = lax.ppermute(
            lax.slice_in_dim(block, block.shape[dim] - width, None, axis=dim), axis, forward
        )
        high = lax.ppermute(lax.slice_in_dim(block, 0, width, axis=dim), axis, backward)
        block = jnp.concatenate([low, block, high], axis=dim)
    return block


def central(field, dimension):
    widths = [(0, 0)] * field.ndim
    widths[dimension] = (1, 1)
    padded = jnp.pad(field, widths)
    length = field.shape[dimension]
    return 0.5 * (
        lax.slice_in_dim(padded, 2, length + 2, axis=dimension)
        - lax.slice_in_dim(padded, 0, length, axis=dimension)
    )


def phase_term(obj_real, obj_imag, grad_x, grad_y, grad_z, qrow):
    term_x = obj_real * grad_x[:, :, 1] - obj_imag * grad_x[:, :, 0]
    term_y = obj_real * grad_y[:, :, 1] - obj_imag * grad_y[:, :, 0]
    term_z = obj_real * grad_z[:, :, 1] - obj_imag * grad_z[:, :, 0]
    return qrow[0] * term_x + qrow[1] * term_y + qrow[2] * term_z


def butterfly_sum(value, axis):
    count = lax.axis_size(axis)
    distance = 1
    while distance < count:
        pairs = [(i, i ^ distance) for i in range(count)]
        value = value + lax.ppermute(value, axis, pairs)
        distance *= 2
    return value


def per_device(detector, owners, block_ids, kernel_ids, kernels, bragg_vectors, object_field):
    slab_count = lax.axis_size("slab")
    plane_count = object_field.shape[1]
    row_count = object_field.shape[2]
    block_count = plane_count * row_count
    kernel_count = kernels.shape[0]
    tile_count = detector.shape[1]
    tile_width = detector.shape[3]
    row_width = 2 * tile_width
    capacity = 2 * tile_count // slab_count
    values = detector[0].reshape(tile_count, row_width)
    owner = owners[0, :, 0]
    order = lax.broadcasted_iota(jnp.int32, (tile_count, tile_count), 1) < lax.broadcasted_iota(
        jnp.int32, (tile_count, tile_count), 0
    )
    same = (owner[:, None] == owner[None, :]) & order
    slots = jnp.sum(same.astype(jnp.int32), axis=1)
    flat_slot = owner * capacity + slots
    placed = (
        flat_slot[None, :] == lax.broadcasted_iota(jnp.int32, (slab_count * capacity, tile_count), 0)
    ).astype(jnp.bfloat16)
    lane = lax.broadcasted_iota(jnp.int32, (tile_count, 128), 1)
    extra = jnp.where(
        lane == 0, block_ids[0][:, None], jnp.where(lane == 1, kernel_ids[0][:, None], 0)
    ).astype(jnp.bfloat16)
    table = jnp.concatenate([values, extra], axis=1)
    sent = jnp.dot(placed, table, preferred_element_type=jnp.float32)
    sent = sent.reshape(slab_count, capacity, row_width + 128)
    data = sent[:, :, :row_width].astype(jnp.bfloat16).reshape(slab_count, capacity * row_width)
    code_rows = jnp.concatenate(
        [sent[:, :, row_width], sent[:, :, row_width + 1], jnp.zeros((slab_count, 128 - 2 * capacity), jnp.float32)],
        axis=1,
    ).astype(jnp.bfloat16)
    packet = jnp.concatenate([data, code_rows], axis=1)
    got = lax.all_to_all(packet, "slab", split_axis=0, concat_axis=0, tiled=True)
    row_total = slab_count * capacity
    rows = got[:, : capacity * row_width].reshape(row_total, row_width)
    got_blocks = got[:, capacity * row_width : capacity * row_width + capacity].astype(jnp.int32)
    got_kernels = got[
        :, capacity * row_width + capacity : capacity * row_width + 2 * capacity
    ].astype(jnp.int32)
    got_codes = (got_blocks * kernel_count + got_kernels).reshape(row_total)
    chosen = (
        got_codes[None, :]
        == lax.broadcasted_iota(jnp.int32, (block_count * kernel_count, row_total), 0)
    ).astype(jnp.bfloat16)
    summed = jnp.dot(chosen, rows, preferred_element_type=jnp.float32)
    summed = summed.reshape(block_count, kernel_count, 2, tile_width).transpose(0, 2, 1, 3)
    gridded = jnp.dot(
        summed.reshape(block_count * 2, kernel_count * tile_width),
        kernels.astype(jnp.float32).reshape(kernel_count * tile_width, tile_width),
        precision=lax.Precision.HIGHEST,
        preferred_element_type=jnp.float32,
    )
    gridded = gridded.reshape(plane_count, row_count, 2, tile_width)
    padded = extended(gridded, (("slab", 0),), 1)
    grad_x = 0.5 * (padded[2:] - padded[:-2])
    grad_y = central(gridded, 1)
    grad_z = central(gridded, 3)
    refl_count = bragg_vectors.shape[0]
    places = jnp.arange(refl_count, dtype=jnp.int32)
    my_refl = lax.axis_index("refl")
    q_self = jnp.sum(jnp.where((places == my_refl)[:, None], bragg_vectors, 0.0), axis=0)
    mate = my_refl + 1 - 2 * (my_refl % 2)
    q_other = jnp.sum(jnp.where((places == mate)[:, None], bragg_vectors, 0.0), axis=0)
    obj = object_field[0]
    obj_real = obj[:, :, 0]
    obj_imag = obj[:, :, 1]
    phase = phase_term(obj_real, obj_imag, grad_x, grad_y, grad_z, q_self)
    diff = q_self - q_other
    total = butterfly_sum(q_self[:, None, None, None] * phase[None], "refl")
    shift = diff[0] * total[0] + diff[1] * total[1] + diff[2] * total[2]
    new_real = obj_real - 0.5 * (gridded[:, :, 0] - obj_imag * shift)
    new_imag = obj_imag - 0.5 * (gridded[:, :, 1] + obj_real * shift)
    return jnp.stack([new_real, new_imag], axis=2)[None]


def solution(mesh):
    in_specs = (
        P("refl", "slab", None, None),
        P("refl", "slab", None),
        P("refl", "slab"),
        P("refl", "slab"),
        P(),
        P(),
        P("refl", "slab", None, None, None),
    )
    out_specs = P("refl", "slab", None, None, None)
    return jax.shard_map(
        per_device, mesh=mesh, in_specs=in_specs, out_specs=out_specs, check_vma=False
    )
```

```python
import jax
import jax.numpy as jnp
from jax import lax
from jax.experimental import pallas as pl
from jax.experimental.pallas import tpu as pltpu
from jax.sharding import PartitionSpec as P

MESH = pl.DeviceIdType.MESH


def extended(block, sides, width):
    for axis, dim in sides:
        count = lax.axis_size(axis)
        forward = [(i, i + 1) for i in range(count - 1)]
        backward = [(target, source) for source, target in forward]
        low = lax.ppermute(
            lax.slice_in_dim(block, block.shape[dim] - width, None, axis=dim), axis, forward
        )
        high = lax.ppermute(lax.slice_in_dim(block, 0, width, axis=dim), axis, backward)
        block = jnp.concatenate([low, block, high], axis=dim)
    return block


def central(field, dimension):
    widths = [(0, 0)] * field.ndim
    widths[dimension] = (1, 1)
    padded = jnp.pad(field, widths)
    length = field.shape[dimension]
    return 0.5 * (
        lax.slice_in_dim(padded, 2, length + 2, axis=dimension)
        - lax.slice_in_dim(padded, 0, length, axis=dimension)
    )


def phase_term(obj_real, obj_imag, grad_x, grad_y, grad_z, qrow):
    term_x = obj_real * grad_x[:, :, 1] - obj_imag * grad_x[:, :, 0]
    term_y = obj_real * grad_y[:, :, 1] - obj_imag * grad_y[:, :, 0]
    term_z = obj_real * grad_z[:, :, 1] - obj_imag * grad_z[:, :, 0]
    return qrow[0] * term_x + qrow[1] * term_y + qrow[2] * term_z


def gather_kernel(phase_ref, out_ref, send_sem, recv_sem):
    count = out_ref.shape[0]
    me = lax.axis_index("refl")
    slab = lax.axis_index("slab")
    barrier = pltpu.get_barrier_semaphore()
    for step in range(1, count):
        peer = lax.rem(me + step, count)
        pl.semaphore_signal(barrier, 1, device_id=(peer, slab), device_id_type=MESH)
    pl.semaphore_wait(barrier, count - 1)
    copies = []
    for step in range(1, count):
        peer = lax.rem(me + step, count)
        copy = pltpu.make_async_remote_copy(
            src_ref=phase_ref,
            dst_ref=out_ref.at[me],
            send_sem=send_sem.at[step],
            recv_sem=recv_sem.at[step],
            device_id=(peer, slab),
            device_id_type=MESH,
        )
        copy.start()
        copies.append(copy)
    out_ref[me] = phase_ref[...]
    for copy in copies:
        copy.wait_send()
    for step in range(1, count):
        source = lax.rem(me + count - step, count)
        pltpu.make_async_remote_copy(
            src_ref=phase_ref,
            dst_ref=out_ref.at[source],
            send_sem=send_sem.at[step],
            recv_sem=recv_sem.at[step],
            device_id=(source, slab),
            device_id_type=MESH,
        ).wait_recv()


def gather_refl(phase, count):
    return pl.pallas_call(
        gather_kernel,
        out_shape=jax.ShapeDtypeStruct((count,) + phase.shape, phase.dtype),
        in_specs=[pl.BlockSpec(memory_space=pltpu.VMEM)],
        out_specs=pl.BlockSpec(memory_space=pltpu.VMEM),
        scratch_shapes=[pltpu.SemaphoreType.DMA((count,)), pltpu.SemaphoreType.DMA((count,))],
        compiler_params=pltpu.CompilerParams(collective_id=0, has_side_effects=True),
    )(phase)


def per_device(detector, owners, block_ids, kernel_ids, kernels, bragg_vectors, object_field):
    slab_count = lax.axis_size("slab")
    plane_count = object_field.shape[1]
    row_count = object_field.shape[2]
    block_count = plane_count * row_count
    kernel_count = kernels.shape[0]
    tile_count = detector.shape[1]
    tile_width = detector.shape[3]
    row_width = 2 * tile_width
    capacity = 2 * tile_count // slab_count
    values = detector[0].reshape(tile_count, row_width)
    owner = owners[0, :, 0]
    order = lax.broadcasted_iota(jnp.int32, (tile_count, tile_count), 1) < lax.broadcasted_iota(
        jnp.int32, (tile_count, tile_count), 0
    )
    same = (owner[:, None] == owner[None, :]) & order
    slots = jnp.sum(same.astype(jnp.int32), axis=1)
    flat_slot = owner * capacity + slots
    placed = (
        flat_slot[None, :] == lax.broadcasted_iota(jnp.int32, (slab_count * capacity, tile_count), 0)
    ).astype(jnp.bfloat16)
    lane = lax.broadcasted_iota(jnp.int32, (tile_count, 128), 1)
    extra = jnp.where(
        lane == 0, block_ids[0][:, None], jnp.where(lane == 1, kernel_ids[0][:, None], 0)
    ).astype(jnp.bfloat16)
    table = jnp.concatenate([values, extra], axis=1)
    sent = jnp.dot(placed, table, preferred_element_type=jnp.float32)
    sent = sent.reshape(slab_count, capacity, row_width + 128)
    data = sent[:, :, :row_width].astype(jnp.bfloat16).reshape(slab_count, capacity * row_width)
    code_rows = jnp.concatenate(
        [sent[:, :, row_width], sent[:, :, row_width + 1], jnp.zeros((slab_count, 128 - 2 * capacity), jnp.float32)],
        axis=1,
    ).astype(jnp.bfloat16)
    packet = jnp.concatenate([data, code_rows], axis=1)
    got = lax.all_to_all(packet, "slab", split_axis=0, concat_axis=0, tiled=True)
    row_total = slab_count * capacity
    rows = got[:, : capacity * row_width].reshape(row_total, row_width)
    got_blocks = got[:, capacity * row_width : capacity * row_width + capacity].astype(jnp.int32)
    got_kernels = got[
        :, capacity * row_width + capacity : capacity * row_width + 2 * capacity
    ].astype(jnp.int32)
    got_codes = (got_blocks * kernel_count + got_kernels).reshape(row_total)
    chosen = (
        got_codes[None, :]
        == lax.broadcasted_iota(jnp.int32, (block_count * kernel_count, row_total), 0)
    ).astype(jnp.bfloat16)
    summed = jnp.dot(chosen, rows, preferred_element_type=jnp.float32)
    summed = summed.reshape(block_count, kernel_count, 2, tile_width).transpose(0, 2, 1, 3)
    gridded = jnp.dot(
        summed.reshape(block_count * 2, kernel_count * tile_width),
        kernels.astype(jnp.float32).reshape(kernel_count * tile_width, tile_width),
        precision=lax.Precision.HIGHEST,
        preferred_element_type=jnp.float32,
    )
    gridded = gridded.reshape(plane_count, row_count, 2, tile_width)
    padded = extended(gridded, (("slab", 0),), 1)
    grad_x = 0.5 * (padded[2:] - padded[:-2])
    grad_y = central(gridded, 1)
    grad_z = central(gridded, 3)
    refl_count = bragg_vectors.shape[0]
    places = jnp.arange(refl_count, dtype=jnp.int32)
    my_refl = lax.axis_index("refl")
    q_self = jnp.sum(jnp.where((places == my_refl)[:, None], bragg_vectors, 0.0), axis=0)
    mate = my_refl + 1 - 2 * (my_refl % 2)
    q_other = jnp.sum(jnp.where((places == mate)[:, None], bragg_vectors, 0.0), axis=0)
    obj = object_field[0]
    obj_real = obj[:, :, 0]
    obj_imag = obj[:, :, 1]
    phase = phase_term(obj_real, obj_imag, grad_x, grad_y, grad_z, q_self)
    diff = q_self - q_other
    gathered = gather_refl(phase.reshape(plane_count * row_count, tile_width), refl_count)
    weights = jnp.sum(bragg_vectors * diff[None, :], axis=1)
    shift = jnp.sum(weights[:, None, None] * gathered, axis=0).reshape(plane_count, row_count, tile_width)
    new_real = obj_real - 0.5 * (gridded[:, :, 0] - obj_imag * shift)
    new_imag = obj_imag - 0.5 * (gridded[:, :, 1] + obj_real * shift)
    return jnp.stack([new_real, new_imag], axis=2)[None]


def solution(mesh):
    in_specs = (
        P("refl", "slab", None, None),
        P("refl", "slab", None),
        P("refl", "slab"),
        P("refl", "slab"),
        P(),
        P(),
        P("refl", "slab", None, None, None),
    )
    out_specs = P("refl", "slab", None, None, None)
    return jax.shard_map(
        per_device, mesh=mesh, in_specs=in_specs, out_specs=out_specs, check_vma=False
    )
```

```python
import jax
import jax.numpy as jnp
from jax import lax
from jax.experimental import pallas as pl
from jax.experimental.pallas import tpu as pltpu
from jax.sharding import PartitionSpec as P

MESH = pl.DeviceIdType.MESH


def extended(block, sides, width):
    for axis, dim in sides:
        count = lax.axis_size(axis)
        forward = [(i, i + 1) for i in range(count - 1)]
        backward = [(target, source) for source, target in forward]
        low = lax.ppermute(
            lax.slice_in_dim(block, block.shape[dim] - width, None, axis=dim), axis, forward
        )
        high = lax.ppermute(lax.slice_in_dim(block, 0, width, axis=dim), axis, backward)
        block = jnp.concatenate([low, block, high], axis=dim)
    return block


def central(field, dimension):
    widths = [(0, 0)] * field.ndim
    widths[dimension] = (1, 1)
    padded = jnp.pad(field, widths)
    length = field.shape[dimension]
    return 0.5 * (
        lax.slice_in_dim(padded, 2, length + 2, axis=dimension)
        - lax.slice_in_dim(padded, 0, length, axis=dimension)
    )


def phase_term(obj_real, obj_imag, grad_x, grad_y, grad_z, qrow):
    term_x = obj_real * grad_x[:, :, 1] - obj_imag * grad_x[:, :, 0]
    term_y = obj_real * grad_y[:, :, 1] - obj_imag * grad_y[:, :, 0]
    term_z = obj_real * grad_z[:, :, 1] - obj_imag * grad_z[:, :, 0]
    return qrow[0] * term_x + qrow[1] * term_y + qrow[2] * term_z


def gather_kernel(phase_ref, out_ref, send_sem, recv_sem):
    count = out_ref.shape[0]
    me = lax.axis_index("refl")
    slab = lax.axis_index("slab")
    barrier = pltpu.get_barrier_semaphore()
    for step in range(1, count):
        peer = lax.rem(me + step, count)
        pl.semaphore_signal(barrier, 1, device_id=(peer, slab), device_id_type=MESH)
    pl.semaphore_wait(barrier, count - 1)
    copies = []
    for step in range(1, count):
        peer = lax.rem(me + step, count)
        copy = pltpu.make_async_remote_copy(
            src_ref=phase_ref,
            dst_ref=out_ref.at[me],
            send_sem=send_sem.at[step],
            recv_sem=recv_sem.at[step],
            device_id=(peer, slab),
            device_id_type=MESH,
        )
        copy.start()
        copies.append(copy)
    out_ref[me] = phase_ref[...]
    for copy in copies:
        copy.wait_send()
    for step in range(1, count):
        source = lax.rem(me + count - step, count)
        pltpu.make_async_remote_copy(
            src_ref=phase_ref,
            dst_ref=out_ref.at[source],
            send_sem=send_sem.at[step],
            recv_sem=recv_sem.at[step],
            device_id=(source, slab),
            device_id_type=MESH,
        ).wait_recv()


def gather_refl(phase, count):
    return pl.pallas_call(
        gather_kernel,
        out_shape=jax.ShapeDtypeStruct((count,) + phase.shape, phase.dtype),
        in_specs=[pl.BlockSpec(memory_space=pltpu.VMEM)],
        out_specs=pl.BlockSpec(memory_space=pltpu.VMEM),
        scratch_shapes=[pltpu.SemaphoreType.DMA((count,)), pltpu.SemaphoreType.DMA((count,))],
        compiler_params=pltpu.CompilerParams(collective_id=0, has_side_effects=True),
    )(phase)


def exchange_kernel(packet_ref, out_ref, send_sem, recv_sem):
    count = packet_ref.shape[0]
    me = lax.axis_index("slab")
    refl = lax.axis_index("refl")
    barrier = pltpu.get_barrier_semaphore()

    def greet(step, carry):
        peer = lax.rem(me + step, count)
        pl.semaphore_signal(barrier, 1, device_id=(refl, peer), device_id_type=MESH)
        return carry

    lax.fori_loop(1, count, greet, 0)
    pl.semaphore_wait(barrier, count - 1)

    def outgoing(step):
        peer = lax.rem(me + step, count)
        return pltpu.make_async_remote_copy(
            src_ref=packet_ref.at[peer],
            dst_ref=out_ref.at[me],
            send_sem=send_sem.at[step],
            recv_sem=recv_sem.at[step],
            device_id=(refl, peer),
            device_id_type=MESH,
        )

    def incoming(step):
        source = lax.rem(me + count - step, count)
        return pltpu.make_async_remote_copy(
            src_ref=packet_ref.at[source],
            dst_ref=out_ref.at[source],
            send_sem=send_sem.at[step],
            recv_sem=recv_sem.at[step],
            device_id=(refl, source),
            device_id_type=MESH,
        )

    def send(step, carry):
        outgoing(step).start()
        return carry

    lax.fori_loop(1, count, send, 0)
    out_ref[me] = packet_ref[me]

    def finish(step, carry):
        outgoing(step).wait_send()
        incoming(step).wait_recv()
        return carry

    lax.fori_loop(1, count, finish, 0)


def exchange_slab(packet):
    count = packet.shape[0]
    return pl.pallas_call(
        exchange_kernel,
        out_shape=jax.ShapeDtypeStruct(packet.shape, packet.dtype),
        in_specs=[pl.BlockSpec(memory_space=pltpu.VMEM)],
        out_specs=pl.BlockSpec(memory_space=pltpu.VMEM),
        scratch_shapes=[pltpu.SemaphoreType.DMA((count,)), pltpu.SemaphoreType.DMA((count,))],
        compiler_params=pltpu.CompilerParams(collective_id=1, has_side_effects=True),
    )(packet)


def per_device(detector, owners, block_ids, kernel_ids, kernels, bragg_vectors, object_field):
    slab_count = lax.axis_size("slab")
    plane_count = object_field.shape[1]
    row_count = object_field.shape[2]
    block_count = plane_count * row_count
    kernel_count = kernels.shape[0]
    tile_count = detector.shape[1]
    tile_width = detector.shape[3]
    row_width = 2 * tile_width
    capacity = 2 * tile_count // slab_count
    values = detector[0].reshape(tile_count, row_width)
    owner = owners[0, :, 0]
    order = lax.broadcasted_iota(jnp.int32, (tile_count, tile_count), 1) < lax.broadcasted_iota(
        jnp.int32, (tile_count, tile_count), 0
    )
    same = (owner[:, None] == owner[None, :]) & order
    slots = jnp.sum(same.astype(jnp.int32), axis=1)
    flat_slot = owner * capacity + slots
    placed = (
        flat_slot[None, :] == lax.broadcasted_iota(jnp.int32, (slab_count * capacity, tile_count), 0)
    ).astype(jnp.bfloat16)
    lane = lax.broadcasted_iota(jnp.int32, (tile_count, 128), 1)
    extra = jnp.where(
        lane == 0, block_ids[0][:, None], jnp.where(lane == 1, kernel_ids[0][:, None], 0)
    ).astype(jnp.bfloat16)
    table = jnp.concatenate([values, extra], axis=1)
    sent = jnp.dot(placed, table, preferred_element_type=jnp.float32)
    sent = sent.reshape(slab_count, capacity, row_width + 128)
    data = sent[:, :, :row_width].astype(jnp.bfloat16).reshape(slab_count, 2 * capacity, tile_width)
    code_rows = jnp.concatenate(
        [sent[:, :, row_width], sent[:, :, row_width + 1], jnp.zeros((slab_count, tile_width - 2 * capacity), jnp.float32)],
        axis=1,
    ).astype(jnp.bfloat16)
    code_pad = jnp.zeros((slab_count, 15, tile_width), jnp.bfloat16)
    packet = jnp.concatenate([data, code_rows[:, None, :], code_pad], axis=1)
    got = exchange_slab(packet)
    row_total = slab_count * capacity
    rows = got[:, : 2 * capacity].reshape(row_total, row_width)
    got_blocks = got[:, 2 * capacity, :capacity].astype(jnp.int32)
    got_kernels = got[:, 2 * capacity, capacity : 2 * capacity].astype(jnp.int32)
    got_codes = (got_blocks * kernel_count + got_kernels).reshape(row_total)
    chosen = (
        got_codes[None, :]
        == lax.broadcasted_iota(jnp.int32, (block_count * kernel_count, row_total), 0)
    ).astype(jnp.bfloat16)
    summed = jnp.dot(chosen, rows, preferred_element_type=jnp.float32)
    summed = summed.reshape(block_count, kernel_count, 2, tile_width).transpose(0, 2, 1, 3)
    gridded = jnp.dot(
        summed.reshape(block_count * 2, kernel_count * tile_width),
        kernels.astype(jnp.float32).reshape(kernel_count * tile_width, tile_width),
        precision=lax.Precision.HIGHEST,
        preferred_element_type=jnp.float32,
    )
    gridded = gridded.reshape(plane_count, row_count, 2, tile_width)
    padded = extended(gridded, (("slab", 0),), 1)
    grad_x = 0.5 * (padded[2:] - padded[:-2])
    grad_y = central(gridded, 1)
    grad_z = central(gridded, 3)
    refl_count = bragg_vectors.shape[0]
    places = jnp.arange(refl_count, dtype=jnp.int32)
    my_refl = lax.axis_index("refl")
    q_self = jnp.sum(jnp.where((places == my_refl)[:, None], bragg_vectors, 0.0), axis=0)
    mate = my_refl + 1 - 2 * (my_refl % 2)
    q_other = jnp.sum(jnp.where((places == mate)[:, None], bragg_vectors, 0.0), axis=0)
    obj = object_field[0]
    obj_real = obj[:, :, 0]
    obj_imag = obj[:, :, 1]
    phase = phase_term(obj_real, obj_imag, grad_x, grad_y, grad_z, q_self)
    diff = q_self - q_other
    gathered = gather_refl(phase.reshape(plane_count * row_count, tile_width), refl_count)
    weights = jnp.sum(bragg_vectors * diff[None, :], axis=1)
    shift = jnp.sum(weights[:, None, None] * gathered, axis=0).reshape(plane_count, row_count, tile_width)
    new_real = obj_real - 0.5 * (gridded[:, :, 0] - obj_imag * shift)
    new_imag = obj_imag - 0.5 * (gridded[:, :, 1] + obj_real * shift)
    return jnp.stack([new_real, new_imag], axis=2)[None]


def solution(mesh):
    in_specs = (
        P("refl", "slab", None, None),
        P("refl", "slab", None),
        P("refl", "slab"),
        P("refl", "slab"),
        P(),
        P(),
        P("refl", "slab", None, None, None),
    )
    out_specs = P("refl", "slab", None, None, None)
    return jax.shard_map(
        per_device, mesh=mesh, in_specs=in_specs, out_specs=out_specs, check_vma=False
    )
```

```python
import jax
import jax.numpy as jnp
from jax import lax
from jax.experimental import pallas as pl
from jax.experimental.pallas import tpu as pltpu
from jax.sharding import PartitionSpec as P

MESH = pl.DeviceIdType.MESH


def extended(block, sides, width):
    for axis, dim in sides:
        count = lax.axis_size(axis)
        forward = [(i, i + 1) for i in range(count - 1)]
        backward = [(target, source) for source, target in forward]
        low = lax.ppermute(
            lax.slice_in_dim(block, block.shape[dim] - width, None, axis=dim), axis, forward
        )
        high = lax.ppermute(lax.slice_in_dim(block, 0, width, axis=dim), axis, backward)
        block = jnp.concatenate([low, block, high], axis=dim)
    return block


def central(field, dimension):
    widths = [(0, 0)] * field.ndim
    widths[dimension] = (1, 1)
    padded = jnp.pad(field, widths)
    length = field.shape[dimension]
    return 0.5 * (
        lax.slice_in_dim(padded, 2, length + 2, axis=dimension)
        - lax.slice_in_dim(padded, 0, length, axis=dimension)
    )


def phase_term(obj_real, obj_imag, grad_x, grad_y, grad_z, qrow):
    term_x = obj_real * grad_x[:, :, 1] - obj_imag * grad_x[:, :, 0]
    term_y = obj_real * grad_y[:, :, 1] - obj_imag * grad_y[:, :, 0]
    term_z = obj_real * grad_z[:, :, 1] - obj_imag * grad_z[:, :, 0]
    return qrow[0] * term_x + qrow[1] * term_y + qrow[2] * term_z


def gather_kernel(phase_ref, out_ref, send_sem, recv_sem):
    count = out_ref.shape[0]
    me = lax.axis_index("refl")
    slab = lax.axis_index("slab")
    barrier = pltpu.get_barrier_semaphore()
    for step in range(1, count):
        peer = lax.rem(me + step, count)
        pl.semaphore_signal(barrier, 1, device_id=(peer, slab), device_id_type=MESH)
    pl.semaphore_wait(barrier, count - 1)
    copies = []
    for step in range(1, count):
        peer = lax.rem(me + step, count)
        copy = pltpu.make_async_remote_copy(
            src_ref=phase_ref,
            dst_ref=out_ref.at[me],
            send_sem=send_sem.at[step],
            recv_sem=recv_sem.at[step],
            device_id=(peer, slab),
            device_id_type=MESH,
        )
        copy.start()
        copies.append(copy)
    out_ref[me] = phase_ref[...]
    for copy in copies:
        copy.wait_send()
    for step in range(1, count):
        source = lax.rem(me + count - step, count)
        pltpu.make_async_remote_copy(
            src_ref=phase_ref,
            dst_ref=out_ref.at[source],
            send_sem=send_sem.at[step],
            recv_sem=recv_sem.at[step],
            device_id=(source, slab),
            device_id_type=MESH,
        ).wait_recv()


def gather_refl(phase, count):
    return pl.pallas_call(
        gather_kernel,
        out_shape=jax.ShapeDtypeStruct((count,) + phase.shape, phase.dtype),
        in_specs=[pl.BlockSpec(memory_space=pltpu.VMEM)],
        out_specs=pl.BlockSpec(memory_space=pltpu.VMEM),
        scratch_shapes=[pltpu.SemaphoreType.DMA((count,)), pltpu.SemaphoreType.DMA((count,))],
        compiler_params=pltpu.CompilerParams(collective_id=0, has_side_effects=True),
    )(phase)


def exchange_kernel(
    slot_ref, values_ref, ids_ref, data_out, code_out,
    data_buf, code_buf, data_send, data_recv, code_send, code_recv,
):
    count, capacity = data_out.shape[0], data_out.shape[1]
    group = 8 if count >= 16 else count // 2
    groups = count // group
    rows = group * capacity
    me = lax.axis_index("slab")
    refl = lax.axis_index("refl")
    barrier = pltpu.get_barrier_semaphore()

    def greet(step, carry):
        peer = lax.rem(me + step, count)
        pl.semaphore_signal(barrier, 1, device_id=(refl, peer), device_id_type=MESH)
        return carry

    lax.fori_loop(1, count, greet, 0)

    def pack(g):
        target = lax.broadcasted_iota(jnp.int32, (rows, slot_ref.shape[1]), 0) + g * rows
        chosen = (slot_ref[...] == target).astype(jnp.bfloat16)
        sent = jnp.dot(chosen, values_ref[...], preferred_element_type=jnp.float32)
        data_buf[pl.ds(g * group, group)] = sent.astype(jnp.bfloat16).reshape(
            group, capacity, sent.shape[1]
        )
        codes = lax.dot_general(
            ids_ref[...], chosen, (((1,), (1,)), ((), ())), preferred_element_type=jnp.float32
        ).astype(jnp.bfloat16)
        for part in range(group):
            window = (part * capacity) // 128
            code_buf[g * group + part] = codes[:, window * 128 : (window + 1) * 128]

    def outgoing(d):
        data = pltpu.make_async_remote_copy(
            src_ref=data_buf.at[d], dst_ref=data_out.at[me], send_sem=data_send.at[d],
            recv_sem=data_recv.at[me], device_id=(refl, d), device_id_type=MESH,
        )
        code = pltpu.make_async_remote_copy(
            src_ref=code_buf.at[d], dst_ref=code_out.at[me], send_sem=code_send.at[d],
            recv_sem=code_recv.at[me], device_id=(refl, d), device_id_type=MESH,
        )
        return data, code

    def incoming(s):
        data = pltpu.make_async_remote_copy(
            src_ref=data_buf.at[s], dst_ref=data_out.at[s], send_sem=data_send.at[s],
            recv_sem=data_recv.at[s], device_id=(refl, s), device_id_type=MESH,
        )
        code = pltpu.make_async_remote_copy(
            src_ref=code_buf.at[s], dst_ref=code_out.at[s], send_sem=code_send.at[s],
            recv_sem=code_recv.at[s], device_id=(refl, s), device_id_type=MESH,
        )
        return data, code

    def send(g):
        for part in range(group):
            d = g * group + part

            @pl.when(d != me)
            def _():
                data, code = outgoing(d)
                data.start()
                code.start()

    home = me // group
    pack(home)
    pl.semaphore_wait(barrier, count - 1)
    send(home)

    def later(j, carry):
        g = lax.rem(home + j, groups)
        pack(g)
        send(g)
        return carry

    lax.fori_loop(1, groups, later, 0)
    data_out[me] = data_buf[me]
    code_out[me] = code_buf[me]

    def finish(step, carry):
        data, code = outgoing(lax.rem(me + step, count))
        data.wait_send()
        code.wait_send()
        data, code = incoming(lax.rem(me + count - step, count))
        data.wait_recv()
        code.wait_recv()
        return carry

    lax.fori_loop(1, count, finish, 0)


def exchange_slab(flat_slot, values, ids, count, capacity):
    data_shape = (count, capacity, values.shape[1])
    code_shape = (count, ids.shape[0], 128)
    return pl.pallas_call(
        exchange_kernel,
        out_shape=(
            jax.ShapeDtypeStruct(data_shape, jnp.bfloat16),
            jax.ShapeDtypeStruct(code_shape, jnp.bfloat16),
        ),
        in_specs=[pl.BlockSpec(memory_space=pltpu.VMEM)] * 3,
        out_specs=(pl.BlockSpec(memory_space=pltpu.VMEM), pl.BlockSpec(memory_space=pltpu.VMEM)),
        scratch_shapes=[
            pltpu.VMEM(data_shape, jnp.bfloat16),
            pltpu.VMEM(code_shape, jnp.bfloat16),
            pltpu.SemaphoreType.DMA((count,)),
            pltpu.SemaphoreType.DMA((count,)),
            pltpu.SemaphoreType.DMA((count,)),
            pltpu.SemaphoreType.DMA((count,)),
        ],
        compiler_params=pltpu.CompilerParams(collective_id=1, has_side_effects=True),
    )(flat_slot, values, ids)


def per_device(detector, owners, block_ids, kernel_ids, kernels, bragg_vectors, object_field):
    slab_count = lax.axis_size("slab")
    plane_count = object_field.shape[1]
    row_count = object_field.shape[2]
    block_count = plane_count * row_count
    kernel_count = kernels.shape[0]
    tile_count = detector.shape[1]
    tile_width = detector.shape[3]
    row_width = 2 * tile_width
    capacity = 2 * tile_count // slab_count
    values = detector[0].reshape(tile_count, row_width)
    owner = owners[0, :, 0]
    order = lax.broadcasted_iota(jnp.int32, (tile_count, tile_count), 1) < lax.broadcasted_iota(
        jnp.int32, (tile_count, tile_count), 0
    )
    same = (owner[:, None] == owner[None, :]) & order
    slots = jnp.sum(same.astype(jnp.int32), axis=1)
    flat_slot = owner * capacity + slots
    ids = jnp.concatenate(
        [block_ids, kernel_ids, jnp.zeros((14, tile_count), jnp.int32)], axis=0
    ).astype(jnp.bfloat16)
    got, got_code = exchange_slab(flat_slot[None, :], values, ids, slab_count, capacity)
    row_total = slab_count * capacity
    rows = got.reshape(row_total, row_width)
    offset = lax.rem(lax.axis_index("slab"), 4) * capacity
    got_blocks = lax.dynamic_slice_in_dim(got_code[:, 0, :], offset, capacity, axis=1).astype(jnp.int32)
    got_kernels = lax.dynamic_slice_in_dim(got_code[:, 1, :], offset, capacity, axis=1).astype(jnp.int32)
    got_codes = (got_blocks * kernel_count + got_kernels).reshape(row_total)
    chosen = (
        got_codes[None, :]
        == lax.broadcasted_iota(jnp.int32, (block_count * kernel_count, row_total), 0)
    ).astype(jnp.bfloat16)
    summed = jnp.dot(chosen, rows, preferred_element_type=jnp.float32)
    summed = summed.reshape(block_count, kernel_count, 2, tile_width).transpose(0, 2, 1, 3)
    gridded = jnp.dot(
        summed.reshape(block_count * 2, kernel_count * tile_width),
        kernels.astype(jnp.float32).reshape(kernel_count * tile_width, tile_width),
        precision=lax.Precision.HIGHEST,
        preferred_element_type=jnp.float32,
    )
    gridded = gridded.reshape(plane_count, row_count, 2, tile_width)
    padded = extended(gridded, (("slab", 0),), 1)
    grad_x = 0.5 * (padded[2:] - padded[:-2])
    grad_y = central(gridded, 1)
    grad_z = central(gridded, 3)
    refl_count = bragg_vectors.shape[0]
    places = jnp.arange(refl_count, dtype=jnp.int32)
    my_refl = lax.axis_index("refl")
    q_self = jnp.sum(jnp.where((places == my_refl)[:, None], bragg_vectors, 0.0), axis=0)
    mate = my_refl + 1 - 2 * (my_refl % 2)
    q_other = jnp.sum(jnp.where((places == mate)[:, None], bragg_vectors, 0.0), axis=0)
    obj = object_field[0]
    obj_real = obj[:, :, 0]
    obj_imag = obj[:, :, 1]
    phase = phase_term(obj_real, obj_imag, grad_x, grad_y, grad_z, q_self)
    diff = q_self - q_other
    gathered = gather_refl(phase.reshape(plane_count * row_count, tile_width), refl_count)
    weights = jnp.sum(bragg_vectors * diff[None, :], axis=1)
    shift = jnp.sum(weights[:, None, None] * gathered, axis=0).reshape(plane_count, row_count, tile_width)
    new_real = obj_real - 0.5 * (gridded[:, :, 0] - obj_imag * shift)
    new_imag = obj_imag - 0.5 * (gridded[:, :, 1] + obj_real * shift)
    return jnp.stack([new_real, new_imag], axis=2)[None]


def solution(mesh):
    in_specs = (
        P("refl", "slab", None, None),
        P("refl", "slab", None),
        P("refl", "slab"),
        P("refl", "slab"),
        P(),
        P(),
        P("refl", "slab", None, None, None),
    )
    out_specs = P("refl", "slab", None, None, None)
    return jax.shard_map(
        per_device, mesh=mesh, in_specs=in_specs, out_specs=out_specs, check_vma=False
    )
```

```python
import jax
import jax.numpy as jnp
from jax import lax
from jax.experimental import pallas as pl
from jax.experimental.pallas import tpu as pltpu
from jax.sharding import PartitionSpec as P

MESH = pl.DeviceIdType.MESH


def extended(block, sides, width):
    for axis, dim in sides:
        count = lax.axis_size(axis)
        forward = [(i, i + 1) for i in range(count - 1)]
        backward = [(target, source) for source, target in forward]
        low = lax.ppermute(
            lax.slice_in_dim(block, block.shape[dim] - width, None, axis=dim), axis, forward
        )
        high = lax.ppermute(lax.slice_in_dim(block, 0, width, axis=dim), axis, backward)
        block = jnp.concatenate([low, block, high], axis=dim)
    return block


def central(field, dimension):
    widths = [(0, 0)] * field.ndim
    widths[dimension] = (1, 1)
    padded = jnp.pad(field, widths)
    length = field.shape[dimension]
    return 0.5 * (
        lax.slice_in_dim(padded, 2, length + 2, axis=dimension)
        - lax.slice_in_dim(padded, 0, length, axis=dimension)
    )


def phase_term(obj_real, obj_imag, grad_x, grad_y, grad_z, qrow):
    term_x = obj_real * grad_x[:, :, 1] - obj_imag * grad_x[:, :, 0]
    term_y = obj_real * grad_y[:, :, 1] - obj_imag * grad_y[:, :, 0]
    term_z = obj_real * grad_z[:, :, 1] - obj_imag * grad_z[:, :, 0]
    return qrow[0] * term_x + qrow[1] * term_y + qrow[2] * term_z


def gather_kernel(phase_ref, out_ref, send_sem, recv_sem):
    count = out_ref.shape[0]
    me = lax.axis_index("refl")
    slab = lax.axis_index("slab")
    barrier = pltpu.get_barrier_semaphore()
    for step in range(1, count):
        peer = lax.rem(me + step, count)
        pl.semaphore_signal(barrier, 1, device_id=(peer, slab), device_id_type=MESH)
    pl.semaphore_wait(barrier, count - 1)
    copies = []
    for step in range(1, count):
        peer = lax.rem(me + step, count)
        copy = pltpu.make_async_remote_copy(
            src_ref=phase_ref,
            dst_ref=out_ref.at[me],
            send_sem=send_sem.at[step],
            recv_sem=recv_sem.at[step],
            device_id=(peer, slab),
            device_id_type=MESH,
        )
        copy.start()
        copies.append(copy)
    out_ref[me] = phase_ref[...]
    for copy in copies:
        copy.wait_send()
    for step in range(1, count):
        source = lax.rem(me + count - step, count)
        pltpu.make_async_remote_copy(
            src_ref=phase_ref,
            dst_ref=out_ref.at[source],
            send_sem=send_sem.at[step],
            recv_sem=recv_sem.at[step],
            device_id=(source, slab),
            device_id_type=MESH,
        ).wait_recv()


def gather_refl(phase, count):
    return pl.pallas_call(
        gather_kernel,
        out_shape=jax.ShapeDtypeStruct((count,) + phase.shape, phase.dtype),
        in_specs=[pl.BlockSpec(memory_space=pltpu.VMEM)],
        out_specs=pl.BlockSpec(memory_space=pltpu.VMEM),
        scratch_shapes=[pltpu.SemaphoreType.DMA((count,)), pltpu.SemaphoreType.DMA((count,))],
        compiler_params=pltpu.CompilerParams(collective_id=0, has_side_effects=True),
    )(phase)


def exchange_kernel(slot_ref, values_ref, data_out, data_buf, data_send, data_recv):
    count, capacity = data_out.shape[0], data_out.shape[1]
    group = 8 if count >= 16 else count // 2
    groups = count // group
    rows = group * capacity
    me = lax.axis_index("slab")
    refl = lax.axis_index("refl")
    barrier = pltpu.get_barrier_semaphore()

    def greet(step, carry):
        peer = lax.rem(me + step, count)
        pl.semaphore_signal(barrier, 1, device_id=(refl, peer), device_id_type=MESH)
        return carry

    lax.fori_loop(1, count, greet, 0)

    def pack(g):
        target = lax.broadcasted_iota(jnp.int32, (rows, slot_ref.shape[1]), 0) + g * rows
        chosen = (slot_ref[...] == target).astype(jnp.bfloat16)
        sent = jnp.dot(chosen, values_ref[...], preferred_element_type=jnp.float32)
        data_buf[pl.ds(g * group, group)] = sent.astype(jnp.bfloat16).reshape(
            group, capacity, sent.shape[1]
        )

    def outgoing(d):
        return pltpu.make_async_remote_copy(
            src_ref=data_buf.at[d], dst_ref=data_out.at[me], send_sem=data_send.at[d],
            recv_sem=data_recv.at[me], device_id=(refl, d), device_id_type=MESH,
        )

    def incoming(s):
        return pltpu.make_async_remote_copy(
            src_ref=data_buf.at[s], dst_ref=data_out.at[s], send_sem=data_send.at[s],
            recv_sem=data_recv.at[s], device_id=(refl, s), device_id_type=MESH,
        )

    def send(g):
        for part in range(group):
            d = g * group + part

            @pl.when(d != me)
            def _():
                outgoing(d).start()

    home = me // group
    pack(home)
    pl.semaphore_wait(barrier, count - 1)
    send(home)

    def later(j, carry):
        g = lax.rem(home + j, groups)
        pack(g)
        send(g)
        return carry

    lax.fori_loop(1, groups, later, 0)
    data_out[me] = data_buf[me]

    def finish(step, carry):
        outgoing(lax.rem(me + step, count)).wait_send()
        incoming(lax.rem(me + count - step, count)).wait_recv()
        return carry

    lax.fori_loop(1, count, finish, 0)


def exchange_slab(flat_slot, values, count, capacity):
    data_shape = (count, capacity, values.shape[1])
    return pl.pallas_call(
        exchange_kernel,
        out_shape=jax.ShapeDtypeStruct(data_shape, jnp.bfloat16),
        in_specs=[pl.BlockSpec(memory_space=pltpu.VMEM)] * 2,
        out_specs=pl.BlockSpec(memory_space=pltpu.VMEM),
        scratch_shapes=[
            pltpu.VMEM(data_shape, jnp.bfloat16),
            pltpu.SemaphoreType.DMA((count,)),
            pltpu.SemaphoreType.DMA((count,)),
        ],
        compiler_params=pltpu.CompilerParams(collective_id=1, has_side_effects=True),
    )(flat_slot, values)


def per_device(detector, owners, block_ids, kernel_ids, kernels, bragg_vectors, object_field):
    slab_count = lax.axis_size("slab")
    plane_count = object_field.shape[1]
    row_count = object_field.shape[2]
    block_count = plane_count * row_count
    kernel_count = kernels.shape[0]
    tile_count = detector.shape[1]
    tile_width = detector.shape[3]
    row_width = 2 * tile_width
    capacity = 2 * tile_count // slab_count
    values = detector[0].reshape(tile_count, row_width)
    owner = owners[0, :, 0]
    order = lax.broadcasted_iota(jnp.int32, (tile_count, tile_count), 1) < lax.broadcasted_iota(
        jnp.int32, (tile_count, tile_count), 0
    )
    same = (owner[:, None] == owner[None, :]) & order
    slots = jnp.sum(same.astype(jnp.int32), axis=1)
    flat_slot = owner * capacity + slots
    codes = block_ids[0] * kernel_count + kernel_ids[0]
    placed = flat_slot[None, :] == lax.broadcasted_iota(jnp.int32, (slab_count * capacity, tile_count), 0)
    sent_codes = jnp.max(jnp.where(placed, codes[None, :], -1), axis=1).reshape(slab_count, capacity)
    got_codes = lax.all_to_all(sent_codes, "slab", split_axis=0, concat_axis=0, tiled=True)
    got = exchange_slab(flat_slot[None, :], values, slab_count, capacity)
    row_total = slab_count * capacity
    rows = got.reshape(row_total, row_width)
    got_codes = jnp.maximum(got_codes, 0).reshape(row_total)
    chosen = (
        got_codes[None, :]
        == lax.broadcasted_iota(jnp.int32, (block_count * kernel_count, row_total), 0)
    ).astype(jnp.bfloat16)
    summed = jnp.dot(chosen, rows, preferred_element_type=jnp.float32)
    summed = summed.reshape(block_count, kernel_count, 2, tile_width).transpose(0, 2, 1, 3)
    gridded = jnp.dot(
        summed.reshape(block_count * 2, kernel_count * tile_width),
        kernels.astype(jnp.float32).reshape(kernel_count * tile_width, tile_width),
        precision=lax.Precision.HIGHEST,
        preferred_element_type=jnp.float32,
    )
    gridded = gridded.reshape(plane_count, row_count, 2, tile_width)
    padded = extended(gridded, (("slab", 0),), 1)
    grad_x = 0.5 * (padded[2:] - padded[:-2])
    grad_y = central(gridded, 1)
    grad_z = central(gridded, 3)
    refl_count = bragg_vectors.shape[0]
    places = jnp.arange(refl_count, dtype=jnp.int32)
    my_refl = lax.axis_index("refl")
    q_self = jnp.sum(jnp.where((places == my_refl)[:, None], bragg_vectors, 0.0), axis=0)
    mate = my_refl + 1 - 2 * (my_refl % 2)
    q_other = jnp.sum(jnp.where((places == mate)[:, None], bragg_vectors, 0.0), axis=0)
    obj = object_field[0]
    obj_real = obj[:, :, 0]
    obj_imag = obj[:, :, 1]
    phase = phase_term(obj_real, obj_imag, grad_x, grad_y, grad_z, q_self)
    diff = q_self - q_other
    gathered = gather_refl(phase.reshape(plane_count * row_count, tile_width), refl_count)
    weights = jnp.sum(bragg_vectors * diff[None, :], axis=1)
    shift = jnp.sum(weights[:, None, None] * gathered, axis=0).reshape(plane_count, row_count, tile_width)
    new_real = obj_real - 0.5 * (gridded[:, :, 0] - obj_imag * shift)
    new_imag = obj_imag - 0.5 * (gridded[:, :, 1] + obj_real * shift)
    return jnp.stack([new_real, new_imag], axis=2)[None]


def solution(mesh):
    in_specs = (
        P("refl", "slab", None, None),
        P("refl", "slab", None),
        P("refl", "slab"),
        P("refl", "slab"),
        P(),
        P(),
        P("refl", "slab", None, None, None),
    )
    out_specs = P("refl", "slab", None, None, None)
    return jax.shard_map(
        per_device, mesh=mesh, in_specs=in_specs, out_specs=out_specs, check_vma=False
    )
```

```python
import functools

import jax
import jax.numpy as jnp
from jax import lax
from jax.experimental import pallas as pl
from jax.experimental.pallas import tpu as pltpu
from jax.sharding import PartitionSpec as P

MESH = pl.DeviceIdType.MESH


def extended(block, sides, width):
    for axis, dim in sides:
        count = lax.axis_size(axis)
        forward = [(i, i + 1) for i in range(count - 1)]
        backward = [(target, source) for source, target in forward]
        low = lax.ppermute(
            lax.slice_in_dim(block, block.shape[dim] - width, None, axis=dim), axis, forward
        )
        high = lax.ppermute(lax.slice_in_dim(block, 0, width, axis=dim), axis, backward)
        block = jnp.concatenate([low, block, high], axis=dim)
    return block


def central(field, dimension):
    widths = [(0, 0)] * field.ndim
    widths[dimension] = (1, 1)
    padded = jnp.pad(field, widths)
    length = field.shape[dimension]
    return 0.5 * (
        lax.slice_in_dim(padded, 2, length + 2, axis=dimension)
        - lax.slice_in_dim(padded, 0, length, axis=dimension)
    )


def phase_term(obj_real, obj_imag, grad_x, grad_y, grad_z, qrow):
    term_x = obj_real * grad_x[:, :, 1] - obj_imag * grad_x[:, :, 0]
    term_y = obj_real * grad_y[:, :, 1] - obj_imag * grad_y[:, :, 0]
    term_z = obj_real * grad_z[:, :, 1] - obj_imag * grad_z[:, :, 0]
    return qrow[0] * term_x + qrow[1] * term_y + qrow[2] * term_z


def post_kernel(
    scalars, grid_ref, obj_ref, out_ref, halo, gathered, phase_buf, halo_send, halo_recv, send_sem, recv_sem,
    slab_count,
):
    refl_count = gathered.shape[0]
    planes, rows, width = grid_ref.shape[0], grid_ref.shape[2], grid_ref.shape[3]
    me = lax.axis_index("slab")
    refl = lax.axis_index("refl")
    up = lax.rem(me + 1, slab_count)
    down = lax.rem(me + slab_count - 1, slab_count)
    barrier = pltpu.get_barrier_semaphore()
    pl.semaphore_signal(barrier, 1, device_id=(refl, up), device_id_type=MESH)
    pl.semaphore_signal(barrier, 1, device_id=(refl, down), device_id_type=MESH)
    for step in range(1, refl_count):
        peer = lax.rem(refl + step, refl_count)
        pl.semaphore_signal(barrier, 1, device_id=(peer, me), device_id_type=MESH)
    pl.semaphore_wait(barrier, refl_count + 1)
    low_copy = pltpu.make_async_remote_copy(
        src_ref=grid_ref.at[planes - 1], dst_ref=halo.at[0], send_sem=halo_send.at[0],
        recv_sem=halo_recv.at[0], device_id=(refl, up), device_id_type=MESH,
    )
    high_copy = pltpu.make_async_remote_copy(
        src_ref=grid_ref.at[0], dst_ref=halo.at[1], send_sem=halo_send.at[1],
        recv_sem=halo_recv.at[1], device_id=(refl, down), device_id_type=MESH,
    )
    low_copy.start()
    high_copy.start()
    row_of = lax.broadcasted_iota(jnp.int32, (rows, width), 0)
    lane_of = lax.broadcasted_iota(jnp.int32, (rows, width), 1)

    def along_y(field):
        after = jnp.where(row_of == rows - 1, 0.0, pltpu.roll(field, rows - 1, 0))
        before = jnp.where(row_of == 0, 0.0, pltpu.roll(field, 1, 0))
        return 0.5 * (after - before)

    def along_w(field):
        after = jnp.where(lane_of == width - 1, 0.0, pltpu.roll(field, width - 1, 1))
        before = jnp.where(lane_of == 0, 0.0, pltpu.roll(field, 1, 1))
        return 0.5 * (after - before)

    q0, q1, q2 = scalars[0], scalars[1], scalars[2]
    partial = []
    for p in range(planes):
        obj_re, obj_im = obj_ref[p, 0], obj_ref[p, 1]
        term_y = obj_re * along_y(grid_ref[p, 1]) - obj_im * along_y(grid_ref[p, 0])
        term_z = obj_re * along_w(grid_ref[p, 1]) - obj_im * along_w(grid_ref[p, 0])
        partial.append((term_y, term_z))
    low_copy.wait_send()
    high_copy.wait_send()
    low_copy.wait_recv()
    high_copy.wait_recv()
    has_low = me > 0
    has_high = me < slab_count - 1
    for p in range(planes):
        obj_re, obj_im = obj_ref[p, 0], obj_ref[p, 1]
        grad = []
        for c in range(2):
            ahead = grid_ref[p + 1, c] if p + 1 < planes else jnp.where(has_high, halo[1, c], 0.0)
            behind = grid_ref[p - 1, c] if p > 0 else jnp.where(has_low, halo[0, c], 0.0)
            grad.append(0.5 * (ahead - behind))
        term_x = obj_re * grad[1] - obj_im * grad[0]
        term_y, term_z = partial[p]
        phase_buf[p] = q0 * term_x + q1 * term_y + q2 * term_z
    copies = []
    for step in range(1, refl_count):
        peer = lax.rem(refl + step, refl_count)
        copy = pltpu.make_async_remote_copy(
            src_ref=phase_buf, dst_ref=gathered.at[refl], send_sem=send_sem.at[step],
            recv_sem=recv_sem.at[step], device_id=(peer, me), device_id_type=MESH,
        )
        copy.start()
        copies.append(copy)
    gathered[refl] = phase_buf[...]
    for copy in copies:
        copy.wait_send()
    for step in range(1, refl_count):
        source = lax.rem(refl + refl_count - step, refl_count)
        pltpu.make_async_remote_copy(
            src_ref=phase_buf, dst_ref=gathered.at[source], send_sem=send_sem.at[step],
            recv_sem=recv_sem.at[step], device_id=(source, me), device_id_type=MESH,
        ).wait_recv()
    shift = scalars[3] * gathered[0]
    for r in range(1, refl_count):
        shift = shift + scalars[3 + r] * gathered[r]
    for p in range(planes):
        obj_re, obj_im = obj_ref[p, 0], obj_ref[p, 1]
        out_ref[p, 0] = obj_re - 0.5 * (grid_ref[p, 0] - obj_im * shift[p])
        out_ref[p, 1] = obj_im - 0.5 * (grid_ref[p, 1] + obj_re * shift[p])


def post_step(scalars, grid, obj, slab_count, refl_count):
    planes, _, rows, width = grid.shape
    return pl.pallas_call(
        functools.partial(post_kernel, slab_count=slab_count),
        out_shape=jax.ShapeDtypeStruct(grid.shape, jnp.float32),
        in_specs=[pl.BlockSpec(memory_space=pltpu.SMEM)]
        + [pl.BlockSpec(memory_space=pltpu.VMEM)] * 2,
        out_specs=pl.BlockSpec(memory_space=pltpu.VMEM),
        scratch_shapes=[
            pltpu.VMEM((2, 2, rows, width), jnp.float32),
            pltpu.VMEM((refl_count, planes, rows, width), jnp.float32),
            pltpu.VMEM((planes, rows, width), jnp.float32),
            pltpu.SemaphoreType.DMA((2,)),
            pltpu.SemaphoreType.DMA((2,)),
            pltpu.SemaphoreType.DMA((refl_count,)),
            pltpu.SemaphoreType.DMA((refl_count,)),
        ],
        compiler_params=pltpu.CompilerParams(collective_id=0, has_side_effects=True),
    )(scalars, grid, obj)


def exchange_kernel(
    slot_ref, values_ref, ids_ref, data_out, code_out,
    data_buf, code_buf, data_send, data_recv, code_send, code_recv,
):
    count, capacity = data_out.shape[0], data_out.shape[1]
    group = 8 if count >= 16 else count // 2
    groups = count // group
    rows = group * capacity
    me = lax.axis_index("slab")
    refl = lax.axis_index("refl")
    barrier = pltpu.get_barrier_semaphore()

    def greet(step, carry):
        peer = lax.rem(me + step, count)
        pl.semaphore_signal(barrier, 1, device_id=(refl, peer), device_id_type=MESH)
        return carry

    lax.fori_loop(1, count, greet, 0)

    def pack(g):
        target = lax.broadcasted_iota(jnp.int32, (rows, slot_ref.shape[1]), 0) + g * rows
        chosen = (slot_ref[...] == target).astype(jnp.bfloat16)
        sent = jnp.dot(chosen, values_ref[...], preferred_element_type=jnp.float32)
        data_buf[pl.ds(g * group, group)] = sent.astype(jnp.bfloat16).reshape(
            group, capacity, sent.shape[1]
        )
        codes = lax.dot_general(
            ids_ref[...], chosen, (((1,), (1,)), ((), ())), preferred_element_type=jnp.float32
        ).astype(jnp.bfloat16)
        for part in range(group):
            window = (part * capacity) // 128
            code_buf[g * group + part] = codes[:, window * 128 : (window + 1) * 128]

    def outgoing(d):
        data = pltpu.make_async_remote_copy(
            src_ref=data_buf.at[d], dst_ref=data_out.at[me], send_sem=data_send.at[d],
            recv_sem=data_recv.at[me], device_id=(refl, d), device_id_type=MESH,
        )
        code = pltpu.make_async_remote_copy(
            src_ref=code_buf.at[d], dst_ref=code_out.at[me], send_sem=code_send.at[d],
            recv_sem=code_recv.at[me], device_id=(refl, d), device_id_type=MESH,
        )
        return data, code

    def incoming(s):
        data = pltpu.make_async_remote_copy(
            src_ref=data_buf.at[s], dst_ref=data_out.at[s], send_sem=data_send.at[s],
            recv_sem=data_recv.at[s], device_id=(refl, s), device_id_type=MESH,
        )
        code = pltpu.make_async_remote_copy(
            src_ref=code_buf.at[s], dst_ref=code_out.at[s], send_sem=code_send.at[s],
            recv_sem=code_recv.at[s], device_id=(refl, s), device_id_type=MESH,
        )
        return data, code

    def send(g):
        for part in range(group):
            d = g * group + part

            @pl.when(d != me)
            def _():
                data, code = outgoing(d)
                data.start()
                code.start()

    home = me // group
    pack(home)
    pl.semaphore_wait(barrier, count - 1)
    send(home)

    def later(j, carry):
        g = lax.rem(home + j, groups)
        pack(g)
        send(g)
        return carry

    lax.fori_loop(1, groups, later, 0)
    data_out[me] = data_buf[me]
    code_out[me] = code_buf[me]

    def finish(step, carry):
        data, code = outgoing(lax.rem(me + step, count))
        data.wait_send()
        code.wait_send()
        data, code = incoming(lax.rem(me + count - step, count))
        data.wait_recv()
        code.wait_recv()
        return carry

    lax.fori_loop(1, count, finish, 0)


def exchange_slab(flat_slot, values, ids, count, capacity):
    data_shape = (count, capacity, values.shape[1])
    code_shape = (count, ids.shape[0], 128)
    return pl.pallas_call(
        exchange_kernel,
        out_shape=(
            jax.ShapeDtypeStruct(data_shape, jnp.bfloat16),
            jax.ShapeDtypeStruct(code_shape, jnp.bfloat16),
        ),
        in_specs=[pl.BlockSpec(memory_space=pltpu.VMEM)] * 3,
        out_specs=(pl.BlockSpec(memory_space=pltpu.VMEM), pl.BlockSpec(memory_space=pltpu.VMEM)),
        scratch_shapes=[
            pltpu.VMEM(data_shape, jnp.bfloat16),
            pltpu.VMEM(code_shape, jnp.bfloat16),
            pltpu.SemaphoreType.DMA((count,)),
            pltpu.SemaphoreType.DMA((count,)),
            pltpu.SemaphoreType.DMA((count,)),
            pltpu.SemaphoreType.DMA((count,)),
        ],
        compiler_params=pltpu.CompilerParams(collective_id=1, has_side_effects=True),
    )(flat_slot, values, ids)


def per_device(detector, owners, block_ids, kernel_ids, kernels, bragg_vectors, object_field):
    slab_count = lax.axis_size("slab")
    plane_count = object_field.shape[1]
    row_count = object_field.shape[2]
    block_count = plane_count * row_count
    kernel_count = kernels.shape[0]
    tile_count = detector.shape[1]
    tile_width = detector.shape[3]
    row_width = 2 * tile_width
    capacity = 2 * tile_count // slab_count
    values = detector[0].reshape(tile_count, row_width)
    owner = owners[0, :, 0]
    order = lax.broadcasted_iota(jnp.int32, (tile_count, tile_count), 1) < lax.broadcasted_iota(
        jnp.int32, (tile_count, tile_count), 0
    )
    same = (owner[:, None] == owner[None, :]) & order
    slots = jnp.sum(same.astype(jnp.int32), axis=1)
    flat_slot = owner * capacity + slots
    ids = jnp.concatenate(
        [block_ids, kernel_ids, jnp.zeros((14, tile_count), jnp.int32)], axis=0
    ).astype(jnp.bfloat16)
    got, got_code = exchange_slab(flat_slot[None, :], values, ids, slab_count, capacity)
    row_total = slab_count * capacity
    rows = got.reshape(row_total, row_width)
    offset = lax.rem(lax.axis_index("slab"), 4) * capacity
    got_blocks = lax.dynamic_slice_in_dim(got_code[:, 0, :], offset, capacity, axis=1).astype(jnp.int32)
    got_kernels = lax.dynamic_slice_in_dim(got_code[:, 1, :], offset, capacity, axis=1).astype(jnp.int32)
    got_codes = (got_blocks * kernel_count + got_kernels).reshape(row_total)
    chosen = (
        got_codes[None, :]
        == lax.broadcasted_iota(jnp.int32, (block_count * kernel_count, row_total), 0)
    ).astype(jnp.bfloat16)
    summed = jnp.dot(chosen, rows, preferred_element_type=jnp.float32)
    summed = summed.reshape(block_count, kernel_count, 2, tile_width).transpose(0, 2, 1, 3)
    gridded = jnp.dot(
        summed.reshape(block_count * 2, kernel_count * tile_width),
        kernels.astype(jnp.float32).reshape(kernel_count * tile_width, tile_width),
        precision=lax.Precision.HIGHEST,
        preferred_element_type=jnp.float32,
    )
    gridded = gridded.reshape(plane_count, row_count, 2, tile_width).transpose(0, 2, 1, 3)
    refl_count = bragg_vectors.shape[0]
    places = jnp.arange(refl_count, dtype=jnp.int32)
    my_refl = lax.axis_index("refl")
    q_self = jnp.sum(jnp.where((places == my_refl)[:, None], bragg_vectors, 0.0), axis=0)
    mate = my_refl + 1 - 2 * (my_refl % 2)
    q_other = jnp.sum(jnp.where((places == mate)[:, None], bragg_vectors, 0.0), axis=0)
    diff = q_self - q_other
    weights = jnp.sum(bragg_vectors * diff[None, :], axis=1)
    scalars = jnp.concatenate([q_self, weights])
    obj = object_field[0].transpose(0, 2, 1, 3)
    updated = post_step(scalars, gridded, obj, slab_count, refl_count)
    return updated.transpose(0, 2, 1, 3)[None]


def solution(mesh):
    in_specs = (
        P("refl", "slab", None, None),
        P("refl", "slab", None),
        P("refl", "slab"),
        P("refl", "slab"),
        P(),
        P(),
        P("refl", "slab", None, None, None),
    )
    out_specs = P("refl", "slab", None, None, None)
    return jax.shard_map(
        per_device, mesh=mesh, in_specs=in_specs, out_specs=out_specs, check_vma=False
    )
```

```python
import functools

import jax
import jax.numpy as jnp
from jax import lax
from jax.experimental import pallas as pl
from jax.experimental.pallas import tpu as pltpu
from jax.sharding import PartitionSpec as P

MESH = pl.DeviceIdType.MESH


def extended(block, sides, width):
    for axis, dim in sides:
        count = lax.axis_size(axis)
        forward = [(i, i + 1) for i in range(count - 1)]
        backward = [(target, source) for source, target in forward]
        low = lax.ppermute(
            lax.slice_in_dim(block, block.shape[dim] - width, None, axis=dim), axis, forward
        )
        high = lax.ppermute(lax.slice_in_dim(block, 0, width, axis=dim), axis, backward)
        block = jnp.concatenate([low, block, high], axis=dim)
    return block


def central(field, dimension):
    widths = [(0, 0)] * field.ndim
    widths[dimension] = (1, 1)
    padded = jnp.pad(field, widths)
    length = field.shape[dimension]
    return 0.5 * (
        lax.slice_in_dim(padded, 2, length + 2, axis=dimension)
        - lax.slice_in_dim(padded, 0, length, axis=dimension)
    )


def phase_term(obj_real, obj_imag, grad_x, grad_y, grad_z, qrow):
    term_x = obj_real * grad_x[:, :, 1] - obj_imag * grad_x[:, :, 0]
    term_y = obj_real * grad_y[:, :, 1] - obj_imag * grad_y[:, :, 0]
    term_z = obj_real * grad_z[:, :, 1] - obj_imag * grad_z[:, :, 0]
    return qrow[0] * term_x + qrow[1] * term_y + qrow[2] * term_z


def post_kernel(
    scalars, grid_ref, obj_ref, out_ref, halo, gathered, phase_buf, halo_send, halo_recv, send_sem, recv_sem,
    slab_count,
):
    refl_count = gathered.shape[0]
    planes, rows, width = grid_ref.shape[0], grid_ref.shape[2], grid_ref.shape[3]
    me = lax.axis_index("slab")
    refl = lax.axis_index("refl")
    up = lax.rem(me + 1, slab_count)
    down = lax.rem(me + slab_count - 1, slab_count)
    barrier = pltpu.get_barrier_semaphore()
    pl.semaphore_signal(barrier, 1, device_id=(refl, up), device_id_type=MESH)
    pl.semaphore_signal(barrier, 1, device_id=(refl, down), device_id_type=MESH)
    for step in range(1, refl_count):
        peer = lax.rem(refl + step, refl_count)
        pl.semaphore_signal(barrier, 1, device_id=(peer, me), device_id_type=MESH)
    pl.semaphore_wait(barrier, refl_count + 1)
    low_copy = pltpu.make_async_remote_copy(
        src_ref=grid_ref.at[planes - 1], dst_ref=halo.at[0], send_sem=halo_send.at[0],
        recv_sem=halo_recv.at[0], device_id=(refl, up), device_id_type=MESH,
    )
    high_copy = pltpu.make_async_remote_copy(
        src_ref=grid_ref.at[0], dst_ref=halo.at[1], send_sem=halo_send.at[1],
        recv_sem=halo_recv.at[1], device_id=(refl, down), device_id_type=MESH,
    )
    low_copy.start()
    high_copy.start()
    row_of = lax.broadcasted_iota(jnp.int32, (rows, width), 0)
    lane_of = lax.broadcasted_iota(jnp.int32, (rows, width), 1)

    def along_y(field):
        after = jnp.where(row_of == rows - 1, 0.0, pltpu.roll(field, rows - 1, 0))
        before = jnp.where(row_of == 0, 0.0, pltpu.roll(field, 1, 0))
        return 0.5 * (after - before)

    def along_w(field):
        after = jnp.where(lane_of == width - 1, 0.0, pltpu.roll(field, width - 1, 1))
        before = jnp.where(lane_of == 0, 0.0, pltpu.roll(field, 1, 1))
        return 0.5 * (after - before)

    q0, q1, q2 = scalars[0], scalars[1], scalars[2]
    partial = []
    for p in range(planes):
        obj_re, obj_im = obj_ref[p, 0], obj_ref[p, 1]
        term_y = obj_re * along_y(grid_ref[p, 1]) - obj_im * along_y(grid_ref[p, 0])
        term_z = obj_re * along_w(grid_ref[p, 1]) - obj_im * along_w(grid_ref[p, 0])
        partial.append((term_y, term_z))
    low_copy.wait_send()
    high_copy.wait_send()
    low_copy.wait_recv()
    high_copy.wait_recv()
    has_low = me > 0
    has_high = me < slab_count - 1
    for p in range(planes):
        obj_re, obj_im = obj_ref[p, 0], obj_ref[p, 1]
        grad = []
        for c in range(2):
            ahead = grid_ref[p + 1, c] if p + 1 < planes else jnp.where(has_high, halo[1, c], 0.0)
            behind = grid_ref[p - 1, c] if p > 0 else jnp.where(has_low, halo[0, c], 0.0)
            grad.append(0.5 * (ahead - behind))
        term_x = obj_re * grad[1] - obj_im * grad[0]
        term_y, term_z = partial[p]
        phase_buf[p] = q0 * term_x + q1 * term_y + q2 * term_z
    copies = []
    for step in range(1, refl_count):
        peer = lax.rem(refl + step, refl_count)
        copy = pltpu.make_async_remote_copy(
            src_ref=phase_buf, dst_ref=gathered.at[refl], send_sem=send_sem.at[step],
            recv_sem=recv_sem.at[step], device_id=(peer, me), device_id_type=MESH,
        )
        copy.start()
        copies.append(copy)
    gathered[refl] = phase_buf[...]
    for copy in copies:
        copy.wait_send()
    for step in range(1, refl_count):
        source = lax.rem(refl + refl_count - step, refl_count)
        pltpu.make_async_remote_copy(
            src_ref=phase_buf, dst_ref=gathered.at[source], send_sem=send_sem.at[step],
            recv_sem=recv_sem.at[step], device_id=(source, me), device_id_type=MESH,
        ).wait_recv()
    shift = scalars[3] * gathered[0]
    for r in range(1, refl_count):
        shift = shift + scalars[3 + r] * gathered[r]
    for p in range(planes):
        obj_re, obj_im = obj_ref[p, 0], obj_ref[p, 1]
        out_ref[p, 0] = obj_re - 0.5 * (grid_ref[p, 0] - obj_im * shift[p])
        out_ref[p, 1] = obj_im - 0.5 * (grid_ref[p, 1] + obj_re * shift[p])


def post_step(scalars, grid, obj, slab_count, refl_count):
    planes, _, rows, width = grid.shape
    return pl.pallas_call(
        functools.partial(post_kernel, slab_count=slab_count),
        out_shape=jax.ShapeDtypeStruct(grid.shape, jnp.float32),
        in_specs=[pl.BlockSpec(memory_space=pltpu.SMEM)]
        + [pl.BlockSpec(memory_space=pltpu.VMEM)] * 2,
        out_specs=pl.BlockSpec(memory_space=pltpu.VMEM),
        scratch_shapes=[
            pltpu.VMEM((2, 2, rows, width), jnp.float32),
            pltpu.VMEM((refl_count, planes, rows, width), jnp.float32),
            pltpu.VMEM((planes, rows, width), jnp.float32),
            pltpu.SemaphoreType.DMA((2,)),
            pltpu.SemaphoreType.DMA((2,)),
            pltpu.SemaphoreType.DMA((refl_count,)),
            pltpu.SemaphoreType.DMA((refl_count,)),
        ],
        compiler_params=pltpu.CompilerParams(collective_id=0, has_side_effects=True),
    )(scalars, grid, obj)


def exchange_kernel(
    slot_ref, values_ref, code_in, data_out, code_out, data_buf, data_send, data_recv, code_send, code_recv,
):
    count, capacity = data_out.shape[0], data_out.shape[1]
    group = 8 if count >= 16 else count // 2
    groups = count // group
    rows = group * capacity
    me = lax.axis_index("slab")
    refl = lax.axis_index("refl")
    barrier = pltpu.get_barrier_semaphore()

    def greet(step, carry):
        peer = lax.rem(me + step, count)
        pl.semaphore_signal(barrier, 1, device_id=(refl, peer), device_id_type=MESH)
        return carry

    lax.fori_loop(1, count, greet, 0)

    def pack(g):
        target = lax.broadcasted_iota(jnp.int32, (rows, slot_ref.shape[1]), 0) + g * rows
        chosen = (slot_ref[...] == target).astype(jnp.bfloat16)
        sent = jnp.dot(chosen, values_ref[...], preferred_element_type=jnp.float32)
        data_buf[pl.ds(g * group, group)] = sent.astype(jnp.bfloat16).reshape(
            group, capacity, sent.shape[1]
        )

    def outgoing(d):
        data = pltpu.make_async_remote_copy(
            src_ref=data_buf.at[d], dst_ref=data_out.at[me], send_sem=data_send.at[d],
            recv_sem=data_recv.at[me], device_id=(refl, d), device_id_type=MESH,
        )
        code = pltpu.make_async_remote_copy(
            src_ref=code_in.at[d], dst_ref=code_out.at[me], send_sem=code_send.at[d],
            recv_sem=code_recv.at[me], device_id=(refl, d), device_id_type=MESH,
        )
        return data, code

    def incoming(s):
        data = pltpu.make_async_remote_copy(
            src_ref=data_buf.at[s], dst_ref=data_out.at[s], send_sem=data_send.at[s],
            recv_sem=data_recv.at[s], device_id=(refl, s), device_id_type=MESH,
        )
        code = pltpu.make_async_remote_copy(
            src_ref=code_in.at[s], dst_ref=code_out.at[s], send_sem=code_send.at[s],
            recv_sem=code_recv.at[s], device_id=(refl, s), device_id_type=MESH,
        )
        return data, code

    def send(g):
        for part in range(group):
            d = g * group + part

            @pl.when(d != me)
            def _():
                data, code = outgoing(d)
                code.start()
                data.start()

    home = me // group
    pack(home)
    pl.semaphore_wait(barrier, count - 1)
    send(home)

    def later(j, carry):
        g = lax.rem(home + j, groups)
        pack(g)
        send(g)
        return carry

    lax.fori_loop(1, groups, later, 0)
    data_out[me] = data_buf[me]
    local = pltpu.make_async_copy(code_in.at[me], code_out.at[me], code_send.at[me])
    local.start()

    def finish(step, carry):
        data, code = outgoing(lax.rem(me + step, count))
        data.wait_send()
        code.wait_send()
        data, code = incoming(lax.rem(me + count - step, count))
        data.wait_recv()
        code.wait_recv()
        return carry

    lax.fori_loop(1, count, finish, 0)
    local.wait()


def exchange_slab(flat_slot, values, codes, count, capacity):
    data_shape = (count, capacity, values.shape[1])
    return pl.pallas_call(
        exchange_kernel,
        out_shape=(
            jax.ShapeDtypeStruct(data_shape, jnp.bfloat16),
            jax.ShapeDtypeStruct(codes.shape, codes.dtype),
        ),
        in_specs=[pl.BlockSpec(memory_space=pltpu.VMEM)] * 2 + [pl.BlockSpec(memory_space=pl.ANY)],
        out_specs=(pl.BlockSpec(memory_space=pltpu.VMEM), pl.BlockSpec(memory_space=pl.ANY)),
        scratch_shapes=[
            pltpu.VMEM(data_shape, jnp.bfloat16),
            pltpu.SemaphoreType.DMA((count,)),
            pltpu.SemaphoreType.DMA((count,)),
            pltpu.SemaphoreType.DMA((count,)),
            pltpu.SemaphoreType.DMA((count,)),
        ],
        compiler_params=pltpu.CompilerParams(collective_id=1, has_side_effects=True),
    )(flat_slot, values, codes)


def per_device(detector, owners, block_ids, kernel_ids, kernels, bragg_vectors, object_field):
    slab_count = lax.axis_size("slab")
    plane_count = object_field.shape[1]
    row_count = object_field.shape[2]
    block_count = plane_count * row_count
    kernel_count = kernels.shape[0]
    tile_count = detector.shape[1]
    tile_width = detector.shape[3]
    row_width = 2 * tile_width
    capacity = 2 * tile_count // slab_count
    values = detector[0].reshape(tile_count, row_width)
    owner = owners[0, :, 0]
    order = lax.broadcasted_iota(jnp.int32, (tile_count, tile_count), 1) < lax.broadcasted_iota(
        jnp.int32, (tile_count, tile_count), 0
    )
    same = (owner[:, None] == owner[None, :]) & order
    slots = jnp.sum(same.astype(jnp.int32), axis=1)
    flat_slot = owner * capacity + slots
    codes = block_ids[0] * kernel_count + kernel_ids[0]
    placed = flat_slot[None, :] == lax.broadcasted_iota(jnp.int32, (slab_count * capacity, tile_count), 0)
    sent_codes = jnp.max(jnp.where(placed, codes[None, :], 0), axis=1).reshape(slab_count, 1, capacity)
    sent_codes = jnp.concatenate(
        [sent_codes, jnp.zeros((slab_count, 1, 128 - capacity), jnp.int32)], axis=2
    )
    got, got_code = exchange_slab(flat_slot[None, :], values, sent_codes, slab_count, capacity)
    row_total = slab_count * capacity
    rows = got.reshape(row_total, row_width)
    got_codes = got_code[:, 0, :capacity].reshape(row_total)
    chosen = (
        got_codes[None, :]
        == lax.broadcasted_iota(jnp.int32, (block_count * kernel_count, row_total), 0)
    ).astype(jnp.bfloat16)
    summed = jnp.dot(chosen, rows, preferred_element_type=jnp.float32)
    summed = summed.reshape(block_count, kernel_count, 2, tile_width).transpose(0, 2, 1, 3)
    gridded = jnp.dot(
        summed.reshape(block_count * 2, kernel_count * tile_width),
        kernels.astype(jnp.float32).reshape(kernel_count * tile_width, tile_width),
        precision=lax.Precision.HIGHEST,
        preferred_element_type=jnp.float32,
    )
    gridded = gridded.reshape(plane_count, row_count, 2, tile_width).transpose(0, 2, 1, 3)
    refl_count = bragg_vectors.shape[0]
    places = jnp.arange(refl_count, dtype=jnp.int32)
    my_refl = lax.axis_index("refl")
    q_self = jnp.sum(jnp.where((places == my_refl)[:, None], bragg_vectors, 0.0), axis=0)
    mate = my_refl + 1 - 2 * (my_refl % 2)
    q_other = jnp.sum(jnp.where((places == mate)[:, None], bragg_vectors, 0.0), axis=0)
    diff = q_self - q_other
    weights = jnp.sum(bragg_vectors * diff[None, :], axis=1)
    scalars = jnp.concatenate([q_self, weights])
    obj = object_field[0].transpose(0, 2, 1, 3)
    updated = post_step(scalars, gridded, obj, slab_count, refl_count)
    return updated.transpose(0, 2, 1, 3)[None]


def solution(mesh):
    in_specs = (
        P("refl", "slab", None, None),
        P("refl", "slab", None),
        P("refl", "slab"),
        P("refl", "slab"),
        P(),
        P(),
        P("refl", "slab", None, None, None),
    )
    out_specs = P("refl", "slab", None, None, None)
    return jax.shard_map(
        per_device, mesh=mesh, in_specs=in_specs, out_specs=out_specs, check_vma=False
    )
```

```python
import functools

import jax
import jax.numpy as jnp
from jax import lax
from jax.experimental import pallas as pl
from jax.experimental.pallas import tpu as pltpu
from jax.sharding import PartitionSpec as P

MESH = pl.DeviceIdType.MESH


def extended(block, sides, width):
    for axis, dim in sides:
        count = lax.axis_size(axis)
        forward = [(i, i + 1) for i in range(count - 1)]
        backward = [(target, source) for source, target in forward]
        low = lax.ppermute(
            lax.slice_in_dim(block, block.shape[dim] - width, None, axis=dim), axis, forward
        )
        high = lax.ppermute(lax.slice_in_dim(block, 0, width, axis=dim), axis, backward)
        block = jnp.concatenate([low, block, high], axis=dim)
    return block


def central(field, dimension):
    widths = [(0, 0)] * field.ndim
    widths[dimension] = (1, 1)
    padded = jnp.pad(field, widths)
    length = field.shape[dimension]
    return 0.5 * (
        lax.slice_in_dim(padded, 2, length + 2, axis=dimension)
        - lax.slice_in_dim(padded, 0, length, axis=dimension)
    )


def phase_term(obj_real, obj_imag, grad_x, grad_y, grad_z, qrow):
    term_x = obj_real * grad_x[:, :, 1] - obj_imag * grad_x[:, :, 0]
    term_y = obj_real * grad_y[:, :, 1] - obj_imag * grad_y[:, :, 0]
    term_z = obj_real * grad_z[:, :, 1] - obj_imag * grad_z[:, :, 0]
    return qrow[0] * term_x + qrow[1] * term_y + qrow[2] * term_z


def post_kernel(
    scalars, grid_ref, obj_ref, out_ref, halo, gathered, phase_buf, halo_send, halo_recv, send_sem, recv_sem,
    slab_count,
):
    refl_count = gathered.shape[0]
    planes, rows, width = grid_ref.shape[0], grid_ref.shape[2], grid_ref.shape[3]
    me = lax.axis_index("slab")
    refl = lax.axis_index("refl")
    up = lax.rem(me + 1, slab_count)
    down = lax.rem(me + slab_count - 1, slab_count)
    barrier = pltpu.get_barrier_semaphore()
    pl.semaphore_signal(barrier, 1, device_id=(refl, up), device_id_type=MESH)
    pl.semaphore_signal(barrier, 1, device_id=(refl, down), device_id_type=MESH)
    for step in range(1, refl_count):
        peer = lax.rem(refl + step, refl_count)
        pl.semaphore_signal(barrier, 1, device_id=(peer, me), device_id_type=MESH)
    pl.semaphore_wait(barrier, refl_count + 1)
    low_copy = pltpu.make_async_remote_copy(
        src_ref=grid_ref.at[planes - 1], dst_ref=halo.at[0], send_sem=halo_send.at[0],
        recv_sem=halo_recv.at[0], device_id=(refl, up), device_id_type=MESH,
    )
    high_copy = pltpu.make_async_remote_copy(
        src_ref=grid_ref.at[0], dst_ref=halo.at[1], send_sem=halo_send.at[1],
        recv_sem=halo_recv.at[1], device_id=(refl, down), device_id_type=MESH,
    )
    low_copy.start()
    high_copy.start()
    row_of = lax.broadcasted_iota(jnp.int32, (rows, width), 0)
    lane_of = lax.broadcasted_iota(jnp.int32, (rows, width), 1)

    def along_y(field):
        after = jnp.where(row_of == rows - 1, 0.0, pltpu.roll(field, rows - 1, 0))
        before = jnp.where(row_of == 0, 0.0, pltpu.roll(field, 1, 0))
        return 0.5 * (after - before)

    def along_w(field):
        after = jnp.where(lane_of == width - 1, 0.0, pltpu.roll(field, width - 1, 1))
        before = jnp.where(lane_of == 0, 0.0, pltpu.roll(field, 1, 1))
        return 0.5 * (after - before)

    mate = refl + 1 - 2 * lax.rem(refl, 2)
    q0, q1, q2 = scalars[refl, 0], scalars[refl, 1], scalars[refl, 2]
    d0 = q0 - scalars[mate, 0]
    d1 = q1 - scalars[mate, 1]
    d2 = q2 - scalars[mate, 2]
    partial = []
    for p in range(planes):
        obj_re, obj_im = obj_ref[p, 0], obj_ref[p, 1]
        term_y = obj_re * along_y(grid_ref[p, 1]) - obj_im * along_y(grid_ref[p, 0])
        term_z = obj_re * along_w(grid_ref[p, 1]) - obj_im * along_w(grid_ref[p, 0])
        partial.append((term_y, term_z))
    low_copy.wait_send()
    high_copy.wait_send()
    low_copy.wait_recv()
    high_copy.wait_recv()
    has_low = me > 0
    has_high = me < slab_count - 1
    for p in range(planes):
        obj_re, obj_im = obj_ref[p, 0], obj_ref[p, 1]
        grad = []
        for c in range(2):
            ahead = grid_ref[p + 1, c] if p + 1 < planes else jnp.where(has_high, halo[1, c], 0.0)
            behind = grid_ref[p - 1, c] if p > 0 else jnp.where(has_low, halo[0, c], 0.0)
            grad.append(0.5 * (ahead - behind))
        term_x = obj_re * grad[1] - obj_im * grad[0]
        term_y, term_z = partial[p]
        phase_buf[p] = q0 * term_x + q1 * term_y + q2 * term_z
    copies = []
    for step in range(1, refl_count):
        peer = lax.rem(refl + step, refl_count)
        copy = pltpu.make_async_remote_copy(
            src_ref=phase_buf, dst_ref=gathered.at[refl], send_sem=send_sem.at[step],
            recv_sem=recv_sem.at[step], device_id=(peer, me), device_id_type=MESH,
        )
        copy.start()
        copies.append(copy)
    gathered[refl] = phase_buf[...]
    for copy in copies:
        copy.wait_send()
    for step in range(1, refl_count):
        source = lax.rem(refl + refl_count - step, refl_count)
        pltpu.make_async_remote_copy(
            src_ref=phase_buf, dst_ref=gathered.at[source], send_sem=send_sem.at[step],
            recv_sem=recv_sem.at[step], device_id=(source, me), device_id_type=MESH,
        ).wait_recv()
    def weight(r):
        return scalars[r, 0] * d0 + scalars[r, 1] * d1 + scalars[r, 2] * d2

    shift = weight(0) * gathered[0]
    for r in range(1, refl_count):
        shift = shift + weight(r) * gathered[r]
    for p in range(planes):
        obj_re, obj_im = obj_ref[p, 0], obj_ref[p, 1]
        out_ref[p, 0] = obj_re - 0.5 * (grid_ref[p, 0] - obj_im * shift[p])
        out_ref[p, 1] = obj_im - 0.5 * (grid_ref[p, 1] + obj_re * shift[p])


def post_step(scalars, grid, obj, slab_count, refl_count):
    planes, _, rows, width = grid.shape
    return pl.pallas_call(
        functools.partial(post_kernel, slab_count=slab_count),
        out_shape=jax.ShapeDtypeStruct(grid.shape, jnp.float32),
        in_specs=[pl.BlockSpec(memory_space=pltpu.SMEM)]
        + [pl.BlockSpec(memory_space=pltpu.VMEM)] * 2,
        out_specs=pl.BlockSpec(memory_space=pltpu.VMEM),
        scratch_shapes=[
            pltpu.VMEM((2, 2, rows, width), jnp.float32),
            pltpu.VMEM((refl_count, planes, rows, width), jnp.float32),
            pltpu.VMEM((planes, rows, width), jnp.float32),
            pltpu.SemaphoreType.DMA((2,)),
            pltpu.SemaphoreType.DMA((2,)),
            pltpu.SemaphoreType.DMA((refl_count,)),
            pltpu.SemaphoreType.DMA((refl_count,)),
        ],
        compiler_params=pltpu.CompilerParams(collective_id=0, has_side_effects=True),
    )(scalars, grid, obj)


def exchange_kernel(
    slot_ref, values_ref, code_in, data_out, code_out, data_buf, data_send, data_recv, code_send, code_recv,
):
    count, capacity = data_out.shape[0], data_out.shape[1]
    group = 8 if count >= 16 else count // 2
    groups = count // group
    rows = group * capacity
    me = lax.axis_index("slab")
    refl = lax.axis_index("refl")
    barrier = pltpu.get_barrier_semaphore()

    def greet(step, carry):
        peer = lax.rem(me + step, count)
        pl.semaphore_signal(barrier, 1, device_id=(refl, peer), device_id_type=MESH)
        return carry

    lax.fori_loop(1, count, greet, 0)

    def pack(g):
        target = lax.broadcasted_iota(jnp.int32, (rows, slot_ref.shape[1]), 0) + g * rows
        chosen = (slot_ref[...] == target).astype(jnp.bfloat16)
        sent = jnp.dot(chosen, values_ref[...], preferred_element_type=jnp.float32)
        data_buf[pl.ds(g * group, group)] = sent.astype(jnp.bfloat16).reshape(
            group, capacity, sent.shape[1]
        )

    def outgoing(d):
        data = pltpu.make_async_remote_copy(
            src_ref=data_buf.at[d], dst_ref=data_out.at[me], send_sem=data_send.at[d],
            recv_sem=data_recv.at[me], device_id=(refl, d), device_id_type=MESH,
        )
        code = pltpu.make_async_remote_copy(
            src_ref=code_in.at[d], dst_ref=code_out.at[me], send_sem=code_send.at[d],
            recv_sem=code_recv.at[me], device_id=(refl, d), device_id_type=MESH,
        )
        return data, code

    def incoming(s):
        data = pltpu.make_async_remote_copy(
            src_ref=data_buf.at[s], dst_ref=data_out.at[s], send_sem=data_send.at[s],
            recv_sem=data_recv.at[s], device_id=(refl, s), device_id_type=MESH,
        )
        code = pltpu.make_async_remote_copy(
            src_ref=code_in.at[s], dst_ref=code_out.at[s], send_sem=code_send.at[s],
            recv_sem=code_recv.at[s], device_id=(refl, s), device_id_type=MESH,
        )
        return data, code

    def send(g):
        for part in range(group):
            d = g * group + part

            @pl.when(d != me)
            def _():
                data, code = outgoing(d)
                code.start()
                data.start()

    home = me // group
    pack(home)
    pl.semaphore_wait(barrier, count - 1)
    send(home)

    def later(j, carry):
        g = lax.rem(home + j, groups)
        pack(g)
        send(g)
        return carry

    lax.fori_loop(1, groups, later, 0)
    data_out[me] = data_buf[me]
    local = pltpu.make_async_copy(code_in.at[me], code_out.at[me], code_send.at[me])
    local.start()

    def finish(step, carry):
        data, code = outgoing(lax.rem(me + step, count))
        data.wait_send()
        code.wait_send()
        data, code = incoming(lax.rem(me + count - step, count))
        data.wait_recv()
        code.wait_recv()
        return carry

    lax.fori_loop(1, count, finish, 0)
    local.wait()


def exchange_slab(flat_slot, values, codes, count, capacity):
    data_shape = (count, capacity, values.shape[1])
    return pl.pallas_call(
        exchange_kernel,
        out_shape=(
            jax.ShapeDtypeStruct(data_shape, jnp.bfloat16),
            jax.ShapeDtypeStruct(codes.shape, codes.dtype),
        ),
        in_specs=[pl.BlockSpec(memory_space=pltpu.VMEM)] * 2 + [pl.BlockSpec(memory_space=pl.ANY)],
        out_specs=(pl.BlockSpec(memory_space=pltpu.VMEM), pl.BlockSpec(memory_space=pl.ANY)),
        scratch_shapes=[
            pltpu.VMEM(data_shape, jnp.bfloat16),
            pltpu.SemaphoreType.DMA((count,)),
            pltpu.SemaphoreType.DMA((count,)),
            pltpu.SemaphoreType.DMA((count,)),
            pltpu.SemaphoreType.DMA((count,)),
        ],
        compiler_params=pltpu.CompilerParams(collective_id=1, has_side_effects=True),
    )(flat_slot, values, codes)


def per_device(detector, owners, block_ids, kernel_ids, kernels, bragg_vectors, object_field):
    slab_count = lax.axis_size("slab")
    plane_count = object_field.shape[1]
    row_count = object_field.shape[2]
    block_count = plane_count * row_count
    kernel_count = kernels.shape[0]
    tile_count = detector.shape[1]
    tile_width = detector.shape[3]
    row_width = 2 * tile_width
    capacity = 2 * tile_count // slab_count
    values = detector[0].reshape(tile_count, row_width)
    owner = owners[0, :, 0]
    order = lax.broadcasted_iota(jnp.int32, (tile_count, tile_count), 1) < lax.broadcasted_iota(
        jnp.int32, (tile_count, tile_count), 0
    )
    same = (owner[:, None] == owner[None, :]) & order
    slots = jnp.sum(same.astype(jnp.int32), axis=1)
    flat_slot = owner * capacity + slots
    codes = block_ids[0] * kernel_count + kernel_ids[0]
    placed = flat_slot[None, :] == lax.broadcasted_iota(jnp.int32, (slab_count * capacity, tile_count), 0)
    sent_codes = jnp.max(jnp.where(placed, codes[None, :], 0), axis=1).reshape(slab_count, 1, capacity)
    sent_codes = jnp.concatenate(
        [sent_codes, jnp.zeros((slab_count, 1, 128 - capacity), jnp.int32)], axis=2
    )
    got, got_code = exchange_slab(flat_slot[None, :], values, sent_codes, slab_count, capacity)
    row_total = slab_count * capacity
    rows = got.reshape(row_total, row_width)
    got_codes = got_code[:, 0, :capacity].reshape(row_total)
    chosen = (
        got_codes[None, :]
        == lax.broadcasted_iota(jnp.int32, (block_count * kernel_count, row_total), 0)
    ).astype(jnp.bfloat16)
    summed = jnp.dot(chosen, rows, preferred_element_type=jnp.float32)
    summed = summed.reshape(block_count, kernel_count, 2, tile_width).transpose(0, 2, 1, 3)
    gridded = jnp.dot(
        summed.reshape(block_count * 2, kernel_count * tile_width),
        kernels.astype(jnp.float32).reshape(kernel_count * tile_width, tile_width),
        precision=lax.Precision.HIGHEST,
        preferred_element_type=jnp.float32,
    )
    gridded = gridded.reshape(plane_count, row_count, 2, tile_width).transpose(0, 2, 1, 3)
    refl_count = bragg_vectors.shape[0]
    obj = object_field[0].transpose(0, 2, 1, 3)
    updated = post_step(bragg_vectors, gridded, obj, slab_count, refl_count)
    return updated.transpose(0, 2, 1, 3)[None]


def solution(mesh):
    in_specs = (
        P("refl", "slab", None, None),
        P("refl", "slab", None),
        P("refl", "slab"),
        P("refl", "slab"),
        P(),
        P(),
        P("refl", "slab", None, None, None),
    )
    out_specs = P("refl", "slab", None, None, None)
    return jax.shard_map(
        per_device, mesh=mesh, in_specs=in_specs, out_specs=out_specs, check_vma=False
    )
```

```python
import functools

import jax
import jax.numpy as jnp
from jax import lax
from jax.experimental import pallas as pl
from jax.experimental.pallas import tpu as pltpu
from jax.sharding import PartitionSpec as P

MESH = pl.DeviceIdType.MESH


def extended(block, sides, width):
    for axis, dim in sides:
        count = lax.axis_size(axis)
        forward = [(i, i + 1) for i in range(count - 1)]
        backward = [(target, source) for source, target in forward]
        low = lax.ppermute(
            lax.slice_in_dim(block, block.shape[dim] - width, None, axis=dim), axis, forward
        )
        high = lax.ppermute(lax.slice_in_dim(block, 0, width, axis=dim), axis, backward)
        block = jnp.concatenate([low, block, high], axis=dim)
    return block


def central(field, dimension):
    widths = [(0, 0)] * field.ndim
    widths[dimension] = (1, 1)
    padded = jnp.pad(field, widths)
    length = field.shape[dimension]
    return 0.5 * (
        lax.slice_in_dim(padded, 2, length + 2, axis=dimension)
        - lax.slice_in_dim(padded, 0, length, axis=dimension)
    )


def phase_term(obj_real, obj_imag, grad_x, grad_y, grad_z, qrow):
    term_x = obj_real * grad_x[:, :, 1] - obj_imag * grad_x[:, :, 0]
    term_y = obj_real * grad_y[:, :, 1] - obj_imag * grad_y[:, :, 0]
    term_z = obj_real * grad_z[:, :, 1] - obj_imag * grad_z[:, :, 0]
    return qrow[0] * term_x + qrow[1] * term_y + qrow[2] * term_z


def post_kernel(
    scalars, grid_ref, obj_ref, out_ref, halo, gathered, phase_buf, halo_send, halo_recv, send_sem, recv_sem,
    slab_count,
):
    refl_count = gathered.shape[0]
    planes, rows, width = grid_ref.shape[0], grid_ref.shape[2], grid_ref.shape[3]
    me = lax.axis_index("slab")
    refl = lax.axis_index("refl")
    up = lax.rem(me + 1, slab_count)
    down = lax.rem(me + slab_count - 1, slab_count)
    barrier = pltpu.get_barrier_semaphore()
    pl.semaphore_signal(barrier, 1, device_id=(refl, up), device_id_type=MESH)
    pl.semaphore_signal(barrier, 1, device_id=(refl, down), device_id_type=MESH)
    for step in range(1, refl_count):
        peer = lax.rem(refl + step, refl_count)
        pl.semaphore_signal(barrier, 1, device_id=(peer, me), device_id_type=MESH)
    pl.semaphore_wait(barrier, refl_count + 1)
    low_copy = pltpu.make_async_remote_copy(
        src_ref=grid_ref.at[planes - 1], dst_ref=halo.at[0], send_sem=halo_send.at[0],
        recv_sem=halo_recv.at[0], device_id=(refl, up), device_id_type=MESH,
    )
    high_copy = pltpu.make_async_remote_copy(
        src_ref=grid_ref.at[0], dst_ref=halo.at[1], send_sem=halo_send.at[1],
        recv_sem=halo_recv.at[1], device_id=(refl, down), device_id_type=MESH,
    )
    low_copy.start()
    high_copy.start()
    row_of = lax.broadcasted_iota(jnp.int32, (rows, width), 0)
    lane_of = lax.broadcasted_iota(jnp.int32, (rows, width), 1)

    def along_y(field):
        after = jnp.where(row_of == rows - 1, 0.0, pltpu.roll(field, rows - 1, 0))
        before = jnp.where(row_of == 0, 0.0, pltpu.roll(field, 1, 0))
        return 0.5 * (after - before)

    def along_w(field):
        after = jnp.where(lane_of == width - 1, 0.0, pltpu.roll(field, width - 1, 1))
        before = jnp.where(lane_of == 0, 0.0, pltpu.roll(field, 1, 1))
        return 0.5 * (after - before)

    mate = refl + 1 - 2 * lax.rem(refl, 2)
    q0, q1, q2 = scalars[refl, 0], scalars[refl, 1], scalars[refl, 2]
    d0 = q0 - scalars[mate, 0]
    d1 = q1 - scalars[mate, 1]
    d2 = q2 - scalars[mate, 2]
    partial = []
    for p in range(planes):
        obj_re, obj_im = obj_ref[p, 0], obj_ref[p, 1]
        term_y = obj_re * along_y(grid_ref[p, 1]) - obj_im * along_y(grid_ref[p, 0])
        term_z = obj_re * along_w(grid_ref[p, 1]) - obj_im * along_w(grid_ref[p, 0])
        partial.append((term_y, term_z))
    low_copy.wait_send()
    high_copy.wait_send()
    low_copy.wait_recv()
    high_copy.wait_recv()
    has_low = me > 0
    has_high = me < slab_count - 1
    for p in range(planes):
        obj_re, obj_im = obj_ref[p, 0], obj_ref[p, 1]
        grad = []
        for c in range(2):
            ahead = grid_ref[p + 1, c] if p + 1 < planes else jnp.where(has_high, halo[1, c], 0.0)
            behind = grid_ref[p - 1, c] if p > 0 else jnp.where(has_low, halo[0, c], 0.0)
            grad.append(0.5 * (ahead - behind))
        term_x = obj_re * grad[1] - obj_im * grad[0]
        term_y, term_z = partial[p]
        phase_buf[p] = q0 * term_x + q1 * term_y + q2 * term_z
    copies = []
    for step in range(1, refl_count):
        peer = lax.rem(refl + step, refl_count)
        copy = pltpu.make_async_remote_copy(
            src_ref=phase_buf, dst_ref=gathered.at[refl], send_sem=send_sem.at[step],
            recv_sem=recv_sem.at[step], device_id=(peer, me), device_id_type=MESH,
        )
        copy.start()
        copies.append(copy)
    gathered[refl] = phase_buf[...]
    for copy in copies:
        copy.wait_send()
    for step in range(1, refl_count):
        source = lax.rem(refl + refl_count - step, refl_count)
        pltpu.make_async_remote_copy(
            src_ref=phase_buf, dst_ref=gathered.at[source], send_sem=send_sem.at[step],
            recv_sem=recv_sem.at[step], device_id=(source, me), device_id_type=MESH,
        ).wait_recv()
    def weight(r):
        return scalars[r, 0] * d0 + scalars[r, 1] * d1 + scalars[r, 2] * d2

    shift = weight(0) * gathered[0]
    for r in range(1, refl_count):
        shift = shift + weight(r) * gathered[r]
    for p in range(planes):
        obj_re, obj_im = obj_ref[p, 0], obj_ref[p, 1]
        out_ref[p, 0] = obj_re - 0.5 * (grid_ref[p, 0] - obj_im * shift[p])
        out_ref[p, 1] = obj_im - 0.5 * (grid_ref[p, 1] + obj_re * shift[p])


def post_step(scalars, grid, obj, slab_count, refl_count):
    planes, _, rows, width = grid.shape
    return pl.pallas_call(
        functools.partial(post_kernel, slab_count=slab_count),
        out_shape=jax.ShapeDtypeStruct(grid.shape, jnp.float32),
        in_specs=[pl.BlockSpec(memory_space=pltpu.SMEM)]
        + [pl.BlockSpec(memory_space=pltpu.VMEM)] * 2,
        out_specs=pl.BlockSpec(memory_space=pltpu.VMEM),
        scratch_shapes=[
            pltpu.VMEM((2, 2, rows, width), jnp.float32),
            pltpu.VMEM((refl_count, planes, rows, width), jnp.float32),
            pltpu.VMEM((planes, rows, width), jnp.float32),
            pltpu.SemaphoreType.DMA((2,)),
            pltpu.SemaphoreType.DMA((2,)),
            pltpu.SemaphoreType.DMA((refl_count,)),
            pltpu.SemaphoreType.DMA((refl_count,)),
        ],
        compiler_params=pltpu.CompilerParams(collective_id=0, has_side_effects=True),
    )(scalars, grid, obj)


def exchange_kernel(
    slot_ref, values_ref, ids_ref, data_out, code_out, data_buf, code_in, data_send, data_recv, code_send,
    code_recv,
):
    count, capacity = data_out.shape[0], data_out.shape[1]
    group = 8 if count >= 16 else count // 2
    groups = count // group
    rows = group * capacity
    me = lax.axis_index("slab")
    refl = lax.axis_index("refl")
    barrier = pltpu.get_barrier_semaphore()

    def greet(step, carry):
        peer = lax.rem(me + step, count)
        pl.semaphore_signal(barrier, 1, device_id=(refl, peer), device_id_type=MESH)
        return carry

    lax.fori_loop(1, count, greet, 0)

    def pack(g):
        target = lax.broadcasted_iota(jnp.int32, (rows, slot_ref.shape[1]), 0) + g * rows
        chosen = (slot_ref[...] == target).astype(jnp.bfloat16)
        sent = jnp.dot(chosen, values_ref[...], preferred_element_type=jnp.float32)
        data_buf[pl.ds(g * group, group)] = sent.astype(jnp.bfloat16).reshape(
            group, capacity, sent.shape[1]
        )
        codes = lax.dot_general(
            ids_ref[...], chosen, (((1,), (1,)), ((), ())), preferred_element_type=jnp.float32
        )
        codes = (codes[0:1] * 8.0 + codes[1:2]).astype(jnp.int32)
        for part in range(group):
            window = (part * capacity) // 128
            code_in[g * group + part] = codes[:, window * 128 : (window + 1) * 128]

    def outgoing(d):
        data = pltpu.make_async_remote_copy(
            src_ref=data_buf.at[d], dst_ref=data_out.at[me], send_sem=data_send.at[d],
            recv_sem=data_recv.at[me], device_id=(refl, d), device_id_type=MESH,
        )
        code = pltpu.make_async_remote_copy(
            src_ref=code_in.at[d], dst_ref=code_out.at[me], send_sem=code_send.at[d],
            recv_sem=code_recv.at[me], device_id=(refl, d), device_id_type=MESH,
        )
        return data, code

    def incoming(s):
        data = pltpu.make_async_remote_copy(
            src_ref=data_buf.at[s], dst_ref=data_out.at[s], send_sem=data_send.at[s],
            recv_sem=data_recv.at[s], device_id=(refl, s), device_id_type=MESH,
        )
        code = pltpu.make_async_remote_copy(
            src_ref=code_in.at[s], dst_ref=code_out.at[s], send_sem=code_send.at[s],
            recv_sem=code_recv.at[s], device_id=(refl, s), device_id_type=MESH,
        )
        return data, code

    def send(g):
        for part in range(group):
            d = g * group + part

            @pl.when(d != me)
            def _():
                data, code = outgoing(d)
                code.start()
                data.start()

    home = me // group
    pack(home)
    pl.semaphore_wait(barrier, count - 1)
    send(home)

    def later(j, carry):
        g = lax.rem(home + j, groups)
        pack(g)
        send(g)
        return carry

    lax.fori_loop(1, groups, later, 0)
    data_out[me] = data_buf[me]
    local = pltpu.make_async_copy(code_in.at[me], code_out.at[me], code_send.at[me])
    local.start()

    def finish(step, carry):
        data, code = outgoing(lax.rem(me + step, count))
        data.wait_send()
        code.wait_send()
        data, code = incoming(lax.rem(me + count - step, count))
        data.wait_recv()
        code.wait_recv()
        return carry

    lax.fori_loop(1, count, finish, 0)
    local.wait()


def exchange_slab(flat_slot, values, ids, count, capacity):
    data_shape = (count, capacity, values.shape[1])
    code_shape = (count, 1, 128)
    return pl.pallas_call(
        exchange_kernel,
        out_shape=(
            jax.ShapeDtypeStruct(data_shape, jnp.bfloat16),
            jax.ShapeDtypeStruct(code_shape, jnp.int32),
        ),
        in_specs=[pl.BlockSpec(memory_space=pltpu.VMEM)] * 3,
        out_specs=(pl.BlockSpec(memory_space=pltpu.VMEM), pl.BlockSpec(memory_space=pl.ANY)),
        scratch_shapes=[
            pltpu.VMEM(data_shape, jnp.bfloat16),
            pltpu.VMEM(code_shape, jnp.int32),
            pltpu.SemaphoreType.DMA((count,)),
            pltpu.SemaphoreType.DMA((count,)),
            pltpu.SemaphoreType.DMA((count,)),
            pltpu.SemaphoreType.DMA((count,)),
        ],
        compiler_params=pltpu.CompilerParams(collective_id=1, has_side_effects=True),
    )(flat_slot, values, ids)


def per_device(detector, owners, block_ids, kernel_ids, kernels, bragg_vectors, object_field):
    slab_count = lax.axis_size("slab")
    plane_count = object_field.shape[1]
    row_count = object_field.shape[2]
    block_count = plane_count * row_count
    kernel_count = kernels.shape[0]
    tile_count = detector.shape[1]
    tile_width = detector.shape[3]
    row_width = 2 * tile_width
    capacity = 2 * tile_count // slab_count
    values = detector[0].reshape(tile_count, row_width)
    owner = owners[0, :, 0]
    order = lax.broadcasted_iota(jnp.int32, (tile_count, tile_count), 1) < lax.broadcasted_iota(
        jnp.int32, (tile_count, tile_count), 0
    )
    same = (owner[:, None] == owner[None, :]) & order
    slots = jnp.sum(same.astype(jnp.int32), axis=1)
    flat_slot = owner * capacity + slots
    ids = jnp.concatenate(
        [block_ids, kernel_ids, jnp.zeros((6, tile_count), jnp.int32)], axis=0
    ).astype(jnp.bfloat16)
    got, got_code = exchange_slab(flat_slot[None, :], values, ids, slab_count, capacity)
    row_total = slab_count * capacity
    rows = got.reshape(row_total, row_width)
    offset = lax.rem(lax.axis_index("slab"), 4) * capacity
    got_codes = lax.dynamic_slice_in_dim(got_code[:, 0, :], offset, capacity, axis=1).reshape(row_total)
    chosen = (
        got_codes[None, :]
        == lax.broadcasted_iota(jnp.int32, (block_count * kernel_count, row_total), 0)
    ).astype(jnp.bfloat16)
    summed = jnp.dot(chosen, rows, preferred_element_type=jnp.float32)
    summed = summed.reshape(block_count, kernel_count, 2, tile_width).transpose(0, 2, 1, 3)
    gridded = jnp.dot(
        summed.reshape(block_count * 2, kernel_count * tile_width),
        kernels.astype(jnp.float32).reshape(kernel_count * tile_width, tile_width),
        precision=lax.Precision.HIGHEST,
        preferred_element_type=jnp.float32,
    )
    gridded = gridded.reshape(plane_count, row_count, 2, tile_width).transpose(0, 2, 1, 3)
    refl_count = bragg_vectors.shape[0]
    obj = object_field[0].transpose(0, 2, 1, 3)
    updated = post_step(bragg_vectors, gridded, obj, slab_count, refl_count)
    return updated.transpose(0, 2, 1, 3)[None]


def solution(mesh):
    in_specs = (
        P("refl", "slab", None, None),
        P("refl", "slab", None),
        P("refl", "slab"),
        P("refl", "slab"),
        P(),
        P(),
        P("refl", "slab", None, None, None),
    )
    out_specs = P("refl", "slab", None, None, None)
    return jax.shard_map(
        per_device, mesh=mesh, in_specs=in_specs, out_specs=out_specs, check_vma=False
    )
```

```python
import functools

import jax
import jax.numpy as jnp
from jax import lax
from jax.experimental import pallas as pl
from jax.experimental.pallas import tpu as pltpu
from jax.sharding import PartitionSpec as P

MESH = pl.DeviceIdType.MESH


def extended(block, sides, width):
    for axis, dim in sides:
        count = lax.axis_size(axis)
        forward = [(i, i + 1) for i in range(count - 1)]
        backward = [(target, source) for source, target in forward]
        low = lax.ppermute(
            lax.slice_in_dim(block, block.shape[dim] - width, None, axis=dim), axis, forward
        )
        high = lax.ppermute(lax.slice_in_dim(block, 0, width, axis=dim), axis, backward)
        block = jnp.concatenate([low, block, high], axis=dim)
    return block


def central(field, dimension):
    widths = [(0, 0)] * field.ndim
    widths[dimension] = (1, 1)
    padded = jnp.pad(field, widths)
    length = field.shape[dimension]
    return 0.5 * (
        lax.slice_in_dim(padded, 2, length + 2, axis=dimension)
        - lax.slice_in_dim(padded, 0, length, axis=dimension)
    )


def phase_term(obj_real, obj_imag, grad_x, grad_y, grad_z, qrow):
    term_x = obj_real * grad_x[:, :, 1] - obj_imag * grad_x[:, :, 0]
    term_y = obj_real * grad_y[:, :, 1] - obj_imag * grad_y[:, :, 0]
    term_z = obj_real * grad_z[:, :, 1] - obj_imag * grad_z[:, :, 0]
    return qrow[0] * term_x + qrow[1] * term_y + qrow[2] * term_z


def post_kernel(
    scalars, grid_ref, obj_ref, out_ref, halo, gathered, phase_buf, halo_send, halo_recv, send_sem, recv_sem,
    slab_count,
):
    refl_count = gathered.shape[0]
    planes, rows, width = grid_ref.shape[0], grid_ref.shape[2], grid_ref.shape[3]
    me = lax.axis_index("slab")
    refl = lax.axis_index("refl")
    up = lax.rem(me + 1, slab_count)
    down = lax.rem(me + slab_count - 1, slab_count)
    barrier = pltpu.get_barrier_semaphore()
    pl.semaphore_signal(barrier, 1, device_id=(refl, up), device_id_type=MESH)
    pl.semaphore_signal(barrier, 1, device_id=(refl, down), device_id_type=MESH)
    for step in range(1, refl_count):
        peer = lax.rem(refl + step, refl_count)
        pl.semaphore_signal(barrier, 1, device_id=(peer, me), device_id_type=MESH)
    pl.semaphore_wait(barrier, refl_count + 1)
    low_copy = pltpu.make_async_remote_copy(
        src_ref=grid_ref.at[planes - 1], dst_ref=halo.at[0], send_sem=halo_send.at[0],
        recv_sem=halo_recv.at[0], device_id=(refl, up), device_id_type=MESH,
    )
    high_copy = pltpu.make_async_remote_copy(
        src_ref=grid_ref.at[0], dst_ref=halo.at[1], send_sem=halo_send.at[1],
        recv_sem=halo_recv.at[1], device_id=(refl, down), device_id_type=MESH,
    )
    low_copy.start()
    high_copy.start()
    row_of = lax.broadcasted_iota(jnp.int32, (rows, width), 0)
    lane_of = lax.broadcasted_iota(jnp.int32, (rows, width), 1)

    def along_y(field):
        after = jnp.where(row_of == rows - 1, 0.0, pltpu.roll(field, rows - 1, 0))
        before = jnp.where(row_of == 0, 0.0, pltpu.roll(field, 1, 0))
        return 0.5 * (after - before)

    def along_w(field):
        after = jnp.where(lane_of == width - 1, 0.0, pltpu.roll(field, width - 1, 1))
        before = jnp.where(lane_of == 0, 0.0, pltpu.roll(field, 1, 1))
        return 0.5 * (after - before)

    mate = refl + 1 - 2 * lax.rem(refl, 2)
    q0, q1, q2 = scalars[refl, 0], scalars[refl, 1], scalars[refl, 2]
    d0 = q0 - scalars[mate, 0]
    d1 = q1 - scalars[mate, 1]
    d2 = q2 - scalars[mate, 2]
    partial = []
    for p in range(planes):
        obj_re, obj_im = obj_ref[p, 0], obj_ref[p, 1]
        term_y = obj_re * along_y(grid_ref[p, 1]) - obj_im * along_y(grid_ref[p, 0])
        term_z = obj_re * along_w(grid_ref[p, 1]) - obj_im * along_w(grid_ref[p, 0])
        partial.append((term_y, term_z))
    low_copy.wait_send()
    high_copy.wait_send()
    low_copy.wait_recv()
    high_copy.wait_recv()
    has_low = me > 0
    has_high = me < slab_count - 1
    for p in range(planes):
        obj_re, obj_im = obj_ref[p, 0], obj_ref[p, 1]
        grad = []
        for c in range(2):
            ahead = grid_ref[p + 1, c] if p + 1 < planes else jnp.where(has_high, halo[1, c], 0.0)
            behind = grid_ref[p - 1, c] if p > 0 else jnp.where(has_low, halo[0, c], 0.0)
            grad.append(0.5 * (ahead - behind))
        term_x = obj_re * grad[1] - obj_im * grad[0]
        term_y, term_z = partial[p]
        phase_buf[p] = q0 * term_x + q1 * term_y + q2 * term_z
    copies = []
    for step in range(1, refl_count):
        peer = lax.rem(refl + step, refl_count)
        copy = pltpu.make_async_remote_copy(
            src_ref=phase_buf, dst_ref=gathered.at[refl], send_sem=send_sem.at[step],
            recv_sem=recv_sem.at[step], device_id=(peer, me), device_id_type=MESH,
        )
        copy.start()
        copies.append(copy)
    gathered[refl] = phase_buf[...]
    for copy in copies:
        copy.wait_send()
    for step in range(1, refl_count):
        source = lax.rem(refl + refl_count - step, refl_count)
        pltpu.make_async_remote_copy(
            src_ref=phase_buf, dst_ref=gathered.at[source], send_sem=send_sem.at[step],
            recv_sem=recv_sem.at[step], device_id=(source, me), device_id_type=MESH,
        ).wait_recv()
    def weight(r):
        return scalars[r, 0] * d0 + scalars[r, 1] * d1 + scalars[r, 2] * d2

    shift = weight(0) * gathered[0]
    for r in range(1, refl_count):
        shift = shift + weight(r) * gathered[r]
    for p in range(planes):
        obj_re, obj_im = obj_ref[p, 0], obj_ref[p, 1]
        out_ref[p, 0] = obj_re - 0.5 * (grid_ref[p, 0] - obj_im * shift[p])
        out_ref[p, 1] = obj_im - 0.5 * (grid_ref[p, 1] + obj_re * shift[p])


def post_step(scalars, grid, obj, slab_count, refl_count):
    planes, _, rows, width = grid.shape
    return pl.pallas_call(
        functools.partial(post_kernel, slab_count=slab_count),
        out_shape=jax.ShapeDtypeStruct(grid.shape, jnp.float32),
        in_specs=[pl.BlockSpec(memory_space=pltpu.SMEM)]
        + [pl.BlockSpec(memory_space=pltpu.VMEM)] * 2,
        out_specs=pl.BlockSpec(memory_space=pltpu.VMEM),
        scratch_shapes=[
            pltpu.VMEM((2, 2, rows, width), jnp.float32),
            pltpu.VMEM((refl_count, planes, rows, width), jnp.float32),
            pltpu.VMEM((planes, rows, width), jnp.float32),
            pltpu.SemaphoreType.DMA((2,)),
            pltpu.SemaphoreType.DMA((2,)),
            pltpu.SemaphoreType.DMA((refl_count,)),
            pltpu.SemaphoreType.DMA((refl_count,)),
        ],
        compiler_params=pltpu.CompilerParams(collective_id=0, has_side_effects=True),
    )(scalars, grid, obj)


def exchange_kernel(
    slot_ref, values_ref, ids_ref, data_out, code_out, data_buf, code_in, data_send, data_recv, code_send,
    code_recv,
):
    count, capacity = data_out.shape[0], data_out.shape[1]
    group = 8 if count >= 16 else count // 2
    groups = count // group
    rows = group * capacity
    me = lax.axis_index("slab")
    refl = lax.axis_index("refl")
    barrier = pltpu.get_barrier_semaphore()

    def greet(step, carry):
        peer = lax.rem(me + step, count)
        pl.semaphore_signal(barrier, 1, device_id=(refl, peer), device_id_type=MESH)
        return carry

    lax.fori_loop(1, count, greet, 0)

    def pack(g):
        target = lax.broadcasted_iota(jnp.int32, (rows, slot_ref.shape[1]), 0) + g * rows
        chosen = (slot_ref[...] == target).astype(jnp.bfloat16)
        sent = jnp.dot(chosen, values_ref[...], preferred_element_type=jnp.float32)
        data_buf[pl.ds(g * group, group)] = sent.astype(jnp.bfloat16).reshape(
            group, capacity, sent.shape[1]
        )
        codes = lax.dot_general(
            ids_ref[...], chosen, (((1,), (1,)), ((), ())), preferred_element_type=jnp.float32
        )
        codes = (codes[0:1] * 8.0 + codes[1:2]).astype(jnp.int32)
        for part in range(group):
            window = (part * capacity) // 128
            code_in[g * group + part] = codes[:, window * 128 : (window + 1) * 128]

    def outgoing(d):
        data = pltpu.make_async_remote_copy(
            src_ref=data_buf.at[d], dst_ref=data_out.at[me], send_sem=data_send.at[d],
            recv_sem=data_recv.at[me], device_id=(refl, d), device_id_type=MESH,
        )
        code = pltpu.make_async_remote_copy(
            src_ref=code_in.at[d], dst_ref=code_out.at[me], send_sem=code_send.at[d],
            recv_sem=code_recv.at[me], device_id=(refl, d), device_id_type=MESH,
        )
        return data, code

    def incoming(s):
        data = pltpu.make_async_remote_copy(
            src_ref=data_buf.at[s], dst_ref=data_out.at[s], send_sem=data_send.at[s],
            recv_sem=data_recv.at[s], device_id=(refl, s), device_id_type=MESH,
        )
        code = pltpu.make_async_remote_copy(
            src_ref=code_in.at[s], dst_ref=code_out.at[s], send_sem=code_send.at[s],
            recv_sem=code_recv.at[s], device_id=(refl, s), device_id_type=MESH,
        )
        return data, code

    def send(g):
        for part in range(group):
            d = g * group + part

            @pl.when(d != me)
            def _():
                data, code = outgoing(d)
                code.start()
                data.start()

    home = me // group
    middle = groups // 2

    def order(j):
        return lax.rem(home + middle + (1 - 2 * lax.rem(j, 2)) * ((j + 1) // 2) + groups, groups)

    first = order(0)
    pack(first)
    pl.semaphore_wait(barrier, count - 1)
    send(first)

    def later(j, carry):
        g = order(j)
        pack(g)
        send(g)
        return carry

    lax.fori_loop(1, groups, later, 0)
    data_out[me] = data_buf[me]
    local = pltpu.make_async_copy(code_in.at[me], code_out.at[me], code_send.at[me])
    local.start()

    def finish(step, carry):
        data, code = outgoing(lax.rem(me + step, count))
        data.wait_send()
        code.wait_send()
        data, code = incoming(lax.rem(me + count - step, count))
        data.wait_recv()
        code.wait_recv()
        return carry

    lax.fori_loop(1, count, finish, 0)
    local.wait()


def exchange_slab(flat_slot, values, ids, count, capacity):
    data_shape = (count, capacity, values.shape[1])
    code_shape = (count, 1, 128)
    return pl.pallas_call(
        exchange_kernel,
        out_shape=(
            jax.ShapeDtypeStruct(data_shape, jnp.bfloat16),
            jax.ShapeDtypeStruct(code_shape, jnp.int32),
        ),
        in_specs=[pl.BlockSpec(memory_space=pltpu.VMEM)] * 3,
        out_specs=(pl.BlockSpec(memory_space=pltpu.VMEM), pl.BlockSpec(memory_space=pl.ANY)),
        scratch_shapes=[
            pltpu.VMEM(data_shape, jnp.bfloat16),
            pltpu.VMEM(code_shape, jnp.int32),
            pltpu.SemaphoreType.DMA((count,)),
            pltpu.SemaphoreType.DMA((count,)),
            pltpu.SemaphoreType.DMA((count,)),
            pltpu.SemaphoreType.DMA((count,)),
        ],
        compiler_params=pltpu.CompilerParams(collective_id=1, has_side_effects=True),
    )(flat_slot, values, ids)


def per_device(detector, owners, block_ids, kernel_ids, kernels, bragg_vectors, object_field):
    slab_count = lax.axis_size("slab")
    plane_count = object_field.shape[1]
    row_count = object_field.shape[2]
    block_count = plane_count * row_count
    kernel_count = kernels.shape[0]
    tile_count = detector.shape[1]
    tile_width = detector.shape[3]
    row_width = 2 * tile_width
    capacity = 2 * tile_count // slab_count
    values = detector[0].reshape(tile_count, row_width)
    owner = owners[0, :, 0]
    order = lax.broadcasted_iota(jnp.int32, (tile_count, tile_count), 1) < lax.broadcasted_iota(
        jnp.int32, (tile_count, tile_count), 0
    )
    same = (owner[:, None] == owner[None, :]) & order
    slots = jnp.sum(same.astype(jnp.int32), axis=1)
    flat_slot = owner * capacity + slots
    ids = jnp.concatenate(
        [block_ids, kernel_ids, jnp.zeros((6, tile_count), jnp.int32)], axis=0
    ).astype(jnp.bfloat16)
    got, got_code = exchange_slab(flat_slot[None, :], values, ids, slab_count, capacity)
    row_total = slab_count * capacity
    rows = got.reshape(row_total, row_width)
    offset = lax.rem(lax.axis_index("slab"), 4) * capacity
    got_codes = lax.dynamic_slice_in_dim(got_code[:, 0, :], offset, capacity, axis=1).reshape(row_total)
    chosen = (
        got_codes[None, :]
        == lax.broadcasted_iota(jnp.int32, (block_count * kernel_count, row_total), 0)
    ).astype(jnp.bfloat16)
    summed = jnp.dot(chosen, rows, preferred_element_type=jnp.float32)
    summed = summed.reshape(block_count, kernel_count, 2, tile_width).transpose(0, 2, 1, 3)
    gridded = jnp.dot(
        summed.reshape(block_count * 2, kernel_count * tile_width),
        kernels.astype(jnp.float32).reshape(kernel_count * tile_width, tile_width),
        precision=lax.Precision.HIGHEST,
        preferred_element_type=jnp.float32,
    )
    gridded = gridded.reshape(plane_count, row_count, 2, tile_width).transpose(0, 2, 1, 3)
    refl_count = bragg_vectors.shape[0]
    obj = object_field[0].transpose(0, 2, 1, 3)
    updated = post_step(bragg_vectors, gridded, obj, slab_count, refl_count)
    return updated.transpose(0, 2, 1, 3)[None]


def solution(mesh):
    in_specs = (
        P("refl", "slab", None, None),
        P("refl", "slab", None),
        P("refl", "slab"),
        P("refl", "slab"),
        P(),
        P(),
        P("refl", "slab", None, None, None),
    )
    out_specs = P("refl", "slab", None, None, None)
    return jax.shard_map(
        per_device, mesh=mesh, in_specs=in_specs, out_specs=out_specs, check_vma=False
    )
```

```python
import functools

import jax
import jax.numpy as jnp
from jax import lax
from jax.experimental import pallas as pl
from jax.experimental.pallas import tpu as pltpu
from jax.sharding import PartitionSpec as P

MESH = pl.DeviceIdType.MESH


def extended(block, sides, width):
    for axis, dim in sides:
        count = lax.axis_size(axis)
        forward = [(i, i + 1) for i in range(count - 1)]
        backward = [(target, source) for source, target in forward]
        low = lax.ppermute(
            lax.slice_in_dim(block, block.shape[dim] - width, None, axis=dim), axis, forward
        )
        high = lax.ppermute(lax.slice_in_dim(block, 0, width, axis=dim), axis, backward)
        block = jnp.concatenate([low, block, high], axis=dim)
    return block


def central(field, dimension):
    widths = [(0, 0)] * field.ndim
    widths[dimension] = (1, 1)
    padded = jnp.pad(field, widths)
    length = field.shape[dimension]
    return 0.5 * (
        lax.slice_in_dim(padded, 2, length + 2, axis=dimension)
        - lax.slice_in_dim(padded, 0, length, axis=dimension)
    )


def phase_term(obj_real, obj_imag, grad_x, grad_y, grad_z, qrow):
    term_x = obj_real * grad_x[:, :, 1] - obj_imag * grad_x[:, :, 0]
    term_y = obj_real * grad_y[:, :, 1] - obj_imag * grad_y[:, :, 0]
    term_z = obj_real * grad_z[:, :, 1] - obj_imag * grad_z[:, :, 0]
    return qrow[0] * term_x + qrow[1] * term_y + qrow[2] * term_z


def post_kernel(
    scalars, grid_ref, obj_ref, out_ref, halo, gathered, phase_buf, partial_buf, mate_buf,
    halo_send, halo_recv, send_sem, recv_sem, mate_send, mate_recv, slab_count, refl_count,
):
    share = gathered.shape[0]
    planes, rows, width = grid_ref.shape[0], grid_ref.shape[2], grid_ref.shape[3]
    me = lax.axis_index("slab")
    refl = lax.axis_index("refl")
    up = lax.rem(me + 1, slab_count)
    down = lax.rem(me + slab_count - 1, slab_count)
    barrier = pltpu.get_barrier_semaphore()
    pl.semaphore_signal(barrier, 1, device_id=(refl, up), device_id_type=MESH)
    pl.semaphore_signal(barrier, 1, device_id=(refl, down), device_id_type=MESH)
    mate = refl + 1 - 2 * lax.rem(refl, 2)
    for step in range(1, share):
        peer = lax.rem(refl + 2 * step, refl_count)
        pl.semaphore_signal(barrier, 1, device_id=(peer, me), device_id_type=MESH)
    pl.semaphore_signal(barrier, 1, device_id=(mate, me), device_id_type=MESH)
    pl.semaphore_wait(barrier, share + 2)
    low_copy = pltpu.make_async_remote_copy(
        src_ref=grid_ref.at[planes - 1], dst_ref=halo.at[0], send_sem=halo_send.at[0],
        recv_sem=halo_recv.at[0], device_id=(refl, up), device_id_type=MESH,
    )
    high_copy = pltpu.make_async_remote_copy(
        src_ref=grid_ref.at[0], dst_ref=halo.at[1], send_sem=halo_send.at[1],
        recv_sem=halo_recv.at[1], device_id=(refl, down), device_id_type=MESH,
    )
    low_copy.start()
    high_copy.start()
    row_of = lax.broadcasted_iota(jnp.int32, (rows, width), 0)
    lane_of = lax.broadcasted_iota(jnp.int32, (rows, width), 1)

    def along_y(field):
        after = jnp.where(row_of == rows - 1, 0.0, pltpu.roll(field, rows - 1, 0))
        before = jnp.where(row_of == 0, 0.0, pltpu.roll(field, 1, 0))
        return 0.5 * (after - before)

    def along_w(field):
        after = jnp.where(lane_of == width - 1, 0.0, pltpu.roll(field, width - 1, 1))
        before = jnp.where(lane_of == 0, 0.0, pltpu.roll(field, 1, 1))
        return 0.5 * (after - before)

    mate = refl + 1 - 2 * lax.rem(refl, 2)
    q0, q1, q2 = scalars[refl, 0], scalars[refl, 1], scalars[refl, 2]
    d0 = q0 - scalars[mate, 0]
    d1 = q1 - scalars[mate, 1]
    d2 = q2 - scalars[mate, 2]
    partial = []
    for p in range(planes):
        obj_re, obj_im = obj_ref[p, 0], obj_ref[p, 1]
        term_y = obj_re * along_y(grid_ref[p, 1]) - obj_im * along_y(grid_ref[p, 0])
        term_z = obj_re * along_w(grid_ref[p, 1]) - obj_im * along_w(grid_ref[p, 0])
        partial.append((term_y, term_z))
    low_copy.wait_send()
    high_copy.wait_send()
    low_copy.wait_recv()
    high_copy.wait_recv()
    has_low = me > 0
    has_high = me < slab_count - 1
    for p in range(planes):
        obj_re, obj_im = obj_ref[p, 0], obj_ref[p, 1]
        grad = []
        for c in range(2):
            ahead = grid_ref[p + 1, c] if p + 1 < planes else jnp.where(has_high, halo[1, c], 0.0)
            behind = grid_ref[p - 1, c] if p > 0 else jnp.where(has_low, halo[0, c], 0.0)
            grad.append(0.5 * (ahead - behind))
        term_x = obj_re * grad[1] - obj_im * grad[0]
        term_y, term_z = partial[p]
        phase_buf[p] = q0 * term_x + q1 * term_y + q2 * term_z
    copies = []
    for step in range(1, share):
        peer = lax.rem(refl + 2 * step, refl_count)
        copy = pltpu.make_async_remote_copy(
            src_ref=phase_buf, dst_ref=gathered.at[step], send_sem=send_sem.at[step],
            recv_sem=recv_sem.at[step], device_id=(peer, me), device_id_type=MESH,
        )
        copy.start()
        copies.append(copy)
    gathered[0] = phase_buf[...]
    for copy in copies:
        copy.wait_send()
    for step in range(1, share):
        source = lax.rem(refl + refl_count - 2 * step, refl_count)
        pltpu.make_async_remote_copy(
            src_ref=phase_buf, dst_ref=gathered.at[step], send_sem=send_sem.at[step],
            recv_sem=recv_sem.at[step], device_id=(source, me), device_id_type=MESH,
        ).wait_recv()

    def weight(r):
        return scalars[r, 0] * d0 + scalars[r, 1] * d1 + scalars[r, 2] * d2

    own = weight(refl) * gathered[0]
    for step in range(1, share):
        own = own + weight(lax.rem(refl + refl_count - 2 * step, refl_count)) * gathered[step]
    partial_buf[...] = own
    to_mate = pltpu.make_async_remote_copy(
        src_ref=partial_buf, dst_ref=mate_buf, send_sem=mate_send.at[0], recv_sem=mate_recv.at[0],
        device_id=(mate, me), device_id_type=MESH,
    )
    to_mate.start()
    to_mate.wait_send()
    to_mate.wait_recv()
    shift = partial_buf[...] - mate_buf[...]
    for p in range(planes):
        obj_re, obj_im = obj_ref[p, 0], obj_ref[p, 1]
        out_ref[p, 0] = obj_re - 0.5 * (grid_ref[p, 0] - obj_im * shift[p])
        out_ref[p, 1] = obj_im - 0.5 * (grid_ref[p, 1] + obj_re * shift[p])


def post_step(scalars, grid, obj, slab_count, refl_count):
    planes, _, rows, width = grid.shape
    share = refl_count // 2
    return pl.pallas_call(
        functools.partial(post_kernel, slab_count=slab_count, refl_count=refl_count),
        out_shape=jax.ShapeDtypeStruct(grid.shape, jnp.float32),
        in_specs=[pl.BlockSpec(memory_space=pltpu.SMEM)]
        + [pl.BlockSpec(memory_space=pltpu.VMEM)] * 2,
        out_specs=pl.BlockSpec(memory_space=pltpu.VMEM),
        scratch_shapes=[
            pltpu.VMEM((2, 2, rows, width), jnp.float32),
            pltpu.VMEM((share, planes, rows, width), jnp.float32),
            pltpu.VMEM((planes, rows, width), jnp.float32),
            pltpu.VMEM((planes, rows, width), jnp.float32),
            pltpu.VMEM((planes, rows, width), jnp.float32),
            pltpu.SemaphoreType.DMA((2,)),
            pltpu.SemaphoreType.DMA((2,)),
            pltpu.SemaphoreType.DMA((share,)),
            pltpu.SemaphoreType.DMA((share,)),
            pltpu.SemaphoreType.DMA((1,)),
            pltpu.SemaphoreType.DMA((1,)),
        ],
        compiler_params=pltpu.CompilerParams(collective_id=0, has_side_effects=True),
    )(scalars, grid, obj)


def exchange_kernel(
    slot_ref, values_ref, ids_ref, data_out, code_out, data_buf, code_in, data_send, data_recv, code_send,
    code_recv,
):
    count, capacity = data_out.shape[0], data_out.shape[1]
    group = 8 if count >= 16 else count // 2
    groups = count // group
    rows = group * capacity
    me = lax.axis_index("slab")
    refl = lax.axis_index("refl")
    barrier = pltpu.get_barrier_semaphore()

    def greet(step, carry):
        peer = lax.rem(me + step, count)
        pl.semaphore_signal(barrier, 1, device_id=(refl, peer), device_id_type=MESH)
        return carry

    lax.fori_loop(1, count, greet, 0)

    def pack(g):
        target = lax.broadcasted_iota(jnp.int32, (rows, slot_ref.shape[1]), 0) + g * rows
        chosen = (slot_ref[...] == target).astype(jnp.bfloat16)
        sent = jnp.dot(chosen, values_ref[...], preferred_element_type=jnp.float32)
        data_buf[pl.ds(g * group, group)] = sent.astype(jnp.bfloat16).reshape(
            group, capacity, sent.shape[1]
        )
        codes = lax.dot_general(
            ids_ref[...], chosen, (((1,), (1,)), ((), ())), preferred_element_type=jnp.float32
        )
        codes = (codes[0:1] * 8.0 + codes[1:2]).astype(jnp.int32)
        for part in range(group):
            window = (part * capacity) // 128
            code_in[g * group + part] = codes[:, window * 128 : (window + 1) * 128]

    def outgoing(d):
        data = pltpu.make_async_remote_copy(
            src_ref=data_buf.at[d], dst_ref=data_out.at[me], send_sem=data_send.at[d],
            recv_sem=data_recv.at[me], device_id=(refl, d), device_id_type=MESH,
        )
        code = pltpu.make_async_remote_copy(
            src_ref=code_in.at[d], dst_ref=code_out.at[me], send_sem=code_send.at[d],
            recv_sem=code_recv.at[me], device_id=(refl, d), device_id_type=MESH,
        )
        return data, code

    def incoming(s):
        data = pltpu.make_async_remote_copy(
            src_ref=data_buf.at[s], dst_ref=data_out.at[s], send_sem=data_send.at[s],
            recv_sem=data_recv.at[s], device_id=(refl, s), device_id_type=MESH,
        )
        code = pltpu.make_async_remote_copy(
            src_ref=code_in.at[s], dst_ref=code_out.at[s], send_sem=code_send.at[s],
            recv_sem=code_recv.at[s], device_id=(refl, s), device_id_type=MESH,
        )
        return data, code

    def send(g):
        for part in range(group):
            d = g * group + part

            @pl.when(d != me)
            def _():
                data, code = outgoing(d)
                code.start()
                data.start()

    home = me // group
    middle = groups // 2

    def order(j):
        return lax.rem(home + middle + (1 - 2 * lax.rem(j, 2)) * ((j + 1) // 2) + groups, groups)

    first = order(0)
    pack(first)
    pl.semaphore_wait(barrier, count - 1)
    send(first)

    def later(j, carry):
        g = order(j)
        pack(g)
        send(g)
        return carry

    lax.fori_loop(1, groups, later, 0)
    data_out[me] = data_buf[me]
    local = pltpu.make_async_copy(code_in.at[me], code_out.at[me], code_send.at[me])
    local.start()

    def finish(step, carry):
        data, code = outgoing(lax.rem(me + step, count))
        data.wait_send()
        code.wait_send()
        data, code = incoming(lax.rem(me + count - step, count))
        data.wait_recv()
        code.wait_recv()
        return carry

    lax.fori_loop(1, count, finish, 0)
    local.wait()


def exchange_slab(flat_slot, values, ids, count, capacity):
    data_shape = (count, capacity, values.shape[1])
    code_shape = (count, 1, 128)
    return pl.pallas_call(
        exchange_kernel,
        out_shape=(
            jax.ShapeDtypeStruct(data_shape, jnp.bfloat16),
            jax.ShapeDtypeStruct(code_shape, jnp.int32),
        ),
        in_specs=[pl.BlockSpec(memory_space=pltpu.VMEM)] * 3,
        out_specs=(pl.BlockSpec(memory_space=pltpu.VMEM), pl.BlockSpec(memory_space=pl.ANY)),
        scratch_shapes=[
            pltpu.VMEM(data_shape, jnp.bfloat16),
            pltpu.VMEM(code_shape, jnp.int32),
            pltpu.SemaphoreType.DMA((count,)),
            pltpu.SemaphoreType.DMA((count,)),
            pltpu.SemaphoreType.DMA((count,)),
            pltpu.SemaphoreType.DMA((count,)),
        ],
        compiler_params=pltpu.CompilerParams(collective_id=1, has_side_effects=True),
    )(flat_slot, values, ids)


def per_device(detector, owners, block_ids, kernel_ids, kernels, bragg_vectors, object_field):
    slab_count = lax.axis_size("slab")
    plane_count = object_field.shape[1]
    row_count = object_field.shape[2]
    block_count = plane_count * row_count
    kernel_count = kernels.shape[0]
    tile_count = detector.shape[1]
    tile_width = detector.shape[3]
    row_width = 2 * tile_width
    capacity = 2 * tile_count // slab_count
    values = detector[0].reshape(tile_count, row_width)
    owner = owners[0, :, 0]
    order = lax.broadcasted_iota(jnp.int32, (tile_count, tile_count), 1) < lax.broadcasted_iota(
        jnp.int32, (tile_count, tile_count), 0
    )
    same = (owner[:, None] == owner[None, :]) & order
    slots = jnp.sum(same.astype(jnp.int32), axis=1)
    flat_slot = owner * capacity + slots
    ids = jnp.concatenate(
        [block_ids, kernel_ids, jnp.zeros((6, tile_count), jnp.int32)], axis=0
    ).astype(jnp.bfloat16)
    got, got_code = exchange_slab(flat_slot[None, :], values, ids, slab_count, capacity)
    row_total = slab_count * capacity
    rows = got.reshape(row_total, row_width)
    offset = lax.rem(lax.axis_index("slab"), 4) * capacity
    got_codes = lax.dynamic_slice_in_dim(got_code[:, 0, :], offset, capacity, axis=1).reshape(row_total)
    chosen = (
        got_codes[None, :]
        == lax.broadcasted_iota(jnp.int32, (block_count * kernel_count, row_total), 0)
    ).astype(jnp.bfloat16)
    summed = jnp.dot(chosen, rows, preferred_element_type=jnp.float32)
    summed = summed.reshape(block_count, kernel_count, 2, tile_width).transpose(0, 2, 1, 3)
    gridded = jnp.dot(
        summed.reshape(block_count * 2, kernel_count * tile_width),
        kernels.astype(jnp.float32).reshape(kernel_count * tile_width, tile_width),
        precision=lax.Precision.HIGHEST,
        preferred_element_type=jnp.float32,
    )
    gridded = gridded.reshape(plane_count, row_count, 2, tile_width).transpose(0, 2, 1, 3)
    refl_count = bragg_vectors.shape[0]
    obj = object_field[0].transpose(0, 2, 1, 3)
    updated = post_step(bragg_vectors, gridded, obj, slab_count, refl_count)
    return updated.transpose(0, 2, 1, 3)[None]


def solution(mesh):
    in_specs = (
        P("refl", "slab", None, None),
        P("refl", "slab", None),
        P("refl", "slab"),
        P("refl", "slab"),
        P(),
        P(),
        P("refl", "slab", None, None, None),
    )
    out_specs = P("refl", "slab", None, None, None)
    return jax.shard_map(
        per_device, mesh=mesh, in_specs=in_specs, out_specs=out_specs, check_vma=False
    )
```

```python
import functools

import jax
import jax.numpy as jnp
from jax import lax
from jax.experimental import pallas as pl
from jax.experimental.pallas import tpu as pltpu
from jax.sharding import PartitionSpec as P

MESH = pl.DeviceIdType.MESH


def extended(block, sides, width):
    for axis, dim in sides:
        count = lax.axis_size(axis)
        forward = [(i, i + 1) for i in range(count - 1)]
        backward = [(target, source) for source, target in forward]
        low = lax.ppermute(
            lax.slice_in_dim(block, block.shape[dim] - width, None, axis=dim), axis, forward
        )
        high = lax.ppermute(lax.slice_in_dim(block, 0, width, axis=dim), axis, backward)
        block = jnp.concatenate([low, block, high], axis=dim)
    return block


def central(field, dimension):
    widths = [(0, 0)] * field.ndim
    widths[dimension] = (1, 1)
    padded = jnp.pad(field, widths)
    length = field.shape[dimension]
    return 0.5 * (
        lax.slice_in_dim(padded, 2, length + 2, axis=dimension)
        - lax.slice_in_dim(padded, 0, length, axis=dimension)
    )


def phase_term(obj_real, obj_imag, grad_x, grad_y, grad_z, qrow):
    term_x = obj_real * grad_x[:, :, 1] - obj_imag * grad_x[:, :, 0]
    term_y = obj_real * grad_y[:, :, 1] - obj_imag * grad_y[:, :, 0]
    term_z = obj_real * grad_z[:, :, 1] - obj_imag * grad_z[:, :, 0]
    return qrow[0] * term_x + qrow[1] * term_y + qrow[2] * term_z


def post_kernel(
    scalars, code_ref, rows_ref, kernels_ref, obj_ref, out_ref, grid_ref, halo, gathered, phase_buf,
    halo_send, halo_recv, send_sem, recv_sem, slab_count,
):
    refl_count = gathered.shape[0]
    planes, rows, width = grid_ref.shape[0], grid_ref.shape[2], grid_ref.shape[3]
    kernel_count = kernels_ref.shape[0]
    blocks = planes * rows
    chosen = (
        code_ref[...] == lax.broadcasted_iota(jnp.int32, (kernel_count * blocks, code_ref.shape[1]), 0)
    ).astype(jnp.bfloat16)
    summed = jnp.dot(chosen, rows_ref[...], preferred_element_type=jnp.float32)
    for c in range(2):
        total = None
        for k in range(kernel_count):
            part = summed[k * blocks : (k + 1) * blocks, c * width : (c + 1) * width]
            weights = kernels_ref[k]
            for _ in range(3):
                piece = part.astype(jnp.bfloat16)
                term = jnp.dot(piece, weights, preferred_element_type=jnp.float32)
                total = term if total is None else total + term
                part = part - piece.astype(jnp.float32)
        for p in range(planes):
            grid_ref[p, c] = total[p * rows : (p + 1) * rows]
    me = lax.axis_index("slab")
    refl = lax.axis_index("refl")
    up = lax.rem(me + 1, slab_count)
    down = lax.rem(me + slab_count - 1, slab_count)
    barrier = pltpu.get_barrier_semaphore()
    pl.semaphore_signal(barrier, 1, device_id=(refl, up), device_id_type=MESH)
    pl.semaphore_signal(barrier, 1, device_id=(refl, down), device_id_type=MESH)
    for step in range(1, refl_count):
        peer = lax.rem(refl + step, refl_count)
        pl.semaphore_signal(barrier, 1, device_id=(peer, me), device_id_type=MESH)
    pl.semaphore_wait(barrier, refl_count + 1)
    low_copy = pltpu.make_async_remote_copy(
        src_ref=grid_ref.at[planes - 1], dst_ref=halo.at[0], send_sem=halo_send.at[0],
        recv_sem=halo_recv.at[0], device_id=(refl, up), device_id_type=MESH,
    )
    high_copy = pltpu.make_async_remote_copy(
        src_ref=grid_ref.at[0], dst_ref=halo.at[1], send_sem=halo_send.at[1],
        recv_sem=halo_recv.at[1], device_id=(refl, down), device_id_type=MESH,
    )
    low_copy.start()
    high_copy.start()
    row_of = lax.broadcasted_iota(jnp.int32, (rows, width), 0)
    lane_of = lax.broadcasted_iota(jnp.int32, (rows, width), 1)

    def along_y(field):
        after = jnp.where(row_of == rows - 1, 0.0, pltpu.roll(field, rows - 1, 0))
        before = jnp.where(row_of == 0, 0.0, pltpu.roll(field, 1, 0))
        return 0.5 * (after - before)

    def along_w(field):
        after = jnp.where(lane_of == width - 1, 0.0, pltpu.roll(field, width - 1, 1))
        before = jnp.where(lane_of == 0, 0.0, pltpu.roll(field, 1, 1))
        return 0.5 * (after - before)

    mate = refl + 1 - 2 * lax.rem(refl, 2)
    q0, q1, q2 = scalars[refl, 0], scalars[refl, 1], scalars[refl, 2]
    d0 = q0 - scalars[mate, 0]
    d1 = q1 - scalars[mate, 1]
    d2 = q2 - scalars[mate, 2]
    partial = []
    for p in range(planes):
        obj_re, obj_im = obj_ref[p, 0], obj_ref[p, 1]
        term_y = obj_re * along_y(grid_ref[p, 1]) - obj_im * along_y(grid_ref[p, 0])
        term_z = obj_re * along_w(grid_ref[p, 1]) - obj_im * along_w(grid_ref[p, 0])
        partial.append((term_y, term_z))
    low_copy.wait_send()
    high_copy.wait_send()
    low_copy.wait_recv()
    high_copy.wait_recv()
    has_low = me > 0
    has_high = me < slab_count - 1
    for p in range(planes):
        obj_re, obj_im = obj_ref[p, 0], obj_ref[p, 1]
        grad = []
        for c in range(2):
            ahead = grid_ref[p + 1, c] if p + 1 < planes else jnp.where(has_high, halo[1, c], 0.0)
            behind = grid_ref[p - 1, c] if p > 0 else jnp.where(has_low, halo[0, c], 0.0)
            grad.append(0.5 * (ahead - behind))
        term_x = obj_re * grad[1] - obj_im * grad[0]
        term_y, term_z = partial[p]
        phase_buf[p] = q0 * term_x + q1 * term_y + q2 * term_z
    copies = []
    for step in range(1, refl_count):
        peer = lax.rem(refl + step, refl_count)
        copy = pltpu.make_async_remote_copy(
            src_ref=phase_buf, dst_ref=gathered.at[refl], send_sem=send_sem.at[step],
            recv_sem=recv_sem.at[step], device_id=(peer, me), device_id_type=MESH,
        )
        copy.start()
        copies.append(copy)
    gathered[refl] = phase_buf[...]
    for copy in copies:
        copy.wait_send()
    for step in range(1, refl_count):
        source = lax.rem(refl + refl_count - step, refl_count)
        pltpu.make_async_remote_copy(
            src_ref=phase_buf, dst_ref=gathered.at[source], send_sem=send_sem.at[step],
            recv_sem=recv_sem.at[step], device_id=(source, me), device_id_type=MESH,
        ).wait_recv()
    def weight(r):
        return scalars[r, 0] * d0 + scalars[r, 1] * d1 + scalars[r, 2] * d2

    shift = weight(0) * gathered[0]
    for r in range(1, refl_count):
        shift = shift + weight(r) * gathered[r]
    for p in range(planes):
        obj_re, obj_im = obj_ref[p, 0], obj_ref[p, 1]
        out_ref[p, 0] = obj_re - 0.5 * (grid_ref[p, 0] - obj_im * shift[p])
        out_ref[p, 1] = obj_im - 0.5 * (grid_ref[p, 1] + obj_re * shift[p])


def post_step(scalars, code_row, rows, kernels, obj, slab_count, refl_count):
    planes, _, rows_per, width = obj.shape
    return pl.pallas_call(
        functools.partial(post_kernel, slab_count=slab_count),
        out_shape=jax.ShapeDtypeStruct(obj.shape, jnp.float32),
        in_specs=[pl.BlockSpec(memory_space=pltpu.SMEM)]
        + [pl.BlockSpec(memory_space=pltpu.VMEM)] * 4,
        out_specs=pl.BlockSpec(memory_space=pltpu.VMEM),
        scratch_shapes=[
            pltpu.VMEM(obj.shape, jnp.float32),
            pltpu.VMEM((2, 2, rows_per, width), jnp.float32),
            pltpu.VMEM((refl_count, planes, rows_per, width), jnp.float32),
            pltpu.VMEM((planes, rows_per, width), jnp.float32),
            pltpu.SemaphoreType.DMA((2,)),
            pltpu.SemaphoreType.DMA((2,)),
            pltpu.SemaphoreType.DMA((refl_count,)),
            pltpu.SemaphoreType.DMA((refl_count,)),
        ],
        compiler_params=pltpu.CompilerParams(collective_id=0, has_side_effects=True),
    )(scalars, code_row, rows, kernels, obj)


def exchange_kernel(
    slot_ref, values_ref, ids_ref, data_out, code_out, data_buf, code_in, data_send, data_recv, code_send,
    code_recv,
):
    count, capacity = data_out.shape[0], data_out.shape[1]
    group = 8 if count >= 16 else count // 2
    groups = count // group
    rows = group * capacity
    me = lax.axis_index("slab")
    refl = lax.axis_index("refl")
    barrier = pltpu.get_barrier_semaphore()

    def greet(step, carry):
        peer = lax.rem(me + step, count)
        pl.semaphore_signal(barrier, 1, device_id=(refl, peer), device_id_type=MESH)
        return carry

    lax.fori_loop(1, count, greet, 0)

    def pack(g):
        target = lax.broadcasted_iota(jnp.int32, (rows, slot_ref.shape[1]), 0) + g * rows
        chosen = (slot_ref[...] == target).astype(jnp.bfloat16)
        sent = jnp.dot(chosen, values_ref[...], preferred_element_type=jnp.float32)
        data_buf[pl.ds(g * group, group)] = sent.astype(jnp.bfloat16).reshape(
            group, capacity, sent.shape[1]
        )
        codes = lax.dot_general(
            ids_ref[...], chosen, (((1,), (1,)), ((), ())), preferred_element_type=jnp.float32
        )
        codes = (codes[0:1] * 8.0 + codes[1:2]).astype(jnp.int32)
        for part in range(group):
            window = (part * capacity) // 128
            code_in[g * group + part] = codes[:, window * 128 : (window + 1) * 128]

    def outgoing(d):
        data = pltpu.make_async_remote_copy(
            src_ref=data_buf.at[d], dst_ref=data_out.at[me], send_sem=data_send.at[d],
            recv_sem=data_recv.at[me], device_id=(refl, d), device_id_type=MESH,
        )
        code = pltpu.make_async_remote_copy(
            src_ref=code_in.at[d], dst_ref=code_out.at[me], send_sem=code_send.at[d],
            recv_sem=code_recv.at[me], device_id=(refl, d), device_id_type=MESH,
        )
        return data, code

    def incoming(s):
        data = pltpu.make_async_remote_copy(
            src_ref=data_buf.at[s], dst_ref=data_out.at[s], send_sem=data_send.at[s],
            recv_sem=data_recv.at[s], device_id=(refl, s), device_id_type=MESH,
        )
        code = pltpu.make_async_remote_copy(
            src_ref=code_in.at[s], dst_ref=code_out.at[s], send_sem=code_send.at[s],
            recv_sem=code_recv.at[s], device_id=(refl, s), device_id_type=MESH,
        )
        return data, code

    def send(g):
        for part in range(group):
            d = g * group + part

            @pl.when(d != me)
            def _():
                data, code = outgoing(d)
                code.start()
                data.start()

    home = me // group
    middle = groups // 2

    def order(j):
        return lax.rem(home + middle + (1 - 2 * lax.rem(j, 2)) * ((j + 1) // 2) + groups, groups)

    first = order(0)
    pack(first)
    pl.semaphore_wait(barrier, count - 1)
    send(first)

    def later(j, carry):
        g = order(j)
        pack(g)
        send(g)
        return carry

    lax.fori_loop(1, groups, later, 0)
    data_out[me] = data_buf[me]
    local = pltpu.make_async_copy(code_in.at[me], code_out.at[me], code_send.at[me])
    local.start()

    def finish(step, carry):
        data, code = outgoing(lax.rem(me + step, count))
        data.wait_send()
        code.wait_send()
        data, code = incoming(lax.rem(me + count - step, count))
        data.wait_recv()
        code.wait_recv()
        return carry

    lax.fori_loop(1, count, finish, 0)
    local.wait()


def exchange_slab(flat_slot, values, ids, count, capacity):
    data_shape = (count, capacity, values.shape[1])
    code_shape = (count, 1, 128)
    return pl.pallas_call(
        exchange_kernel,
        out_shape=(
            jax.ShapeDtypeStruct(data_shape, jnp.bfloat16),
            jax.ShapeDtypeStruct(code_shape, jnp.int32),
        ),
        in_specs=[pl.BlockSpec(memory_space=pltpu.VMEM)] * 3,
        out_specs=(pl.BlockSpec(memory_space=pltpu.VMEM), pl.BlockSpec(memory_space=pl.ANY)),
        scratch_shapes=[
            pltpu.VMEM(data_shape, jnp.bfloat16),
            pltpu.VMEM(code_shape, jnp.int32),
            pltpu.SemaphoreType.DMA((count,)),
            pltpu.SemaphoreType.DMA((count,)),
            pltpu.SemaphoreType.DMA((count,)),
            pltpu.SemaphoreType.DMA((count,)),
        ],
        compiler_params=pltpu.CompilerParams(collective_id=1, has_side_effects=True),
    )(flat_slot, values, ids)


def per_device(detector, owners, block_ids, kernel_ids, kernels, bragg_vectors, object_field):
    slab_count = lax.axis_size("slab")
    plane_count = object_field.shape[1]
    row_count = object_field.shape[2]
    block_count = plane_count * row_count
    kernel_count = kernels.shape[0]
    tile_count = detector.shape[1]
    tile_width = detector.shape[3]
    row_width = 2 * tile_width
    capacity = 2 * tile_count // slab_count
    values = detector[0].reshape(tile_count, row_width)
    owner = owners[0, :, 0]
    order = lax.broadcasted_iota(jnp.int32, (tile_count, tile_count), 1) < lax.broadcasted_iota(
        jnp.int32, (tile_count, tile_count), 0
    )
    same = (owner[:, None] == owner[None, :]) & order
    slots = jnp.sum(same.astype(jnp.int32), axis=1)
    flat_slot = owner * capacity + slots
    ids = jnp.concatenate(
        [block_ids, kernel_ids, jnp.zeros((6, tile_count), jnp.int32)], axis=0
    ).astype(jnp.bfloat16)
    got, got_code = exchange_slab(flat_slot[None, :], values, ids, slab_count, capacity)
    row_total = slab_count * capacity
    rows = got.reshape(row_total, row_width)
    offset = lax.rem(lax.axis_index("slab"), 4) * capacity
    got_codes = lax.dynamic_slice_in_dim(got_code[:, 0, :], offset, capacity, axis=1).reshape(row_total)
    code_row = (lax.rem(got_codes, kernel_count) * block_count + got_codes // kernel_count)[None, :]
    refl_count = bragg_vectors.shape[0]
    obj = object_field[0].transpose(0, 2, 1, 3)
    updated = post_step(bragg_vectors, code_row, rows, kernels, obj, slab_count, refl_count)
    return updated.transpose(0, 2, 1, 3)[None]


def solution(mesh):
    in_specs = (
        P("refl", "slab", None, None),
        P("refl", "slab", None),
        P("refl", "slab"),
        P("refl", "slab"),
        P(),
        P(),
        P("refl", "slab", None, None, None),
    )
    out_specs = P("refl", "slab", None, None, None)
    return jax.shard_map(
        per_device, mesh=mesh, in_specs=in_specs, out_specs=out_specs, check_vma=False
    )
```

```python
import functools

import jax
import jax.numpy as jnp
from jax import lax
from jax.experimental import pallas as pl
from jax.experimental.pallas import tpu as pltpu
from jax.sharding import PartitionSpec as P

MESH = pl.DeviceIdType.MESH


def extended(block, sides, width):
    for axis, dim in sides:
        count = lax.axis_size(axis)
        forward = [(i, i + 1) for i in range(count - 1)]
        backward = [(target, source) for source, target in forward]
        low = lax.ppermute(
            lax.slice_in_dim(block, block.shape[dim] - width, None, axis=dim), axis, forward
        )
        high = lax.ppermute(lax.slice_in_dim(block, 0, width, axis=dim), axis, backward)
        block = jnp.concatenate([low, block, high], axis=dim)
    return block


def central(field, dimension):
    widths = [(0, 0)] * field.ndim
    widths[dimension] = (1, 1)
    padded = jnp.pad(field, widths)
    length = field.shape[dimension]
    return 0.5 * (
        lax.slice_in_dim(padded, 2, length + 2, axis=dimension)
        - lax.slice_in_dim(padded, 0, length, axis=dimension)
    )


def phase_term(obj_real, obj_imag, grad_x, grad_y, grad_z, qrow):
    term_x = obj_real * grad_x[:, :, 1] - obj_imag * grad_x[:, :, 0]
    term_y = obj_real * grad_y[:, :, 1] - obj_imag * grad_y[:, :, 0]
    term_z = obj_real * grad_z[:, :, 1] - obj_imag * grad_z[:, :, 0]
    return qrow[0] * term_x + qrow[1] * term_y + qrow[2] * term_z


def post_kernel(
    scalars, code_ref, rows_ref, kernels_ref, obj_ref, out_ref, grid_ref, halo, gathered, phase_buf,
    halo_send, halo_recv, send_sem, recv_sem, slab_count,
):
    refl_count = gathered.shape[0]
    planes, rows, width = grid_ref.shape[0], grid_ref.shape[2], grid_ref.shape[3]
    kernel_count = kernels_ref.shape[0]
    blocks = planes * rows
    chosen = (
        code_ref[...] == lax.broadcasted_iota(jnp.int32, (kernel_count * blocks, code_ref.shape[1]), 0)
    ).astype(jnp.bfloat16)
    summed = jnp.dot(chosen, rows_ref[...], preferred_element_type=jnp.float32)
    for c in range(2):
        total = None
        for k in range(kernel_count):
            part = summed[k * blocks : (k + 1) * blocks, c * width : (c + 1) * width]
            weights = kernels_ref[k]
            for _ in range(3):
                piece = part.astype(jnp.bfloat16)
                term = jnp.dot(piece, weights, preferred_element_type=jnp.float32)
                total = term if total is None else total + term
                part = part - piece.astype(jnp.float32)
        for p in range(planes):
            grid_ref[p, c] = total[p * rows : (p + 1) * rows]
    me = lax.axis_index("slab")
    refl = lax.axis_index("refl")
    up = lax.rem(me + 1, slab_count)
    down = lax.rem(me + slab_count - 1, slab_count)
    barrier = pltpu.get_barrier_semaphore()
    pl.semaphore_signal(barrier, 1, device_id=(refl, up), device_id_type=MESH)
    pl.semaphore_signal(barrier, 1, device_id=(refl, down), device_id_type=MESH)
    for step in range(1, refl_count):
        peer = lax.rem(refl + step, refl_count)
        pl.semaphore_signal(barrier, 1, device_id=(peer, me), device_id_type=MESH)
    pl.semaphore_wait(barrier, refl_count + 1)
    low_copy = pltpu.make_async_remote_copy(
        src_ref=grid_ref.at[planes - 1], dst_ref=halo.at[0], send_sem=halo_send.at[0],
        recv_sem=halo_recv.at[0], device_id=(refl, up), device_id_type=MESH,
    )
    high_copy = pltpu.make_async_remote_copy(
        src_ref=grid_ref.at[0], dst_ref=halo.at[1], send_sem=halo_send.at[1],
        recv_sem=halo_recv.at[1], device_id=(refl, down), device_id_type=MESH,
    )
    low_copy.start()
    high_copy.start()
    row_of = lax.broadcasted_iota(jnp.int32, (rows, width), 0)
    lane_of = lax.broadcasted_iota(jnp.int32, (rows, width), 1)

    def along_y(field):
        after = jnp.where(row_of == rows - 1, 0.0, pltpu.roll(field, rows - 1, 0))
        before = jnp.where(row_of == 0, 0.0, pltpu.roll(field, 1, 0))
        return 0.5 * (after - before)

    def along_w(field):
        after = jnp.where(lane_of == width - 1, 0.0, pltpu.roll(field, width - 1, 1))
        before = jnp.where(lane_of == 0, 0.0, pltpu.roll(field, 1, 1))
        return 0.5 * (after - before)

    mate = refl + 1 - 2 * lax.rem(refl, 2)
    q0, q1, q2 = scalars[refl, 0], scalars[refl, 1], scalars[refl, 2]
    d0 = q0 - scalars[mate, 0]
    d1 = q1 - scalars[mate, 1]
    d2 = q2 - scalars[mate, 2]
    partial = []
    for p in range(planes):
        obj_re, obj_im = obj_ref[p, :, 0, :], obj_ref[p, :, 1, :]
        term_y = obj_re * along_y(grid_ref[p, 1]) - obj_im * along_y(grid_ref[p, 0])
        term_z = obj_re * along_w(grid_ref[p, 1]) - obj_im * along_w(grid_ref[p, 0])
        partial.append((term_y, term_z))
    low_copy.wait_send()
    high_copy.wait_send()
    low_copy.wait_recv()
    high_copy.wait_recv()
    has_low = me > 0
    has_high = me < slab_count - 1
    for p in range(planes):
        obj_re, obj_im = obj_ref[p, :, 0, :], obj_ref[p, :, 1, :]
        grad = []
        for c in range(2):
            ahead = grid_ref[p + 1, c] if p + 1 < planes else jnp.where(has_high, halo[1, c], 0.0)
            behind = grid_ref[p - 1, c] if p > 0 else jnp.where(has_low, halo[0, c], 0.0)
            grad.append(0.5 * (ahead - behind))
        term_x = obj_re * grad[1] - obj_im * grad[0]
        term_y, term_z = partial[p]
        phase_buf[p] = q0 * term_x + q1 * term_y + q2 * term_z
    copies = []
    for step in range(1, refl_count):
        peer = lax.rem(refl + step, refl_count)
        copy = pltpu.make_async_remote_copy(
            src_ref=phase_buf, dst_ref=gathered.at[refl], send_sem=send_sem.at[step],
            recv_sem=recv_sem.at[step], device_id=(peer, me), device_id_type=MESH,
        )
        copy.start()
        copies.append(copy)
    gathered[refl] = phase_buf[...]
    for copy in copies:
        copy.wait_send()
    for step in range(1, refl_count):
        source = lax.rem(refl + refl_count - step, refl_count)
        pltpu.make_async_remote_copy(
            src_ref=phase_buf, dst_ref=gathered.at[source], send_sem=send_sem.at[step],
            recv_sem=recv_sem.at[step], device_id=(source, me), device_id_type=MESH,
        ).wait_recv()
    def weight(r):
        return scalars[r, 0] * d0 + scalars[r, 1] * d1 + scalars[r, 2] * d2

    shift = weight(0) * gathered[0]
    for r in range(1, refl_count):
        shift = shift + weight(r) * gathered[r]
    for p in range(planes):
        obj_re, obj_im = obj_ref[p, :, 0, :], obj_ref[p, :, 1, :]
        new_re = obj_re - 0.5 * (grid_ref[p, 0] - obj_im * shift[p])
        new_im = obj_im - 0.5 * (grid_ref[p, 1] + obj_re * shift[p])
        out_ref[p] = jnp.stack([new_re, new_im], axis=1)


def post_step(scalars, code_row, rows, kernels, obj, slab_count, refl_count):
    planes, rows_per, _, width = obj.shape
    return pl.pallas_call(
        functools.partial(post_kernel, slab_count=slab_count),
        out_shape=jax.ShapeDtypeStruct(obj.shape, jnp.float32),
        in_specs=[pl.BlockSpec(memory_space=pltpu.SMEM)]
        + [pl.BlockSpec(memory_space=pltpu.VMEM)] * 4,
        out_specs=pl.BlockSpec(memory_space=pltpu.VMEM),
        scratch_shapes=[
            pltpu.VMEM((planes, 2, rows_per, width), jnp.float32),
            pltpu.VMEM((2, 2, rows_per, width), jnp.float32),
            pltpu.VMEM((refl_count, planes, rows_per, width), jnp.float32),
            pltpu.VMEM((planes, rows_per, width), jnp.float32),
            pltpu.SemaphoreType.DMA((2,)),
            pltpu.SemaphoreType.DMA((2,)),
            pltpu.SemaphoreType.DMA((refl_count,)),
            pltpu.SemaphoreType.DMA((refl_count,)),
        ],
        compiler_params=pltpu.CompilerParams(collective_id=0, has_side_effects=True),
    )(scalars, code_row, rows, kernels, obj)


def exchange_kernel(
    slot_ref, values_ref, ids_ref, data_out, code_out, data_buf, code_in, data_send, data_recv, code_send,
    code_recv,
):
    count, capacity = data_out.shape[0], data_out.shape[1]
    group = 8 if count >= 16 else count // 2
    groups = count // group
    rows = group * capacity
    me = lax.axis_index("slab")
    refl = lax.axis_index("refl")
    barrier = pltpu.get_barrier_semaphore()

    def greet(step, carry):
        peer = lax.rem(me + step, count)
        pl.semaphore_signal(barrier, 1, device_id=(refl, peer), device_id_type=MESH)
        return carry

    lax.fori_loop(1, count, greet, 0)

    def pack(g):
        target = lax.broadcasted_iota(jnp.int32, (rows, slot_ref.shape[1]), 0) + g * rows
        chosen = (slot_ref[...] == target).astype(jnp.bfloat16)
        sent = jnp.dot(chosen, values_ref[...], preferred_element_type=jnp.float32)
        data_buf[pl.ds(g * group, group)] = sent.astype(jnp.bfloat16).reshape(
            group, capacity, sent.shape[1]
        )
        codes = lax.dot_general(
            ids_ref[...], chosen, (((1,), (1,)), ((), ())), preferred_element_type=jnp.float32
        )
        codes = (codes[0:1] * 8.0 + codes[1:2]).astype(jnp.int32)
        for part in range(group):
            window = (part * capacity) // 128
            code_in[g * group + part] = codes[:, window * 128 : (window + 1) * 128]

    def outgoing(d):
        data = pltpu.make_async_remote_copy(
            src_ref=data_buf.at[d], dst_ref=data_out.at[me], send_sem=data_send.at[d],
            recv_sem=data_recv.at[me], device_id=(refl, d), device_id_type=MESH,
        )
        code = pltpu.make_async_remote_copy(
            src_ref=code_in.at[d], dst_ref=code_out.at[me], send_sem=code_send.at[d],
            recv_sem=code_recv.at[me], device_id=(refl, d), device_id_type=MESH,
        )
        return data, code

    def incoming(s):
        data = pltpu.make_async_remote_copy(
            src_ref=data_buf.at[s], dst_ref=data_out.at[s], send_sem=data_send.at[s],
            recv_sem=data_recv.at[s], device_id=(refl, s), device_id_type=MESH,
        )
        code = pltpu.make_async_remote_copy(
            src_ref=code_in.at[s], dst_ref=code_out.at[s], send_sem=code_send.at[s],
            recv_sem=code_recv.at[s], device_id=(refl, s), device_id_type=MESH,
        )
        return data, code

    def send(g):
        for part in range(group):
            d = g * group + part

            @pl.when(d != me)
            def _():
                data, code = outgoing(d)
                code.start()
                data.start()

    home = me // group
    middle = groups // 2

    def order(j):
        return lax.rem(home + middle + (1 - 2 * lax.rem(j, 2)) * ((j + 1) // 2) + groups, groups)

    first = order(0)
    pack(first)
    pl.semaphore_wait(barrier, count - 1)
    send(first)

    def later(j, carry):
        g = order(j)
        pack(g)
        send(g)
        return carry

    lax.fori_loop(1, groups, later, 0)
    data_out[me] = data_buf[me]
    local = pltpu.make_async_copy(code_in.at[me], code_out.at[me], code_send.at[me])
    local.start()

    def finish(step, carry):
        data, code = outgoing(lax.rem(me + step, count))
        data.wait_send()
        code.wait_send()
        data, code = incoming(lax.rem(me + count - step, count))
        data.wait_recv()
        code.wait_recv()
        return carry

    lax.fori_loop(1, count, finish, 0)
    local.wait()


def exchange_slab(flat_slot, values, ids, count, capacity):
    data_shape = (count, capacity, values.shape[1])
    code_shape = (count, 1, 128)
    return pl.pallas_call(
        exchange_kernel,
        out_shape=(
            jax.ShapeDtypeStruct(data_shape, jnp.bfloat16),
            jax.ShapeDtypeStruct(code_shape, jnp.int32),
        ),
        in_specs=[pl.BlockSpec(memory_space=pltpu.VMEM)] * 3,
        out_specs=(pl.BlockSpec(memory_space=pltpu.VMEM), pl.BlockSpec(memory_space=pl.ANY)),
        scratch_shapes=[
            pltpu.VMEM(data_shape, jnp.bfloat16),
            pltpu.VMEM(code_shape, jnp.int32),
            pltpu.SemaphoreType.DMA((count,)),
            pltpu.SemaphoreType.DMA((count,)),
            pltpu.SemaphoreType.DMA((count,)),
            pltpu.SemaphoreType.DMA((count,)),
        ],
        compiler_params=pltpu.CompilerParams(collective_id=1, has_side_effects=True),
    )(flat_slot, values, ids)


def per_device(detector, owners, block_ids, kernel_ids, kernels, bragg_vectors, object_field):
    slab_count = lax.axis_size("slab")
    plane_count = object_field.shape[1]
    row_count = object_field.shape[2]
    block_count = plane_count * row_count
    kernel_count = kernels.shape[0]
    tile_count = detector.shape[1]
    tile_width = detector.shape[3]
    row_width = 2 * tile_width
    capacity = 2 * tile_count // slab_count
    values = detector[0].reshape(tile_count, row_width)
    owner = owners[0, :, 0]
    order = lax.broadcasted_iota(jnp.int32, (tile_count, tile_count), 1) < lax.broadcasted_iota(
        jnp.int32, (tile_count, tile_count), 0
    )
    same = (owner[:, None] == owner[None, :]) & order
    slots = jnp.sum(same.astype(jnp.int32), axis=1)
    flat_slot = owner * capacity + slots
    ids = jnp.concatenate(
        [block_ids, kernel_ids, jnp.zeros((6, tile_count), jnp.int32)], axis=0
    ).astype(jnp.bfloat16)
    got, got_code = exchange_slab(flat_slot[None, :], values, ids, slab_count, capacity)
    row_total = slab_count * capacity
    rows = got.reshape(row_total, row_width)
    offset = lax.rem(lax.axis_index("slab"), 4) * capacity
    got_codes = lax.dynamic_slice_in_dim(got_code[:, 0, :], offset, capacity, axis=1).reshape(row_total)
    code_row = (lax.rem(got_codes, kernel_count) * block_count + got_codes // kernel_count)[None, :]
    refl_count = bragg_vectors.shape[0]
    obj = object_field[0]
    updated = post_step(bragg_vectors, code_row, rows, kernels, obj, slab_count, refl_count)
    return updated[None]


def solution(mesh):
    in_specs = (
        P("refl", "slab", None, None),
        P("refl", "slab", None),
        P("refl", "slab"),
        P("refl", "slab"),
        P(),
        P(),
        P("refl", "slab", None, None, None),
    )
    out_specs = P("refl", "slab", None, None, None)
    return jax.shard_map(
        per_device, mesh=mesh, in_specs=in_specs, out_specs=out_specs, check_vma=False
    )
```

```python
import functools

import jax
import jax.numpy as jnp
from jax import lax
from jax.experimental import pallas as pl
from jax.experimental.pallas import tpu as pltpu
from jax.sharding import PartitionSpec as P

MESH = pl.DeviceIdType.MESH


def extended(block, sides, width):
    for axis, dim in sides:
        count = lax.axis_size(axis)
        forward = [(i, i + 1) for i in range(count - 1)]
        backward = [(target, source) for source, target in forward]
        low = lax.ppermute(
            lax.slice_in_dim(block, block.shape[dim] - width, None, axis=dim), axis, forward
        )
        high = lax.ppermute(lax.slice_in_dim(block, 0, width, axis=dim), axis, backward)
        block = jnp.concatenate([low, block, high], axis=dim)
    return block


def central(field, dimension):
    widths = [(0, 0)] * field.ndim
    widths[dimension] = (1, 1)
    padded = jnp.pad(field, widths)
    length = field.shape[dimension]
    return 0.5 * (
        lax.slice_in_dim(padded, 2, length + 2, axis=dimension)
        - lax.slice_in_dim(padded, 0, length, axis=dimension)
    )


def phase_term(obj_real, obj_imag, grad_x, grad_y, grad_z, qrow):
    term_x = obj_real * grad_x[:, :, 1] - obj_imag * grad_x[:, :, 0]
    term_y = obj_real * grad_y[:, :, 1] - obj_imag * grad_y[:, :, 0]
    term_z = obj_real * grad_z[:, :, 1] - obj_imag * grad_z[:, :, 0]
    return qrow[0] * term_x + qrow[1] * term_y + qrow[2] * term_z


def post_kernel(
    scalars, code_ref, rows_ref, kernels_ref, obj_ref, out_ref, grid_ref, halo, gathered, phase_buf,
    halo_send, halo_recv, send_sem, recv_sem, slab_count,
):
    refl_count = gathered.shape[0]
    planes, rows, width = grid_ref.shape[0], grid_ref.shape[2], grid_ref.shape[3]
    kernel_count = kernels_ref.shape[0]
    blocks = planes * rows
    chosen = (
        code_ref[...] == lax.broadcasted_iota(jnp.int32, (kernel_count * blocks, code_ref.shape[1]), 0)
    ).astype(jnp.bfloat16)
    summed = jnp.dot(chosen, rows_ref[...], preferred_element_type=jnp.float32)
    for c in range(2):
        total = None
        for k in range(kernel_count):
            part = summed[k * blocks : (k + 1) * blocks, c * width : (c + 1) * width]
            weights = kernels_ref[k]
            for _ in range(3):
                piece = part.astype(jnp.bfloat16)
                term = jnp.dot(piece, weights, preferred_element_type=jnp.float32)
                total = term if total is None else total + term
                part = part - piece.astype(jnp.float32)
        for p in range(planes):
            grid_ref[p, c] = total[p * rows : (p + 1) * rows]
    me = lax.axis_index("slab")
    refl = lax.axis_index("refl")
    up = lax.rem(me + 1, slab_count)
    down = lax.rem(me + slab_count - 1, slab_count)
    barrier = pltpu.get_barrier_semaphore()
    pl.semaphore_signal(barrier, 1, device_id=(refl, up), device_id_type=MESH)
    pl.semaphore_signal(barrier, 1, device_id=(refl, down), device_id_type=MESH)
    for step in range(1, refl_count):
        peer = lax.rem(refl + step, refl_count)
        pl.semaphore_signal(barrier, 1, device_id=(peer, me), device_id_type=MESH)
    pl.semaphore_wait(barrier, refl_count + 1)
    low_copy = pltpu.make_async_remote_copy(
        src_ref=grid_ref.at[planes - 1], dst_ref=halo.at[0], send_sem=halo_send.at[0],
        recv_sem=halo_recv.at[0], device_id=(refl, up), device_id_type=MESH,
    )
    high_copy = pltpu.make_async_remote_copy(
        src_ref=grid_ref.at[0], dst_ref=halo.at[1], send_sem=halo_send.at[1],
        recv_sem=halo_recv.at[1], device_id=(refl, down), device_id_type=MESH,
    )
    low_copy.start()
    high_copy.start()
    row_of = lax.broadcasted_iota(jnp.int32, (rows, width), 0)
    lane_of = lax.broadcasted_iota(jnp.int32, (rows, width), 1)

    def along_y(field):
        after = jnp.where(row_of == rows - 1, 0.0, pltpu.roll(field, rows - 1, 0))
        before = jnp.where(row_of == 0, 0.0, pltpu.roll(field, 1, 0))
        return 0.5 * (after - before)

    def along_w(field):
        after = jnp.where(lane_of == width - 1, 0.0, pltpu.roll(field, width - 1, 1))
        before = jnp.where(lane_of == 0, 0.0, pltpu.roll(field, 1, 1))
        return 0.5 * (after - before)

    mate = refl + 1 - 2 * lax.rem(refl, 2)
    q0, q1, q2 = scalars[0, refl], scalars[1, refl], scalars[2, refl]
    d0 = q0 - scalars[0, mate]
    d1 = q1 - scalars[1, mate]
    d2 = q2 - scalars[2, mate]
    partial = []
    for p in range(planes):
        obj_re, obj_im = obj_ref[p, :, 0, :], obj_ref[p, :, 1, :]
        term_y = obj_re * along_y(grid_ref[p, 1]) - obj_im * along_y(grid_ref[p, 0])
        term_z = obj_re * along_w(grid_ref[p, 1]) - obj_im * along_w(grid_ref[p, 0])
        partial.append((term_y, term_z))
    low_copy.wait_send()
    high_copy.wait_send()
    low_copy.wait_recv()
    high_copy.wait_recv()
    has_low = me > 0
    has_high = me < slab_count - 1
    for p in range(planes):
        obj_re, obj_im = obj_ref[p, :, 0, :], obj_ref[p, :, 1, :]
        grad = []
        for c in range(2):
            ahead = grid_ref[p + 1, c] if p + 1 < planes else jnp.where(has_high, halo[1, c], 0.0)
            behind = grid_ref[p - 1, c] if p > 0 else jnp.where(has_low, halo[0, c], 0.0)
            grad.append(0.5 * (ahead - behind))
        term_x = obj_re * grad[1] - obj_im * grad[0]
        term_y, term_z = partial[p]
        phase_buf[p] = q0 * term_x + q1 * term_y + q2 * term_z
    copies = []
    for step in range(1, refl_count):
        peer = lax.rem(refl + step, refl_count)
        copy = pltpu.make_async_remote_copy(
            src_ref=phase_buf, dst_ref=gathered.at[refl], send_sem=send_sem.at[step],
            recv_sem=recv_sem.at[step], device_id=(peer, me), device_id_type=MESH,
        )
        copy.start()
        copies.append(copy)
    gathered[refl] = phase_buf[...]
    for copy in copies:
        copy.wait_send()
    for step in range(1, refl_count):
        source = lax.rem(refl + refl_count - step, refl_count)
        pltpu.make_async_remote_copy(
            src_ref=phase_buf, dst_ref=gathered.at[source], send_sem=send_sem.at[step],
            recv_sem=recv_sem.at[step], device_id=(source, me), device_id_type=MESH,
        ).wait_recv()
    def weight(r):
        return scalars[0, r] * d0 + scalars[1, r] * d1 + scalars[2, r] * d2

    shift = weight(0) * gathered[0]
    for r in range(1, refl_count):
        shift = shift + weight(r) * gathered[r]
    for p in range(planes):
        obj_re, obj_im = obj_ref[p, :, 0, :], obj_ref[p, :, 1, :]
        new_re = obj_re - 0.5 * (grid_ref[p, 0] - obj_im * shift[p])
        new_im = obj_im - 0.5 * (grid_ref[p, 1] + obj_re * shift[p])
        out_ref[p] = jnp.stack([new_re, new_im], axis=1)


def post_step(scalars, code_row, rows, kernels, obj, slab_count, refl_count):
    planes, rows_per, _, width = obj.shape
    return pl.pallas_call(
        functools.partial(post_kernel, slab_count=slab_count),
        out_shape=jax.ShapeDtypeStruct(obj.shape, jnp.float32),
        in_specs=[pl.BlockSpec(memory_space=pltpu.SMEM)]
        + [pl.BlockSpec(memory_space=pltpu.VMEM)] * 4,
        out_specs=pl.BlockSpec(memory_space=pltpu.VMEM),
        scratch_shapes=[
            pltpu.VMEM((planes, 2, rows_per, width), jnp.float32),
            pltpu.VMEM((2, 2, rows_per, width), jnp.float32),
            pltpu.VMEM((refl_count, planes, rows_per, width), jnp.float32),
            pltpu.VMEM((planes, rows_per, width), jnp.float32),
            pltpu.SemaphoreType.DMA((2,)),
            pltpu.SemaphoreType.DMA((2,)),
            pltpu.SemaphoreType.DMA((refl_count,)),
            pltpu.SemaphoreType.DMA((refl_count,)),
        ],
        compiler_params=pltpu.CompilerParams(collective_id=0, has_side_effects=True),
    )(scalars, code_row, rows, kernels, obj)


def exchange_kernel(
    slot_ref, values_ref, ids_ref, data_out, code_out, data_buf, code_in, data_send, data_recv, code_send,
    code_recv,
):
    count, capacity = data_out.shape[0], data_out.shape[1]
    group = 8 if count >= 16 else count // 2
    groups = count // group
    rows = group * capacity
    me = lax.axis_index("slab")
    refl = lax.axis_index("refl")
    barrier = pltpu.get_barrier_semaphore()

    def greet(step, carry):
        peer = lax.rem(me + step, count)
        pl.semaphore_signal(barrier, 1, device_id=(refl, peer), device_id_type=MESH)
        return carry

    lax.fori_loop(1, count, greet, 0)

    def pack(g):
        target = lax.broadcasted_iota(jnp.int32, (rows, slot_ref.shape[1]), 0) + g * rows
        chosen = (slot_ref[...] == target).astype(jnp.bfloat16)
        sent = jnp.dot(chosen, values_ref[...], preferred_element_type=jnp.float32)
        data_buf[pl.ds(g * group, group)] = sent.astype(jnp.bfloat16).reshape(
            group, capacity, sent.shape[1]
        )
        codes = lax.dot_general(
            ids_ref[...], chosen, (((1,), (1,)), ((), ())), preferred_element_type=jnp.float32
        )
        codes = (codes[0:1] * 8.0 + codes[1:2]).astype(jnp.int32)
        for part in range(group):
            window = (part * capacity) // 128
            code_in[g * group + part] = codes[:, window * 128 : (window + 1) * 128]

    def outgoing(d):
        data = pltpu.make_async_remote_copy(
            src_ref=data_buf.at[d], dst_ref=data_out.at[me], send_sem=data_send.at[d],
            recv_sem=data_recv.at[me], device_id=(refl, d), device_id_type=MESH,
        )
        code = pltpu.make_async_remote_copy(
            src_ref=code_in.at[d], dst_ref=code_out.at[me], send_sem=code_send.at[d],
            recv_sem=code_recv.at[me], device_id=(refl, d), device_id_type=MESH,
        )
        return data, code

    def incoming(s):
        data = pltpu.make_async_remote_copy(
            src_ref=data_buf.at[s], dst_ref=data_out.at[s], send_sem=data_send.at[s],
            recv_sem=data_recv.at[s], device_id=(refl, s), device_id_type=MESH,
        )
        code = pltpu.make_async_remote_copy(
            src_ref=code_in.at[s], dst_ref=code_out.at[s], send_sem=code_send.at[s],
            recv_sem=code_recv.at[s], device_id=(refl, s), device_id_type=MESH,
        )
        return data, code

    def send(g):
        for part in range(group):
            d = g * group + part

            @pl.when(d != me)
            def _():
                data, code = outgoing(d)
                code.start()
                data.start()

    home = me // group
    middle = groups // 2

    def order(j):
        return lax.rem(home + middle + (1 - 2 * lax.rem(j, 2)) * ((j + 1) // 2) + groups, groups)

    first = order(0)
    pack(first)
    pl.semaphore_wait(barrier, count - 1)
    send(first)

    def later(j, carry):
        g = order(j)
        pack(g)
        send(g)
        return carry

    lax.fori_loop(1, groups, later, 0)
    data_out[me] = data_buf[me]
    local = pltpu.make_async_copy(code_in.at[me], code_out.at[me], code_send.at[me])
    local.start()

    def finish(step, carry):
        data, code = outgoing(lax.rem(me + step, count))
        data.wait_send()
        code.wait_send()
        data, code = incoming(lax.rem(me + count - step, count))
        data.wait_recv()
        code.wait_recv()
        return carry

    lax.fori_loop(1, count, finish, 0)
    local.wait()


def exchange_slab(flat_slot, values, ids, count, capacity):
    data_shape = (count, capacity, values.shape[1])
    code_shape = (count, 1, 128)
    return pl.pallas_call(
        exchange_kernel,
        out_shape=(
            jax.ShapeDtypeStruct(data_shape, jnp.bfloat16),
            jax.ShapeDtypeStruct(code_shape, jnp.int32),
        ),
        in_specs=[pl.BlockSpec(memory_space=pltpu.VMEM)] * 3,
        out_specs=(pl.BlockSpec(memory_space=pltpu.VMEM), pl.BlockSpec(memory_space=pl.ANY)),
        scratch_shapes=[
            pltpu.VMEM(data_shape, jnp.bfloat16),
            pltpu.VMEM(code_shape, jnp.int32),
            pltpu.SemaphoreType.DMA((count,)),
            pltpu.SemaphoreType.DMA((count,)),
            pltpu.SemaphoreType.DMA((count,)),
            pltpu.SemaphoreType.DMA((count,)),
        ],
        compiler_params=pltpu.CompilerParams(collective_id=1, has_side_effects=True),
    )(flat_slot, values, ids)


def per_device(detector, owners, block_ids, kernel_ids, kernels, bragg_vectors, object_field):
    slab_count = lax.axis_size("slab")
    plane_count = object_field.shape[1]
    row_count = object_field.shape[2]
    block_count = plane_count * row_count
    kernel_count = kernels.shape[0]
    tile_count = detector.shape[1]
    tile_width = detector.shape[3]
    row_width = 2 * tile_width
    capacity = 2 * tile_count // slab_count
    values = detector[0].reshape(tile_count, row_width)
    owner = owners[0, :, 0]
    order = lax.broadcasted_iota(jnp.int32, (tile_count, tile_count), 1) < lax.broadcasted_iota(
        jnp.int32, (tile_count, tile_count), 0
    )
    same = (owner[:, None] == owner[None, :]) & order
    slots = jnp.sum(same.astype(jnp.int32), axis=1)
    flat_slot = owner * capacity + slots
    ids = jnp.concatenate(
        [block_ids, kernel_ids, jnp.zeros((6, tile_count), jnp.int32)], axis=0
    ).astype(jnp.bfloat16)
    got, got_code = exchange_slab(flat_slot[None, :], values, ids, slab_count, capacity)
    row_total = slab_count * capacity
    rows = got.reshape(row_total, row_width)
    offset = lax.rem(lax.axis_index("slab"), 4) * capacity
    got_codes = lax.dynamic_slice_in_dim(got_code[:, 0, :], offset, capacity, axis=1).reshape(row_total)
    code_row = (lax.rem(got_codes, kernel_count) * block_count + got_codes // kernel_count)[None, :]
    refl_count = bragg_vectors.shape[0]
    obj = object_field[0]
    updated = post_step(bragg_vectors.T, code_row, rows, kernels, obj, slab_count, refl_count)
    return updated[None]


def solution(mesh):
    in_specs = (
        P("refl", "slab", None, None),
        P("refl", "slab", None),
        P("refl", "slab"),
        P("refl", "slab"),
        P(),
        P(),
        P("refl", "slab", None, None, None),
    )
    out_specs = P("refl", "slab", None, None, None)
    return jax.shard_map(
        per_device, mesh=mesh, in_specs=in_specs, out_specs=out_specs, check_vma=False
    )
```

```python
import functools

import jax
import jax.numpy as jnp
from jax import lax
from jax.experimental import pallas as pl
from jax.experimental.pallas import tpu as pltpu
from jax.sharding import PartitionSpec as P

MESH = pl.DeviceIdType.MESH


def extended(block, sides, width):
    for axis, dim in sides:
        count = lax.axis_size(axis)
        forward = [(i, i + 1) for i in range(count - 1)]
        backward = [(target, source) for source, target in forward]
        low = lax.ppermute(
            lax.slice_in_dim(block, block.shape[dim] - width, None, axis=dim), axis, forward
        )
        high = lax.ppermute(lax.slice_in_dim(block, 0, width, axis=dim), axis, backward)
        block = jnp.concatenate([low, block, high], axis=dim)
    return block


def central(field, dimension):
    widths = [(0, 0)] * field.ndim
    widths[dimension] = (1, 1)
    padded = jnp.pad(field, widths)
    length = field.shape[dimension]
    return 0.5 * (
        lax.slice_in_dim(padded, 2, length + 2, axis=dimension)
        - lax.slice_in_dim(padded, 0, length, axis=dimension)
    )


def phase_term(obj_real, obj_imag, grad_x, grad_y, grad_z, qrow):
    term_x = obj_real * grad_x[:, :, 1] - obj_imag * grad_x[:, :, 0]
    term_y = obj_real * grad_y[:, :, 1] - obj_imag * grad_y[:, :, 0]
    term_z = obj_real * grad_z[:, :, 1] - obj_imag * grad_z[:, :, 0]
    return qrow[0] * term_x + qrow[1] * term_y + qrow[2] * term_z


def post_kernel(
    scalars, code_ref, rows_ref, kernels_ref, obj_ref, out_ref, grid_ref, halo, gathered, phase_buf,
    halo_send, halo_recv, send_sem, recv_sem, slab_count,
):
    refl_count = gathered.shape[0]
    planes, rows, width = grid_ref.shape[0], grid_ref.shape[2], grid_ref.shape[3]
    kernel_count = kernels_ref.shape[0]
    blocks = planes * rows
    chosen = (
        code_ref[...] == lax.broadcasted_iota(jnp.int32, (kernel_count * blocks, code_ref.shape[1]), 0)
    ).astype(jnp.bfloat16)
    summed = jnp.dot(chosen, rows_ref[...], preferred_element_type=jnp.float32)
    for c in range(2):
        total = None
        for k in range(kernel_count):
            part = summed[k * blocks : (k + 1) * blocks, c * width : (c + 1) * width]
            weights = kernels_ref[k]
            for _ in range(3):
                piece = part.astype(jnp.bfloat16)
                term = jnp.dot(piece, weights, preferred_element_type=jnp.float32)
                total = term if total is None else total + term
                part = part - piece.astype(jnp.float32)
        for p in range(planes):
            grid_ref[p, c] = total[p * rows : (p + 1) * rows]
    me = lax.axis_index("slab")
    refl = lax.axis_index("refl")
    up = lax.rem(me + 1, slab_count)
    down = lax.rem(me + slab_count - 1, slab_count)
    barrier = pltpu.get_barrier_semaphore()
    pl.semaphore_signal(barrier, 1, device_id=(refl, up), device_id_type=MESH)
    pl.semaphore_signal(barrier, 1, device_id=(refl, down), device_id_type=MESH)
    for step in range(1, refl_count):
        peer = lax.rem(refl + step, refl_count)
        pl.semaphore_signal(barrier, 1, device_id=(peer, me), device_id_type=MESH)
    pl.semaphore_wait(barrier, refl_count + 1)
    low_copy = pltpu.make_async_remote_copy(
        src_ref=grid_ref.at[planes - 1], dst_ref=halo.at[0], send_sem=halo_send.at[0],
        recv_sem=halo_recv.at[0], device_id=(refl, up), device_id_type=MESH,
    )
    high_copy = pltpu.make_async_remote_copy(
        src_ref=grid_ref.at[0], dst_ref=halo.at[1], send_sem=halo_send.at[1],
        recv_sem=halo_recv.at[1], device_id=(refl, down), device_id_type=MESH,
    )
    low_copy.start()
    high_copy.start()
    row_of = lax.broadcasted_iota(jnp.int32, (rows, width), 0)
    lane_of = lax.broadcasted_iota(jnp.int32, (rows, width), 1)

    def along_y(field):
        after = jnp.where(row_of == rows - 1, 0.0, pltpu.roll(field, rows - 1, 0))
        before = jnp.where(row_of == 0, 0.0, pltpu.roll(field, 1, 0))
        return 0.5 * (after - before)

    def along_w(field):
        after = jnp.where(lane_of == width - 1, 0.0, pltpu.roll(field, width - 1, 1))
        before = jnp.where(lane_of == 0, 0.0, pltpu.roll(field, 1, 1))
        return 0.5 * (after - before)

    mate = refl + 1 - 2 * lax.rem(refl, 2)
    q0, q1, q2 = scalars[0, refl], scalars[1, refl], scalars[2, refl]
    d0 = q0 - scalars[0, mate]
    d1 = q1 - scalars[1, mate]
    d2 = q2 - scalars[2, mate]
    partial = []
    for p in range(planes):
        obj_re, obj_im = obj_ref[p, :, 0, :], obj_ref[p, :, 1, :]
        term_y = obj_re * along_y(grid_ref[p, 1]) - obj_im * along_y(grid_ref[p, 0])
        term_z = obj_re * along_w(grid_ref[p, 1]) - obj_im * along_w(grid_ref[p, 0])
        partial.append((term_y, term_z))
    low_copy.wait_send()
    high_copy.wait_send()
    low_copy.wait_recv()
    high_copy.wait_recv()
    has_low = me > 0
    has_high = me < slab_count - 1
    for p in range(planes):
        obj_re, obj_im = obj_ref[p, :, 0, :], obj_ref[p, :, 1, :]
        grad = []
        for c in range(2):
            ahead = grid_ref[p + 1, c] if p + 1 < planes else jnp.where(has_high, halo[1, c], 0.0)
            behind = grid_ref[p - 1, c] if p > 0 else jnp.where(has_low, halo[0, c], 0.0)
            grad.append(0.5 * (ahead - behind))
        term_x = obj_re * grad[1] - obj_im * grad[0]
        term_y, term_z = partial[p]
        phase_buf[p] = q0 * term_x + q1 * term_y + q2 * term_z
    copies = []
    for step in range(1, refl_count):
        peer = lax.rem(refl + step, refl_count)
        copy = pltpu.make_async_remote_copy(
            src_ref=phase_buf, dst_ref=gathered.at[refl], send_sem=send_sem.at[step],
            recv_sem=recv_sem.at[step], device_id=(peer, me), device_id_type=MESH,
        )
        copy.start()
        copies.append(copy)
    gathered[refl] = phase_buf[...]
    for copy in copies:
        copy.wait_send()
    for step in range(1, refl_count):
        source = lax.rem(refl + refl_count - step, refl_count)
        pltpu.make_async_remote_copy(
            src_ref=phase_buf, dst_ref=gathered.at[source], send_sem=send_sem.at[step],
            recv_sem=recv_sem.at[step], device_id=(source, me), device_id_type=MESH,
        ).wait_recv()
    def weight(r):
        return scalars[0, r] * d0 + scalars[1, r] * d1 + scalars[2, r] * d2

    shift = weight(0) * gathered[0]
    for r in range(1, refl_count):
        shift = shift + weight(r) * gathered[r]
    for p in range(planes):
        obj_re, obj_im = obj_ref[p, :, 0, :], obj_ref[p, :, 1, :]
        new_re = obj_re - 0.5 * (grid_ref[p, 0] - obj_im * shift[p])
        new_im = obj_im - 0.5 * (grid_ref[p, 1] + obj_re * shift[p])
        out_ref[p] = jnp.stack([new_re, new_im], axis=1)


def post_step(scalars, code_row, rows, kernels, obj, slab_count, refl_count):
    planes, rows_per, _, width = obj.shape
    return pl.pallas_call(
        functools.partial(post_kernel, slab_count=slab_count),
        out_shape=jax.ShapeDtypeStruct(obj.shape, jnp.float32),
        in_specs=[pl.BlockSpec(memory_space=pltpu.SMEM)]
        + [pl.BlockSpec(memory_space=pltpu.VMEM)] * 4,
        out_specs=pl.BlockSpec(memory_space=pltpu.VMEM),
        scratch_shapes=[
            pltpu.VMEM((planes, 2, rows_per, width), jnp.float32),
            pltpu.VMEM((2, 2, rows_per, width), jnp.float32),
            pltpu.VMEM((refl_count, planes, rows_per, width), jnp.float32),
            pltpu.VMEM((planes, rows_per, width), jnp.float32),
            pltpu.SemaphoreType.DMA((2,)),
            pltpu.SemaphoreType.DMA((2,)),
            pltpu.SemaphoreType.DMA((refl_count,)),
            pltpu.SemaphoreType.DMA((refl_count,)),
        ],
        compiler_params=pltpu.CompilerParams(collective_id=0, has_side_effects=True),
    )(scalars, code_row, rows, kernels, obj)


def exchange_kernel(
    slot_ref, values_ref, ids_ref, data_out, code_out, data_buf, code_in, data_send, data_recv, code_send,
    code_recv,
):
    count, capacity = data_out.shape[0], data_out.shape[1]
    group = 8 if count >= 16 else count // 2
    groups = count // group
    rows = group * capacity
    me = lax.axis_index("slab")
    refl = lax.axis_index("refl")
    barrier = pltpu.get_barrier_semaphore()

    def greet(step, carry):
        peer = lax.rem(me + step, count)
        pl.semaphore_signal(barrier, 1, device_id=(refl, peer), device_id_type=MESH)
        return carry

    lax.fori_loop(1, count, greet, 0)

    def pack(g):
        target = lax.broadcasted_iota(jnp.int32, (rows, slot_ref.shape[1]), 0) + g * rows
        chosen = (slot_ref[...] == target).astype(jnp.bfloat16)
        sent = jnp.dot(chosen, values_ref[...], preferred_element_type=jnp.float32)
        data_buf[pl.ds(g * group, group)] = sent.astype(jnp.bfloat16).reshape(
            group, capacity, sent.shape[1]
        )
        codes = lax.dot_general(
            ids_ref[...], chosen, (((1,), (1,)), ((), ())), preferred_element_type=jnp.float32
        )
        codes = (codes[0:1] * 8.0 + codes[1:2]).astype(jnp.int32)
        for part in range(group):
            window = (part * capacity) // 128
            code_in[g * group + part] = codes[:, window * 128 : (window + 1) * 128]

    def outgoing(d):
        data = pltpu.make_async_remote_copy(
            src_ref=data_buf.at[d], dst_ref=data_out.at[me], send_sem=data_send.at[d],
            recv_sem=data_recv.at[me], device_id=(refl, d), device_id_type=MESH,
        )
        code = pltpu.make_async_remote_copy(
            src_ref=code_in.at[d], dst_ref=code_out.at[me], send_sem=code_send.at[d],
            recv_sem=code_recv.at[me], device_id=(refl, d), device_id_type=MESH,
        )
        return data, code

    def incoming(s):
        data = pltpu.make_async_remote_copy(
            src_ref=data_buf.at[s], dst_ref=data_out.at[s], send_sem=data_send.at[s],
            recv_sem=data_recv.at[s], device_id=(refl, s), device_id_type=MESH,
        )
        code = pltpu.make_async_remote_copy(
            src_ref=code_in.at[s], dst_ref=code_out.at[s], send_sem=code_send.at[s],
            recv_sem=code_recv.at[s], device_id=(refl, s), device_id_type=MESH,
        )
        return data, code

    def send(g):
        for part in range(group):
            d = g * group + part

            @pl.when(d != me)
            def _():
                data, code = outgoing(d)
                code.start()
                data.start()

    home = me // group
    middle = groups // 2

    def order(j):
        return lax.rem(j + 0 * (home + middle), groups)

    first = order(0)
    pack(first)
    pl.semaphore_wait(barrier, count - 1)
    send(first)

    def later(j, carry):
        g = order(j)
        pack(g)
        send(g)
        return carry

    lax.fori_loop(1, groups, later, 0)
    data_out[me] = data_buf[me]
    local = pltpu.make_async_copy(code_in.at[me], code_out.at[me], code_send.at[me])
    local.start()

    def finish(step, carry):
        data, code = outgoing(lax.rem(me + step, count))
        data.wait_send()
        code.wait_send()
        data, code = incoming(lax.rem(me + count - step, count))
        data.wait_recv()
        code.wait_recv()
        return carry

    lax.fori_loop(1, count, finish, 0)
    local.wait()


def exchange_slab(flat_slot, values, ids, count, capacity):
    data_shape = (count, capacity, values.shape[1])
    code_shape = (count, 1, 128)
    return pl.pallas_call(
        exchange_kernel,
        out_shape=(
            jax.ShapeDtypeStruct(data_shape, jnp.bfloat16),
            jax.ShapeDtypeStruct(code_shape, jnp.int32),
        ),
        in_specs=[pl.BlockSpec(memory_space=pltpu.VMEM)] * 3,
        out_specs=(pl.BlockSpec(memory_space=pltpu.VMEM), pl.BlockSpec(memory_space=pl.ANY)),
        scratch_shapes=[
            pltpu.VMEM(data_shape, jnp.bfloat16),
            pltpu.VMEM(code_shape, jnp.int32),
            pltpu.SemaphoreType.DMA((count,)),
            pltpu.SemaphoreType.DMA((count,)),
            pltpu.SemaphoreType.DMA((count,)),
            pltpu.SemaphoreType.DMA((count,)),
        ],
        compiler_params=pltpu.CompilerParams(collective_id=1, has_side_effects=True),
    )(flat_slot, values, ids)


def per_device(detector, owners, block_ids, kernel_ids, kernels, bragg_vectors, object_field):
    slab_count = lax.axis_size("slab")
    plane_count = object_field.shape[1]
    row_count = object_field.shape[2]
    block_count = plane_count * row_count
    kernel_count = kernels.shape[0]
    tile_count = detector.shape[1]
    tile_width = detector.shape[3]
    row_width = 2 * tile_width
    capacity = 2 * tile_count // slab_count
    values = detector[0].reshape(tile_count, row_width)
    owner = owners[0, :, 0]
    order = lax.broadcasted_iota(jnp.int32, (tile_count, tile_count), 1) < lax.broadcasted_iota(
        jnp.int32, (tile_count, tile_count), 0
    )
    same = (owner[:, None] == owner[None, :]) & order
    slots = jnp.sum(same.astype(jnp.int32), axis=1)
    flat_slot = owner * capacity + slots
    ids = jnp.concatenate(
        [block_ids, kernel_ids, jnp.zeros((6, tile_count), jnp.int32)], axis=0
    ).astype(jnp.bfloat16)
    got, got_code = exchange_slab(flat_slot[None, :], values, ids, slab_count, capacity)
    row_total = slab_count * capacity
    rows = got.reshape(row_total, row_width)
    offset = lax.rem(lax.axis_index("slab"), 4) * capacity
    got_codes = lax.dynamic_slice_in_dim(got_code[:, 0, :], offset, capacity, axis=1).reshape(row_total)
    code_row = (lax.rem(got_codes, kernel_count) * block_count + got_codes // kernel_count)[None, :]
    refl_count = bragg_vectors.shape[0]
    obj = object_field[0]
    updated = post_step(bragg_vectors.T, code_row, rows, kernels, obj, slab_count, refl_count)
    return updated[None]


def solution(mesh):
    in_specs = (
        P("refl", "slab", None, None),
        P("refl", "slab", None),
        P("refl", "slab"),
        P("refl", "slab"),
        P(),
        P(),
        P("refl", "slab", None, None, None),
    )
    out_specs = P("refl", "slab", None, None, None)
    return jax.shard_map(
        per_device, mesh=mesh, in_specs=in_specs, out_specs=out_specs, check_vma=False
    )
```

```python
import functools

import jax
import jax.numpy as jnp
from jax import lax
from jax.experimental import pallas as pl
from jax.experimental.pallas import tpu as pltpu
from jax.sharding import PartitionSpec as P

MESH = pl.DeviceIdType.MESH


def extended(block, sides, width):
    for axis, dim in sides:
        count = lax.axis_size(axis)
        forward = [(i, i + 1) for i in range(count - 1)]
        backward = [(target, source) for source, target in forward]
        low = lax.ppermute(
            lax.slice_in_dim(block, block.shape[dim] - width, None, axis=dim), axis, forward
        )
        high = lax.ppermute(lax.slice_in_dim(block, 0, width, axis=dim), axis, backward)
        block = jnp.concatenate([low, block, high], axis=dim)
    return block


def central(field, dimension):
    widths = [(0, 0)] * field.ndim
    widths[dimension] = (1, 1)
    padded = jnp.pad(field, widths)
    length = field.shape[dimension]
    return 0.5 * (
        lax.slice_in_dim(padded, 2, length + 2, axis=dimension)
        - lax.slice_in_dim(padded, 0, length, axis=dimension)
    )


def phase_term(obj_real, obj_imag, grad_x, grad_y, grad_z, qrow):
    term_x = obj_real * grad_x[:, :, 1] - obj_imag * grad_x[:, :, 0]
    term_y = obj_real * grad_y[:, :, 1] - obj_imag * grad_y[:, :, 0]
    term_z = obj_real * grad_z[:, :, 1] - obj_imag * grad_z[:, :, 0]
    return qrow[0] * term_x + qrow[1] * term_y + qrow[2] * term_z


def post_kernel(
    scalars, code_ref, rows_ref, kernels_ref, obj_ref, grid_ref, out_ref, halo, gathered, phase_buf,
    halo_send, halo_recv, send_sem, recv_sem, slab_count,
):
    refl_count = gathered.shape[0]
    planes, rows, width = grid_ref.shape[0], grid_ref.shape[2], grid_ref.shape[3]
    kernel_count = kernels_ref.shape[0]
    blocks = planes * rows
    chosen = (
        code_ref[...] == lax.broadcasted_iota(jnp.int32, (kernel_count * blocks, code_ref.shape[1]), 0)
    ).astype(jnp.bfloat16)
    summed = jnp.dot(chosen, rows_ref[...], preferred_element_type=jnp.float32)
    for c in range(2):
        total = None
        for k in range(kernel_count):
            part = summed[k * blocks : (k + 1) * blocks, c * width : (c + 1) * width]
            weights = kernels_ref[k]
            for _ in range(3):
                piece = part.astype(jnp.bfloat16)
                term = jnp.dot(piece, weights, preferred_element_type=jnp.float32)
                total = term if total is None else total + term
                part = part - piece.astype(jnp.float32)
        for p in range(planes):
            grid_ref[p, c] = total[p * rows : (p + 1) * rows]
    me = lax.axis_index("slab")
    refl = lax.axis_index("refl")
    up = lax.rem(me + 1, slab_count)
    down = lax.rem(me + slab_count - 1, slab_count)
    barrier = pltpu.get_barrier_semaphore()
    pl.semaphore_signal(barrier, 1, device_id=(refl, up), device_id_type=MESH)
    pl.semaphore_signal(barrier, 1, device_id=(refl, down), device_id_type=MESH)
    for step in range(1, refl_count):
        peer = lax.rem(refl + step, refl_count)
        pl.semaphore_signal(barrier, 1, device_id=(peer, me), device_id_type=MESH)
    pl.semaphore_wait(barrier, refl_count + 1)
    low_copy = pltpu.make_async_remote_copy(
        src_ref=grid_ref.at[planes - 1], dst_ref=halo.at[0], send_sem=halo_send.at[0],
        recv_sem=halo_recv.at[0], device_id=(refl, up), device_id_type=MESH,
    )
    high_copy = pltpu.make_async_remote_copy(
        src_ref=grid_ref.at[0], dst_ref=halo.at[1], send_sem=halo_send.at[1],
        recv_sem=halo_recv.at[1], device_id=(refl, down), device_id_type=MESH,
    )
    low_copy.start()
    high_copy.start()
    row_of = lax.broadcasted_iota(jnp.int32, (rows, width), 0)
    lane_of = lax.broadcasted_iota(jnp.int32, (rows, width), 1)

    def along_y(field):
        after = jnp.where(row_of == rows - 1, 0.0, pltpu.roll(field, rows - 1, 0))
        before = jnp.where(row_of == 0, 0.0, pltpu.roll(field, 1, 0))
        return 0.5 * (after - before)

    def along_w(field):
        after = jnp.where(lane_of == width - 1, 0.0, pltpu.roll(field, width - 1, 1))
        before = jnp.where(lane_of == 0, 0.0, pltpu.roll(field, 1, 1))
        return 0.5 * (after - before)

    mate = refl + 1 - 2 * lax.rem(refl, 2)
    q0, q1, q2 = scalars[0, refl], scalars[1, refl], scalars[2, refl]
    d0 = q0 - scalars[0, mate]
    d1 = q1 - scalars[1, mate]
    d2 = q2 - scalars[2, mate]
    partial = []
    for p in range(planes):
        obj_re, obj_im = obj_ref[p, :, 0, :], obj_ref[p, :, 1, :]
        term_y = obj_re * along_y(grid_ref[p, 1]) - obj_im * along_y(grid_ref[p, 0])
        term_z = obj_re * along_w(grid_ref[p, 1]) - obj_im * along_w(grid_ref[p, 0])
        partial.append((term_y, term_z))
    low_copy.wait_send()
    high_copy.wait_send()
    low_copy.wait_recv()
    high_copy.wait_recv()
    has_low = me > 0
    has_high = me < slab_count - 1
    for p in range(planes):
        obj_re, obj_im = obj_ref[p, :, 0, :], obj_ref[p, :, 1, :]
        grad = []
        for c in range(2):
            ahead = grid_ref[p + 1, c] if p + 1 < planes else jnp.where(has_high, halo[1, c], 0.0)
            behind = grid_ref[p - 1, c] if p > 0 else jnp.where(has_low, halo[0, c], 0.0)
            grad.append(0.5 * (ahead - behind))
        term_x = obj_re * grad[1] - obj_im * grad[0]
        term_y, term_z = partial[p]
        phase_buf[p] = q0 * term_x + q1 * term_y + q2 * term_z
    copies = []
    for step in range(1, refl_count):
        peer = lax.rem(refl + step, refl_count)
        copy = pltpu.make_async_remote_copy(
            src_ref=phase_buf, dst_ref=gathered.at[refl], send_sem=send_sem.at[step],
            recv_sem=recv_sem.at[step], device_id=(peer, me), device_id_type=MESH,
        )
        copy.start()
        copies.append(copy)
    gathered[refl] = phase_buf[...]
    for copy in copies:
        copy.wait_send()
    for step in range(1, refl_count):
        source = lax.rem(refl + refl_count - step, refl_count)
        pltpu.make_async_remote_copy(
            src_ref=phase_buf, dst_ref=gathered.at[source], send_sem=send_sem.at[step],
            recv_sem=recv_sem.at[step], device_id=(source, me), device_id_type=MESH,
        ).wait_recv()
    def weight(r):
        return scalars[0, r] * d0 + scalars[1, r] * d1 + scalars[2, r] * d2

    shift = weight(0) * gathered[0]
    for r in range(1, refl_count):
        shift = shift + weight(r) * gathered[r]
    out_ref[...] = shift


def update_kernel(obj_ref, grid_ref, shift_ref, out_ref):
    for p in range(grid_ref.shape[0]):
        obj_re, obj_im = obj_ref[p, :, 0, :], obj_ref[p, :, 1, :]
        new_re = obj_re - 0.5 * (grid_ref[p, 0] - obj_im * shift_ref[p])
        new_im = obj_im - 0.5 * (grid_ref[p, 1] + obj_re * shift_ref[p])
        out_ref[p] = jnp.stack([new_re, new_im], axis=1)


def update_step(obj, grid, shift):
    return pl.pallas_call(
        update_kernel,
        out_shape=jax.ShapeDtypeStruct(obj.shape, jnp.float32),
        in_specs=[pl.BlockSpec(memory_space=pltpu.VMEM)] * 3,
        out_specs=pl.BlockSpec(memory_space=pltpu.VMEM),
    )(obj, grid, shift)


def post_step(scalars, code_row, rows, kernels, obj, slab_count, refl_count):
    planes, rows_per, _, width = obj.shape
    return pl.pallas_call(
        functools.partial(post_kernel, slab_count=slab_count),
        out_shape=(
            jax.ShapeDtypeStruct((planes, 2, rows_per, width), jnp.float32),
            jax.ShapeDtypeStruct((planes, rows_per, width), jnp.float32),
        ),
        in_specs=[pl.BlockSpec(memory_space=pltpu.SMEM)]
        + [pl.BlockSpec(memory_space=pltpu.VMEM)] * 4,
        out_specs=(pl.BlockSpec(memory_space=pltpu.VMEM), pl.BlockSpec(memory_space=pltpu.VMEM)),
        scratch_shapes=[
            pltpu.VMEM((2, 2, rows_per, width), jnp.float32),
            pltpu.VMEM((refl_count, planes, rows_per, width), jnp.float32),
            pltpu.VMEM((planes, rows_per, width), jnp.float32),
            pltpu.SemaphoreType.DMA((2,)),
            pltpu.SemaphoreType.DMA((2,)),
            pltpu.SemaphoreType.DMA((refl_count,)),
            pltpu.SemaphoreType.DMA((refl_count,)),
        ],
        compiler_params=pltpu.CompilerParams(collective_id=0, has_side_effects=True),
    )(scalars, code_row, rows, kernels, obj)


def exchange_kernel(
    slot_ref, values_ref, ids_ref, data_out, code_out, data_buf, code_in, data_send, data_recv, code_send,
    code_recv,
):
    count, capacity = data_out.shape[0], data_out.shape[1]
    group = 8 if count >= 16 else count // 2
    groups = count // group
    rows = group * capacity
    me = lax.axis_index("slab")
    refl = lax.axis_index("refl")
    barrier = pltpu.get_barrier_semaphore()

    def greet(step, carry):
        peer = lax.rem(me + step, count)
        pl.semaphore_signal(barrier, 1, device_id=(refl, peer), device_id_type=MESH)
        return carry

    lax.fori_loop(1, count, greet, 0)

    def pack(g):
        target = lax.broadcasted_iota(jnp.int32, (rows, slot_ref.shape[1]), 0) + g * rows
        chosen = (slot_ref[...] == target).astype(jnp.bfloat16)
        sent = jnp.dot(chosen, values_ref[...], preferred_element_type=jnp.float32)
        data_buf[pl.ds(g * group, group)] = sent.astype(jnp.bfloat16).reshape(
            group, capacity, sent.shape[1]
        )
        codes = lax.dot_general(
            ids_ref[...], chosen, (((1,), (1,)), ((), ())), preferred_element_type=jnp.float32
        )
        codes = (codes[0:1] * 8.0 + codes[1:2]).astype(jnp.int32)
        for part in range(group):
            window = (part * capacity) // 128
            code_in[g * group + part] = codes[:, window * 128 : (window + 1) * 128]

    def outgoing(d):
        data = pltpu.make_async_remote_copy(
            src_ref=data_buf.at[d], dst_ref=data_out.at[me], send_sem=data_send.at[d],
            recv_sem=data_recv.at[me], device_id=(refl, d), device_id_type=MESH,
        )
        code = pltpu.make_async_remote_copy(
            src_ref=code_in.at[d], dst_ref=code_out.at[me], send_sem=code_send.at[d],
            recv_sem=code_recv.at[me], device_id=(refl, d), device_id_type=MESH,
        )
        return data, code

    def incoming(s):
        data = pltpu.make_async_remote_copy(
            src_ref=data_buf.at[s], dst_ref=data_out.at[s], send_sem=data_send.at[s],
            recv_sem=data_recv.at[s], device_id=(refl, s), device_id_type=MESH,
        )
        code = pltpu.make_async_remote_copy(
            src_ref=code_in.at[s], dst_ref=code_out.at[s], send_sem=code_send.at[s],
            recv_sem=code_recv.at[s], device_id=(refl, s), device_id_type=MESH,
        )
        return data, code

    def send(g):
        for part in range(group):
            d = g * group + part

            @pl.when(d != me)
            def _():
                data, code = outgoing(d)
                code.start()
                data.start()

    home = me // group
    middle = groups // 2

    def order(j):
        return lax.rem(home + middle + (1 - 2 * lax.rem(j, 2)) * ((j + 1) // 2) + groups, groups)

    first = order(0)
    pack(first)
    pl.semaphore_wait(barrier, count - 1)
    send(first)

    def later(j, carry):
        g = order(j)
        pack(g)
        send(g)
        return carry

    lax.fori_loop(1, groups, later, 0)
    data_out[me] = data_buf[me]
    local = pltpu.make_async_copy(code_in.at[me], code_out.at[me], code_send.at[me])
    local.start()

    def finish(step, carry):
        data, code = outgoing(lax.rem(me + step, count))
        data.wait_send()
        code.wait_send()
        data, code = incoming(lax.rem(me + count - step, count))
        data.wait_recv()
        code.wait_recv()
        return carry

    lax.fori_loop(1, count, finish, 0)
    local.wait()


def exchange_slab(flat_slot, values, ids, count, capacity):
    data_shape = (count, capacity, values.shape[1])
    code_shape = (count, 1, 128)
    return pl.pallas_call(
        exchange_kernel,
        out_shape=(
            jax.ShapeDtypeStruct(data_shape, jnp.bfloat16),
            jax.ShapeDtypeStruct(code_shape, jnp.int32),
        ),
        in_specs=[pl.BlockSpec(memory_space=pltpu.VMEM)] * 3,
        out_specs=(pl.BlockSpec(memory_space=pltpu.VMEM), pl.BlockSpec(memory_space=pl.ANY)),
        scratch_shapes=[
            pltpu.VMEM(data_shape, jnp.bfloat16),
            pltpu.VMEM(code_shape, jnp.int32),
            pltpu.SemaphoreType.DMA((count,)),
            pltpu.SemaphoreType.DMA((count,)),
            pltpu.SemaphoreType.DMA((count,)),
            pltpu.SemaphoreType.DMA((count,)),
        ],
        compiler_params=pltpu.CompilerParams(collective_id=1, has_side_effects=True),
    )(flat_slot, values, ids)


def per_device(detector, owners, block_ids, kernel_ids, kernels, bragg_vectors, object_field):
    slab_count = lax.axis_size("slab")
    plane_count = object_field.shape[1]
    row_count = object_field.shape[2]
    block_count = plane_count * row_count
    kernel_count = kernels.shape[0]
    tile_count = detector.shape[1]
    tile_width = detector.shape[3]
    row_width = 2 * tile_width
    capacity = 2 * tile_count // slab_count
    values = detector[0].reshape(tile_count, row_width)
    owner = owners[0, :, 0]
    order = lax.broadcasted_iota(jnp.int32, (tile_count, tile_count), 1) < lax.broadcasted_iota(
        jnp.int32, (tile_count, tile_count), 0
    )
    same = (owner[:, None] == owner[None, :]) & order
    slots = jnp.sum(same.astype(jnp.int32), axis=1)
    flat_slot = owner * capacity + slots
    ids = jnp.concatenate(
        [block_ids, kernel_ids, jnp.zeros((6, tile_count), jnp.int32)], axis=0
    ).astype(jnp.bfloat16)
    got, got_code = exchange_slab(flat_slot[None, :], values, ids, slab_count, capacity)
    row_total = slab_count * capacity
    rows = got.reshape(row_total, row_width)
    offset = lax.rem(lax.axis_index("slab"), 4) * capacity
    got_codes = lax.dynamic_slice_in_dim(got_code[:, 0, :], offset, capacity, axis=1).reshape(row_total)
    code_row = (lax.rem(got_codes, kernel_count) * block_count + got_codes // kernel_count)[None, :]
    refl_count = bragg_vectors.shape[0]
    obj = object_field[0]
    gridded, shift = post_step(bragg_vectors.T, code_row, rows, kernels, obj, slab_count, refl_count)
    return update_step(obj, gridded, shift)[None]


def solution(mesh):
    in_specs = (
        P("refl", "slab", None, None),
        P("refl", "slab", None),
        P("refl", "slab"),
        P("refl", "slab"),
        P(),
        P(),
        P("refl", "slab", None, None, None),
    )
    out_specs = P("refl", "slab", None, None, None)
    return jax.shard_map(
        per_device, mesh=mesh, in_specs=in_specs, out_specs=out_specs, check_vma=False
    )
```

```python
import functools

import jax
import jax.numpy as jnp
from jax import lax
from jax.experimental import pallas as pl
from jax.experimental.pallas import tpu as pltpu
from jax.sharding import PartitionSpec as P

MESH = pl.DeviceIdType.MESH


def extended(block, sides, width):
    for axis, dim in sides:
        count = lax.axis_size(axis)
        forward = [(i, i + 1) for i in range(count - 1)]
        backward = [(target, source) for source, target in forward]
        low = lax.ppermute(
            lax.slice_in_dim(block, block.shape[dim] - width, None, axis=dim), axis, forward
        )
        high = lax.ppermute(lax.slice_in_dim(block, 0, width, axis=dim), axis, backward)
        block = jnp.concatenate([low, block, high], axis=dim)
    return block


def central(field, dimension):
    widths = [(0, 0)] * field.ndim
    widths[dimension] = (1, 1)
    padded = jnp.pad(field, widths)
    length = field.shape[dimension]
    return 0.5 * (
        lax.slice_in_dim(padded, 2, length + 2, axis=dimension)
        - lax.slice_in_dim(padded, 0, length, axis=dimension)
    )


def phase_term(obj_real, obj_imag, grad_x, grad_y, grad_z, qrow):
    term_x = obj_real * grad_x[:, :, 1] - obj_imag * grad_x[:, :, 0]
    term_y = obj_real * grad_y[:, :, 1] - obj_imag * grad_y[:, :, 0]
    term_z = obj_real * grad_z[:, :, 1] - obj_imag * grad_z[:, :, 0]
    return qrow[0] * term_x + qrow[1] * term_y + qrow[2] * term_z


def post_kernel(
    scalars, code_ref, rows_ref, kernels_ref, obj_ref, out_ref, grid_ref, halo, gathered, phase_buf,
    halo_send, halo_recv, send_sem, recv_sem, slab_count,
):
    refl_count = gathered.shape[0]
    planes, rows, width = grid_ref.shape[0], grid_ref.shape[2], grid_ref.shape[3]
    kernel_count = kernels_ref.shape[0]
    blocks = planes * rows
    me = lax.axis_index("slab")
    refl = lax.axis_index("refl")
    up = lax.rem(me + 1, slab_count)
    down = lax.rem(me + slab_count - 1, slab_count)
    barrier = pltpu.get_barrier_semaphore()
    pl.semaphore_signal(barrier, 1, device_id=(refl, up), device_id_type=MESH)
    pl.semaphore_signal(barrier, 1, device_id=(refl, down), device_id_type=MESH)
    for step in range(1, refl_count):
        peer = lax.rem(refl + step, refl_count)
        pl.semaphore_signal(barrier, 1, device_id=(peer, me), device_id_type=MESH)
    chosen = (
        code_ref[...] == lax.broadcasted_iota(jnp.int32, (kernel_count * blocks, code_ref.shape[1]), 0)
    ).astype(jnp.bfloat16)
    summed = jnp.dot(chosen, rows_ref[...], preferred_element_type=jnp.float32)
    for c in range(2):
        total = None
        for k in range(kernel_count):
            part = summed[k * blocks : (k + 1) * blocks, c * width : (c + 1) * width]
            weights = kernels_ref[k]
            for _ in range(3):
                piece = part.astype(jnp.bfloat16)
                term = jnp.dot(piece, weights, preferred_element_type=jnp.float32)
                total = term if total is None else total + term
                part = part - piece.astype(jnp.float32)
        for p in range(planes):
            grid_ref[p, c] = total[p * rows : (p + 1) * rows]
    pl.semaphore_wait(barrier, refl_count + 1)
    low_copy = pltpu.make_async_remote_copy(
        src_ref=grid_ref.at[planes - 1], dst_ref=halo.at[0], send_sem=halo_send.at[0],
        recv_sem=halo_recv.at[0], device_id=(refl, up), device_id_type=MESH,
    )
    high_copy = pltpu.make_async_remote_copy(
        src_ref=grid_ref.at[0], dst_ref=halo.at[1], send_sem=halo_send.at[1],
        recv_sem=halo_recv.at[1], device_id=(refl, down), device_id_type=MESH,
    )
    low_copy.start()
    high_copy.start()
    row_of = lax.broadcasted_iota(jnp.int32, (rows, width), 0)
    lane_of = lax.broadcasted_iota(jnp.int32, (rows, width), 1)

    def along_y(field):
        after = jnp.where(row_of == rows - 1, 0.0, pltpu.roll(field, rows - 1, 0))
        before = jnp.where(row_of == 0, 0.0, pltpu.roll(field, 1, 0))
        return 0.5 * (after - before)

    def along_w(field):
        after = jnp.where(lane_of == width - 1, 0.0, pltpu.roll(field, width - 1, 1))
        before = jnp.where(lane_of == 0, 0.0, pltpu.roll(field, 1, 1))
        return 0.5 * (after - before)

    mate = refl + 1 - 2 * lax.rem(refl, 2)
    q0, q1, q2 = scalars[refl, 0], scalars[refl, 1], scalars[refl, 2]
    d0 = q0 - scalars[mate, 0]
    d1 = q1 - scalars[mate, 1]
    d2 = q2 - scalars[mate, 2]
    partial = []
    for p in range(planes):
        obj_re, obj_im = obj_ref[p, :, 0, :], obj_ref[p, :, 1, :]
        term_y = obj_re * along_y(grid_ref[p, 1]) - obj_im * along_y(grid_ref[p, 0])
        term_z = obj_re * along_w(grid_ref[p, 1]) - obj_im * along_w(grid_ref[p, 0])
        partial.append((term_y, term_z))
    low_copy.wait_send()
    high_copy.wait_send()
    low_copy.wait_recv()
    high_copy.wait_recv()
    has_low = me > 0
    has_high = me < slab_count - 1
    for p in range(planes):
        obj_re, obj_im = obj_ref[p, :, 0, :], obj_ref[p, :, 1, :]
        grad = []
        for c in range(2):
            ahead = grid_ref[p + 1, c] if p + 1 < planes else jnp.where(has_high, halo[1, c], 0.0)
            behind = grid_ref[p - 1, c] if p > 0 else jnp.where(has_low, halo[0, c], 0.0)
            grad.append(0.5 * (ahead - behind))
        term_x = obj_re * grad[1] - obj_im * grad[0]
        term_y, term_z = partial[p]
        phase_buf[p] = q0 * term_x + q1 * term_y + q2 * term_z
    copies = []
    for step in range(1, refl_count):
        peer = lax.rem(refl + step, refl_count)
        copy = pltpu.make_async_remote_copy(
            src_ref=phase_buf, dst_ref=gathered.at[refl], send_sem=send_sem.at[step],
            recv_sem=recv_sem.at[step], device_id=(peer, me), device_id_type=MESH,
        )
        copy.start()
        copies.append(copy)
    gathered[refl] = phase_buf[...]
    for copy in copies:
        copy.wait_send()
    for step in range(1, refl_count):
        source = lax.rem(refl + refl_count - step, refl_count)
        pltpu.make_async_remote_copy(
            src_ref=phase_buf, dst_ref=gathered.at[source], send_sem=send_sem.at[step],
            recv_sem=recv_sem.at[step], device_id=(source, me), device_id_type=MESH,
        ).wait_recv()
    def weight(r):
        return scalars[r, 0] * d0 + scalars[r, 1] * d1 + scalars[r, 2] * d2

    shift = weight(0) * gathered[0]
    for r in range(1, refl_count):
        shift = shift + weight(r) * gathered[r]
    for p in range(planes):
        obj_re, obj_im = obj_ref[p, :, 0, :], obj_ref[p, :, 1, :]
        new_re = obj_re - 0.5 * (grid_ref[p, 0] - obj_im * shift[p])
        new_im = obj_im - 0.5 * (grid_ref[p, 1] + obj_re * shift[p])
        out_ref[p] = jnp.stack([new_re, new_im], axis=1)


def post_step(scalars, code_row, rows, kernels, obj, slab_count, refl_count):
    planes, rows_per, _, width = obj.shape
    return pl.pallas_call(
        functools.partial(post_kernel, slab_count=slab_count),
        out_shape=jax.ShapeDtypeStruct(obj.shape, jnp.float32),
        in_specs=[pl.BlockSpec(memory_space=pltpu.SMEM)]
        + [pl.BlockSpec(memory_space=pltpu.VMEM)] * 4,
        out_specs=pl.BlockSpec(memory_space=pltpu.VMEM),
        scratch_shapes=[
            pltpu.VMEM((planes, 2, rows_per, width), jnp.float32),
            pltpu.VMEM((2, 2, rows_per, width), jnp.float32),
            pltpu.VMEM((refl_count, planes, rows_per, width), jnp.float32),
            pltpu.VMEM((planes, rows_per, width), jnp.float32),
            pltpu.SemaphoreType.DMA((2,)),
            pltpu.SemaphoreType.DMA((2,)),
            pltpu.SemaphoreType.DMA((refl_count,)),
            pltpu.SemaphoreType.DMA((refl_count,)),
        ],
        compiler_params=pltpu.CompilerParams(collective_id=0, has_side_effects=True),
    )(scalars, code_row, rows, kernels, obj)


def exchange_kernel(
    slot_ref, values_ref, ids_ref, data_out, code_out, data_buf, code_in, data_send, data_recv, code_send,
    code_recv,
):
    count, capacity = data_out.shape[0], data_out.shape[1]
    group = 8 if count >= 16 else count // 2
    groups = count // group
    rows = group * capacity
    me = lax.axis_index("slab")
    refl = lax.axis_index("refl")
    barrier = pltpu.get_barrier_semaphore()

    def greet(step, carry):
        peer = lax.rem(me + step, count)
        pl.semaphore_signal(barrier, 1, device_id=(refl, peer), device_id_type=MESH)
        return carry

    lax.fori_loop(1, count, greet, 0)

    def pack(g):
        target = lax.broadcasted_iota(jnp.int32, (rows, slot_ref.shape[1]), 0) + g * rows
        chosen = (slot_ref[...] == target).astype(jnp.bfloat16)
        sent = jnp.dot(chosen, values_ref[...], preferred_element_type=jnp.float32)
        data_buf[pl.ds(g * group, group)] = sent.astype(jnp.bfloat16).reshape(
            group, capacity, sent.shape[1]
        )
        codes = lax.dot_general(
            ids_ref[...], chosen, (((1,), (1,)), ((), ())), preferred_element_type=jnp.float32
        )
        codes = (codes[0:1] * 8.0 + codes[1:2]).astype(jnp.int32)
        for part in range(group):
            window = (part * capacity) // 128
            code_in[g * group + part] = codes[:, window * 128 : (window + 1) * 128]

    def outgoing(d):
        data = pltpu.make_async_remote_copy(
            src_ref=data_buf.at[d], dst_ref=data_out.at[me], send_sem=data_send.at[d],
            recv_sem=data_recv.at[me], device_id=(refl, d), device_id_type=MESH,
        )
        code = pltpu.make_async_remote_copy(
            src_ref=code_in.at[d], dst_ref=code_out.at[me], send_sem=code_send.at[d],
            recv_sem=code_recv.at[me], device_id=(refl, d), device_id_type=MESH,
        )
        return data, code

    def incoming(s):
        data = pltpu.make_async_remote_copy(
            src_ref=data_buf.at[s], dst_ref=data_out.at[s], send_sem=data_send.at[s],
            recv_sem=data_recv.at[s], device_id=(refl, s), device_id_type=MESH,
        )
        code = pltpu.make_async_remote_copy(
            src_ref=code_in.at[s], dst_ref=code_out.at[s], send_sem=code_send.at[s],
            recv_sem=code_recv.at[s], device_id=(refl, s), device_id_type=MESH,
        )
        return data, code

    def send(g):
        for part in range(group):
            d = g * group + part

            @pl.when(d != me)
            def _():
                data, code = outgoing(d)
                code.start()
                data.start()

    home = me // group
    middle = groups // 2

    def order(j):
        return lax.rem(home + middle + (1 - 2 * lax.rem(j, 2)) * ((j + 1) // 2) + groups, groups)

    first = order(0)
    pack(first)
    pl.semaphore_wait(barrier, count - 1)
    send(first)

    def later(j, carry):
        g = order(j)
        pack(g)
        send(g)
        return carry

    lax.fori_loop(1, groups, later, 0)
    data_out[me] = data_buf[me]
    local = pltpu.make_async_copy(code_in.at[me], code_out.at[me], code_send.at[me])
    local.start()

    def finish(step, carry):
        data, code = outgoing(lax.rem(me + step, count))
        data.wait_send()
        code.wait_send()
        data, code = incoming(lax.rem(me + count - step, count))
        data.wait_recv()
        code.wait_recv()
        return carry

    lax.fori_loop(1, count, finish, 0)
    local.wait()


def exchange_slab(flat_slot, values, ids, count, capacity):
    data_shape = (count, capacity, values.shape[1])
    code_shape = (count, 1, 128)
    return pl.pallas_call(
        exchange_kernel,
        out_shape=(
            jax.ShapeDtypeStruct(data_shape, jnp.bfloat16),
            jax.ShapeDtypeStruct(code_shape, jnp.int32),
        ),
        in_specs=[pl.BlockSpec(memory_space=pltpu.VMEM)] * 3,
        out_specs=(pl.BlockSpec(memory_space=pltpu.VMEM), pl.BlockSpec(memory_space=pl.ANY)),
        scratch_shapes=[
            pltpu.VMEM(data_shape, jnp.bfloat16),
            pltpu.VMEM(code_shape, jnp.int32),
            pltpu.SemaphoreType.DMA((count,)),
            pltpu.SemaphoreType.DMA((count,)),
            pltpu.SemaphoreType.DMA((count,)),
            pltpu.SemaphoreType.DMA((count,)),
        ],
        compiler_params=pltpu.CompilerParams(collective_id=1, has_side_effects=True),
    )(flat_slot, values, ids)


def per_device(detector, owners, block_ids, kernel_ids, kernels, bragg_vectors, object_field):
    slab_count = lax.axis_size("slab")
    plane_count = object_field.shape[1]
    row_count = object_field.shape[2]
    block_count = plane_count * row_count
    kernel_count = kernels.shape[0]
    tile_count = detector.shape[1]
    tile_width = detector.shape[3]
    row_width = 2 * tile_width
    capacity = 2 * tile_count // slab_count
    values = detector[0].reshape(tile_count, row_width)
    owner = owners[0, :, 0]
    order = lax.broadcasted_iota(jnp.int32, (tile_count, tile_count), 1) < lax.broadcasted_iota(
        jnp.int32, (tile_count, tile_count), 0
    )
    same = (owner[:, None] == owner[None, :]) & order
    slots = jnp.sum(same.astype(jnp.int32), axis=1)
    flat_slot = owner * capacity + slots
    ids = jnp.concatenate(
        [block_ids, kernel_ids, jnp.zeros((6, tile_count), jnp.int32)], axis=0
    ).astype(jnp.bfloat16)
    got, got_code = exchange_slab(flat_slot[None, :], values, ids, slab_count, capacity)
    row_total = slab_count * capacity
    rows = got.reshape(row_total, row_width)
    offset = lax.rem(lax.axis_index("slab"), 4) * capacity
    got_codes = lax.dynamic_slice_in_dim(got_code[:, 0, :], offset, capacity, axis=1).reshape(row_total)
    code_row = (lax.rem(got_codes, kernel_count) * block_count + got_codes // kernel_count)[None, :]
    refl_count = bragg_vectors.shape[0]
    obj = object_field[0]
    updated = post_step(bragg_vectors, code_row, rows, kernels, obj, slab_count, refl_count)
    return updated[None]


def solution(mesh):
    in_specs = (
        P("refl", "slab", None, None),
        P("refl", "slab", None),
        P("refl", "slab"),
        P("refl", "slab"),
        P(),
        P(),
        P("refl", "slab", None, None, None),
    )
    out_specs = P("refl", "slab", None, None, None)
    return jax.shard_map(
        per_device, mesh=mesh, in_specs=in_specs, out_specs=out_specs, check_vma=False
    )
```

```python
import functools

import jax
import jax.numpy as jnp
from jax import lax
from jax.experimental import pallas as pl
from jax.experimental.pallas import tpu as pltpu
from jax.sharding import PartitionSpec as P

MESH = pl.DeviceIdType.MESH


def extended(block, sides, width):
    for axis, dim in sides:
        count = lax.axis_size(axis)
        forward = [(i, i + 1) for i in range(count - 1)]
        backward = [(target, source) for source, target in forward]
        low = lax.ppermute(
            lax.slice_in_dim(block, block.shape[dim] - width, None, axis=dim), axis, forward
        )
        high = lax.ppermute(lax.slice_in_dim(block, 0, width, axis=dim), axis, backward)
        block = jnp.concatenate([low, block, high], axis=dim)
    return block


def central(field, dimension):
    widths = [(0, 0)] * field.ndim
    widths[dimension] = (1, 1)
    padded = jnp.pad(field, widths)
    length = field.shape[dimension]
    return 0.5 * (
        lax.slice_in_dim(padded, 2, length + 2, axis=dimension)
        - lax.slice_in_dim(padded, 0, length, axis=dimension)
    )


def phase_term(obj_real, obj_imag, grad_x, grad_y, grad_z, qrow):
    term_x = obj_real * grad_x[:, :, 1] - obj_imag * grad_x[:, :, 0]
    term_y = obj_real * grad_y[:, :, 1] - obj_imag * grad_y[:, :, 0]
    term_z = obj_real * grad_z[:, :, 1] - obj_imag * grad_z[:, :, 0]
    return qrow[0] * term_x + qrow[1] * term_y + qrow[2] * term_z


def post_kernel(
    scalars, code_ref, rows_ref, kernels_ref, obj_ref, out_ref, grid_ref, halo, gathered, phase_buf,
    halo_send, halo_recv, send_sem, recv_sem, slab_count,
):
    refl_count = gathered.shape[0]
    planes, rows, width = grid_ref.shape[0], grid_ref.shape[2], grid_ref.shape[3]
    kernel_count = kernels_ref.shape[0]
    blocks = planes * rows
    me = lax.axis_index("slab")
    refl = lax.axis_index("refl")
    up = lax.rem(me + 1, slab_count)
    down = lax.rem(me + slab_count - 1, slab_count)
    barrier = pltpu.get_barrier_semaphore()
    pl.semaphore_signal(barrier, 1, device_id=(refl, up), device_id_type=MESH)
    pl.semaphore_signal(barrier, 1, device_id=(refl, down), device_id_type=MESH)
    for step in range(1, refl_count):
        peer = lax.rem(refl + step, refl_count)
        pl.semaphore_signal(barrier, 1, device_id=(peer, me), device_id_type=MESH)
    chosen = (
        code_ref[...] == lax.broadcasted_iota(jnp.int32, (kernel_count * blocks, code_ref.shape[1]), 0)
    ).astype(jnp.bfloat16)
    summed = jnp.dot(chosen, rows_ref[...], preferred_element_type=jnp.float32)
    for c in range(2):
        total = None
        for k in range(kernel_count):
            part = summed[k * blocks : (k + 1) * blocks, c * width : (c + 1) * width]
            weights = kernels_ref[k]
            for _ in range(3):
                piece = part.astype(jnp.bfloat16)
                term = jnp.dot(piece, weights, preferred_element_type=jnp.float32)
                total = term if total is None else total + term
                part = part - piece.astype(jnp.float32)
        for p in range(planes):
            grid_ref[p, c] = total[p * rows : (p + 1) * rows]
    pl.semaphore_wait(barrier, refl_count + 1)
    low_copy = pltpu.make_async_remote_copy(
        src_ref=grid_ref.at[planes - 1], dst_ref=halo.at[0], send_sem=halo_send.at[0],
        recv_sem=halo_recv.at[0], device_id=(refl, up), device_id_type=MESH,
    )
    high_copy = pltpu.make_async_remote_copy(
        src_ref=grid_ref.at[0], dst_ref=halo.at[1], send_sem=halo_send.at[1],
        recv_sem=halo_recv.at[1], device_id=(refl, down), device_id_type=MESH,
    )
    low_copy.start()
    high_copy.start()
    row_of = lax.broadcasted_iota(jnp.int32, (rows, width), 0)
    lane_of = lax.broadcasted_iota(jnp.int32, (rows, width), 1)

    def along_y(field):
        after = jnp.where(row_of == rows - 1, 0.0, pltpu.roll(field, rows - 1, 0))
        before = jnp.where(row_of == 0, 0.0, pltpu.roll(field, 1, 0))
        return 0.5 * (after - before)

    def along_w(field):
        after = jnp.where(lane_of == width - 1, 0.0, pltpu.roll(field, width - 1, 1))
        before = jnp.where(lane_of == 0, 0.0, pltpu.roll(field, 1, 1))
        return 0.5 * (after - before)

    mate = refl + 1 - 2 * lax.rem(refl, 2)
    q0, q1, q2 = scalars[0, refl], scalars[1, refl], scalars[2, refl]
    d0 = q0 - scalars[0, mate]
    d1 = q1 - scalars[1, mate]
    d2 = q2 - scalars[2, mate]
    partial = []
    for p in range(planes):
        obj_re, obj_im = obj_ref[p, :, 0, :], obj_ref[p, :, 1, :]
        term_y = obj_re * along_y(grid_ref[p, 1]) - obj_im * along_y(grid_ref[p, 0])
        term_z = obj_re * along_w(grid_ref[p, 1]) - obj_im * along_w(grid_ref[p, 0])
        partial.append((term_y, term_z))
    low_copy.wait_send()
    high_copy.wait_send()
    low_copy.wait_recv()
    high_copy.wait_recv()
    has_low = me > 0
    has_high = me < slab_count - 1
    for p in range(planes):
        obj_re, obj_im = obj_ref[p, :, 0, :], obj_ref[p, :, 1, :]
        grad = []
        for c in range(2):
            ahead = grid_ref[p + 1, c] if p + 1 < planes else jnp.where(has_high, halo[1, c], 0.0)
            behind = grid_ref[p - 1, c] if p > 0 else jnp.where(has_low, halo[0, c], 0.0)
            grad.append(0.5 * (ahead - behind))
        term_x = obj_re * grad[1] - obj_im * grad[0]
        term_y, term_z = partial[p]
        phase_buf[p] = q0 * term_x + q1 * term_y + q2 * term_z
    copies = []
    for step in range(1, refl_count):
        peer = lax.rem(refl + step, refl_count)
        copy = pltpu.make_async_remote_copy(
            src_ref=phase_buf, dst_ref=gathered.at[refl], send_sem=send_sem.at[step],
            recv_sem=recv_sem.at[step], device_id=(peer, me), device_id_type=MESH,
        )
        copy.start()
        copies.append(copy)
    gathered[refl] = phase_buf[...]
    for copy in copies:
        copy.wait_send()
    for step in range(1, refl_count):
        source = lax.rem(refl + refl_count - step, refl_count)
        pltpu.make_async_remote_copy(
            src_ref=phase_buf, dst_ref=gathered.at[source], send_sem=send_sem.at[step],
            recv_sem=recv_sem.at[step], device_id=(source, me), device_id_type=MESH,
        ).wait_recv()
    def weight(r):
        return scalars[0, r] * d0 + scalars[1, r] * d1 + scalars[2, r] * d2

    shift = weight(0) * gathered[0]
    for r in range(1, refl_count):
        shift = shift + weight(r) * gathered[r]
    for p in range(planes):
        obj_re, obj_im = obj_ref[p, :, 0, :], obj_ref[p, :, 1, :]
        new_re = obj_re - 0.5 * (grid_ref[p, 0] - obj_im * shift[p])
        new_im = obj_im - 0.5 * (grid_ref[p, 1] + obj_re * shift[p])
        out_ref[p] = jnp.stack([new_re, new_im], axis=1)


def post_step(scalars, code_row, rows, kernels, obj, slab_count, refl_count):
    planes, rows_per, _, width = obj.shape
    return pl.pallas_call(
        functools.partial(post_kernel, slab_count=slab_count),
        out_shape=jax.ShapeDtypeStruct(obj.shape, jnp.float32),
        in_specs=[pl.BlockSpec(memory_space=pltpu.SMEM)]
        + [pl.BlockSpec(memory_space=pltpu.VMEM)] * 4,
        out_specs=pl.BlockSpec(memory_space=pltpu.VMEM),
        scratch_shapes=[
            pltpu.VMEM((planes, 2, rows_per, width), jnp.float32),
            pltpu.VMEM((2, 2, rows_per, width), jnp.float32),
            pltpu.VMEM((refl_count, planes, rows_per, width), jnp.float32),
            pltpu.VMEM((planes, rows_per, width), jnp.float32),
            pltpu.SemaphoreType.DMA((2,)),
            pltpu.SemaphoreType.DMA((2,)),
            pltpu.SemaphoreType.DMA((refl_count,)),
            pltpu.SemaphoreType.DMA((refl_count,)),
        ],
        compiler_params=pltpu.CompilerParams(collective_id=0, has_side_effects=True),
    )(scalars, code_row, rows, kernels, obj)


def exchange_kernel(
    slot_ref, values_ref, ids_ref, data_out, code_out, data_buf, code_in, data_send, data_recv, code_send,
    code_recv,
):
    count, capacity = data_out.shape[0], data_out.shape[1]
    group = 8 if count >= 16 else count // 2
    groups = count // group
    rows = group * capacity
    me = lax.axis_index("slab")
    refl = lax.axis_index("refl")
    barrier = pltpu.get_barrier_semaphore()

    def greet(step, carry):
        peer = lax.rem(me + step, count)
        pl.semaphore_signal(barrier, 1, device_id=(refl, peer), device_id_type=MESH)
        return carry

    lax.fori_loop(1, count, greet, 0)

    def pack(g):
        target = lax.broadcasted_iota(jnp.int32, (rows, slot_ref.shape[1]), 0) + g * rows
        chosen = (slot_ref[...] == target).astype(jnp.bfloat16)
        sent = jnp.dot(chosen, values_ref[...], preferred_element_type=jnp.float32)
        data_buf[pl.ds(g * group, group)] = sent.astype(jnp.bfloat16).reshape(
            group, capacity, sent.shape[1]
        )
        codes = lax.dot_general(
            ids_ref[...], chosen, (((1,), (1,)), ((), ())), preferred_element_type=jnp.float32
        )
        codes = (codes[0:1] * 8.0 + codes[1:2]).astype(jnp.int32)
        for part in range(group):
            window = (part * capacity) // 128
            code_in[g * group + part] = codes[:, window * 128 : (window + 1) * 128]

    def outgoing(d):
        data = pltpu.make_async_remote_copy(
            src_ref=data_buf.at[d], dst_ref=data_out.at[me], send_sem=data_send.at[d],
            recv_sem=data_recv.at[me], device_id=(refl, d), device_id_type=MESH,
        )
        code = pltpu.make_async_remote_copy(
            src_ref=code_in.at[d], dst_ref=code_out.at[me], send_sem=code_send.at[d],
            recv_sem=code_recv.at[me], device_id=(refl, d), device_id_type=MESH,
        )
        return data, code

    def incoming(s):
        data = pltpu.make_async_remote_copy(
            src_ref=data_buf.at[s], dst_ref=data_out.at[s], send_sem=data_send.at[s],
            recv_sem=data_recv.at[s], device_id=(refl, s), device_id_type=MESH,
        )
        code = pltpu.make_async_remote_copy(
            src_ref=code_in.at[s], dst_ref=code_out.at[s], send_sem=code_send.at[s],
            recv_sem=code_recv.at[s], device_id=(refl, s), device_id_type=MESH,
        )
        return data, code

    def send(g):
        for part in range(group):
            d = g * group + part

            @pl.when(d != me)
            def _():
                data, code = outgoing(d)
                code.start()
                data.start()

    home = me // group
    middle = groups // 2

    def order(j):
        return lax.rem(home + middle + (1 - 2 * lax.rem(j, 2)) * ((j + 1) // 2) + groups, groups)

    first = order(0)
    pack(first)
    pl.semaphore_wait(barrier, count - 1)
    send(first)

    def later(j, carry):
        g = order(j)
        pack(g)
        send(g)
        return carry

    lax.fori_loop(1, groups, later, 0)
    data_out[me] = data_buf[me]
    local = pltpu.make_async_copy(code_in.at[me], code_out.at[me], code_send.at[me])
    local.start()

    def finish(step, carry):
        data, code = outgoing(lax.rem(me + step, count))
        data.wait_send()
        code.wait_send()
        data, code = incoming(lax.rem(me + count - step, count))
        data.wait_recv()
        code.wait_recv()
        return carry

    lax.fori_loop(1, count, finish, 0)
    local.wait()


def exchange_slab(flat_slot, values, ids, count, capacity):
    data_shape = (count, capacity, values.shape[1])
    code_shape = (count, 1, 128)
    return pl.pallas_call(
        exchange_kernel,
        out_shape=(
            jax.ShapeDtypeStruct(data_shape, jnp.bfloat16),
            jax.ShapeDtypeStruct(code_shape, jnp.int32),
        ),
        in_specs=[pl.BlockSpec(memory_space=pltpu.VMEM)] * 3,
        out_specs=(pl.BlockSpec(memory_space=pltpu.VMEM), pl.BlockSpec(memory_space=pl.ANY)),
        scratch_shapes=[
            pltpu.VMEM(data_shape, jnp.bfloat16),
            pltpu.VMEM(code_shape, jnp.int32),
            pltpu.SemaphoreType.DMA((count,)),
            pltpu.SemaphoreType.DMA((count,)),
            pltpu.SemaphoreType.DMA((count,)),
            pltpu.SemaphoreType.DMA((count,)),
        ],
        compiler_params=pltpu.CompilerParams(collective_id=1, has_side_effects=True),
    )(flat_slot, values, ids)


def per_device(detector, owners, block_ids, kernel_ids, kernels, bragg_vectors, object_field):
    slab_count = lax.axis_size("slab")
    plane_count = object_field.shape[1]
    row_count = object_field.shape[2]
    block_count = plane_count * row_count
    kernel_count = kernels.shape[0]
    tile_count = detector.shape[1]
    tile_width = detector.shape[3]
    row_width = 2 * tile_width
    capacity = 2 * tile_count // slab_count
    values = detector[0].reshape(tile_count, row_width)
    owner = owners[0, :, 0]
    order = lax.broadcasted_iota(jnp.int32, (tile_count, tile_count), 1) < lax.broadcasted_iota(
        jnp.int32, (tile_count, tile_count), 0
    )
    same = (owner[:, None] == owner[None, :]) & order
    slots = jnp.sum(same.astype(jnp.int32), axis=1)
    flat_slot = owner * capacity + slots
    ids = jnp.concatenate(
        [block_ids, kernel_ids, jnp.zeros((6, tile_count), jnp.int32)], axis=0
    ).astype(jnp.bfloat16)
    got, got_code = exchange_slab(flat_slot[None, :], values, ids, slab_count, capacity)
    row_total = slab_count * capacity
    rows = got.reshape(row_total, row_width)
    offset = lax.rem(lax.axis_index("slab"), 4) * capacity
    got_codes = lax.dynamic_slice_in_dim(got_code[:, 0, :], offset, capacity, axis=1).reshape(row_total)
    code_row = (lax.rem(got_codes, kernel_count) * block_count + got_codes // kernel_count)[None, :]
    refl_count = bragg_vectors.shape[0]
    obj = object_field[0]
    updated = post_step(bragg_vectors.T, code_row, rows, kernels, obj, slab_count, refl_count)
    return updated[None]


def solution(mesh):
    in_specs = (
        P("refl", "slab", None, None),
        P("refl", "slab", None),
        P("refl", "slab"),
        P("refl", "slab"),
        P(),
        P(),
        P("refl", "slab", None, None, None),
    )
    out_specs = P("refl", "slab", None, None, None)
    return jax.shard_map(
        per_device, mesh=mesh, in_specs=in_specs, out_specs=out_specs, check_vma=False
    )
```

```python
import functools

import jax
import jax.numpy as jnp
from jax import lax
from jax.experimental import pallas as pl
from jax.experimental.pallas import tpu as pltpu
from jax.sharding import PartitionSpec as P

MESH = pl.DeviceIdType.MESH


def extended(block, sides, width):
    for axis, dim in sides:
        count = lax.axis_size(axis)
        forward = [(i, i + 1) for i in range(count - 1)]
        backward = [(target, source) for source, target in forward]
        low = lax.ppermute(
            lax.slice_in_dim(block, block.shape[dim] - width, None, axis=dim), axis, forward
        )
        high = lax.ppermute(lax.slice_in_dim(block, 0, width, axis=dim), axis, backward)
        block = jnp.concatenate([low, block, high], axis=dim)
    return block


def central(field, dimension):
    widths = [(0, 0)] * field.ndim
    widths[dimension] = (1, 1)
    padded = jnp.pad(field, widths)
    length = field.shape[dimension]
    return 0.5 * (
        lax.slice_in_dim(padded, 2, length + 2, axis=dimension)
        - lax.slice_in_dim(padded, 0, length, axis=dimension)
    )


def phase_term(obj_real, obj_imag, grad_x, grad_y, grad_z, qrow):
    term_x = obj_real * grad_x[:, :, 1] - obj_imag * grad_x[:, :, 0]
    term_y = obj_real * grad_y[:, :, 1] - obj_imag * grad_y[:, :, 0]
    term_z = obj_real * grad_z[:, :, 1] - obj_imag * grad_z[:, :, 0]
    return qrow[0] * term_x + qrow[1] * term_y + qrow[2] * term_z


def post_kernel(
    scalars, code_ref, rows_ref, kernels_ref, obj_ref, out_ref, grid_ref, halo, gathered, phase_buf,
    halo_send, halo_recv, send_sem, recv_sem, slab_count,
):
    refl_count = gathered.shape[0]
    planes, rows, width = grid_ref.shape[0], grid_ref.shape[2], grid_ref.shape[3]
    kernel_count = kernels_ref.shape[0]
    blocks = planes * rows
    me = lax.axis_index("slab")
    refl = lax.axis_index("refl")
    up = lax.rem(me + 1, slab_count)
    down = lax.rem(me + slab_count - 1, slab_count)
    barrier = pltpu.get_barrier_semaphore()
    pl.semaphore_signal(barrier, 1, device_id=(refl, up), device_id_type=MESH)
    pl.semaphore_signal(barrier, 1, device_id=(refl, down), device_id_type=MESH)
    for step in range(1, refl_count):
        peer = lax.rem(refl + step, refl_count)
        pl.semaphore_signal(barrier, 1, device_id=(peer, me), device_id_type=MESH)
    chosen = (
        code_ref[...] == lax.broadcasted_iota(jnp.int32, (kernel_count * blocks, code_ref.shape[1]), 0)
    ).astype(jnp.bfloat16)
    summed = jnp.dot(chosen, rows_ref[...], preferred_element_type=jnp.float32)
    for c in range(2):
        total = None
        for k in range(kernel_count):
            part = summed[k * blocks : (k + 1) * blocks, c * width : (c + 1) * width]
            weights = kernels_ref[k]
            for _ in range(3):
                piece = part.astype(jnp.bfloat16)
                term = jnp.dot(piece, weights, preferred_element_type=jnp.float32)
                total = term if total is None else total + term
                part = part - piece.astype(jnp.float32)
        for p in range(planes):
            grid_ref[p, c] = total[p * rows : (p + 1) * rows]
    pl.semaphore_wait(barrier, refl_count + 1)
    low_copy = pltpu.make_async_remote_copy(
        src_ref=grid_ref.at[planes - 1], dst_ref=halo.at[0], send_sem=halo_send.at[0],
        recv_sem=halo_recv.at[0], device_id=(refl, up), device_id_type=MESH,
    )
    high_copy = pltpu.make_async_remote_copy(
        src_ref=grid_ref.at[0], dst_ref=halo.at[1], send_sem=halo_send.at[1],
        recv_sem=halo_recv.at[1], device_id=(refl, down), device_id_type=MESH,
    )
    low_copy.start()
    high_copy.start()
    row_of = lax.broadcasted_iota(jnp.int32, (rows, width), 0)
    lane_of = lax.broadcasted_iota(jnp.int32, (rows, width), 1)

    def along_y(field):
        after = jnp.where(row_of == rows - 1, 0.0, pltpu.roll(field, rows - 1, 0))
        before = jnp.where(row_of == 0, 0.0, pltpu.roll(field, 1, 0))
        return 0.5 * (after - before)

    def along_w(field):
        after = jnp.where(lane_of == width - 1, 0.0, pltpu.roll(field, width - 1, 1))
        before = jnp.where(lane_of == 0, 0.0, pltpu.roll(field, 1, 1))
        return 0.5 * (after - before)

    mate = refl + 1 - 2 * lax.rem(refl, 2)
    q0, q1, q2 = scalars[refl, 0], scalars[refl, 1], scalars[refl, 2]
    d0 = q0 - scalars[mate, 0]
    d1 = q1 - scalars[mate, 1]
    d2 = q2 - scalars[mate, 2]
    partial = []
    for p in range(planes):
        obj_re, obj_im = obj_ref[p, :, 0, :], obj_ref[p, :, 1, :]
        term_y = obj_re * along_y(grid_ref[p, 1]) - obj_im * along_y(grid_ref[p, 0])
        term_z = obj_re * along_w(grid_ref[p, 1]) - obj_im * along_w(grid_ref[p, 0])
        partial.append((term_y, term_z))
    low_copy.wait_send()
    high_copy.wait_send()
    low_copy.wait_recv()
    high_copy.wait_recv()
    has_low = me > 0
    has_high = me < slab_count - 1
    for p in range(planes):
        obj_re, obj_im = obj_ref[p, :, 0, :], obj_ref[p, :, 1, :]
        grad = []
        for c in range(2):
            ahead = grid_ref[p + 1, c] if p + 1 < planes else jnp.where(has_high, halo[1, c], 0.0)
            behind = grid_ref[p - 1, c] if p > 0 else jnp.where(has_low, halo[0, c], 0.0)
            grad.append(0.5 * (ahead - behind))
        term_x = obj_re * grad[1] - obj_im * grad[0]
        term_y, term_z = partial[p]
        phase_buf[p] = q0 * term_x + q1 * term_y + q2 * term_z
    copies = []
    for step in range(1, refl_count):
        peer = lax.rem(refl + step, refl_count)
        copy = pltpu.make_async_remote_copy(
            src_ref=phase_buf, dst_ref=gathered.at[refl], send_sem=send_sem.at[step],
            recv_sem=recv_sem.at[step], device_id=(peer, me), device_id_type=MESH,
        )
        copy.start()
        copies.append(copy)
    gathered[refl] = phase_buf[...]
    for copy in copies:
        copy.wait_send()
    for step in range(1, refl_count):
        source = lax.rem(refl + refl_count - step, refl_count)
        pltpu.make_async_remote_copy(
            src_ref=phase_buf, dst_ref=gathered.at[source], send_sem=send_sem.at[step],
            recv_sem=recv_sem.at[step], device_id=(source, me), device_id_type=MESH,
        ).wait_recv()
    def weight(r):
        return scalars[r, 0] * d0 + scalars[r, 1] * d1 + scalars[r, 2] * d2

    shift = weight(0) * gathered[0]
    for r in range(1, refl_count):
        shift = shift + weight(r) * gathered[r]
    for p in range(planes):
        obj_re, obj_im = obj_ref[p, :, 0, :], obj_ref[p, :, 1, :]
        new_re = obj_re - 0.5 * (grid_ref[p, 0] - obj_im * shift[p])
        new_im = obj_im - 0.5 * (grid_ref[p, 1] + obj_re * shift[p])
        out_ref[p] = jnp.stack([new_re, new_im], axis=1)


def post_step(scalars, code_row, rows, kernels, obj, slab_count, refl_count):
    planes, rows_per, _, width = obj.shape
    return pl.pallas_call(
        functools.partial(post_kernel, slab_count=slab_count),
        out_shape=jax.ShapeDtypeStruct(obj.shape, jnp.float32),
        in_specs=[pl.BlockSpec(memory_space=pltpu.SMEM)]
        + [pl.BlockSpec(memory_space=pltpu.VMEM)] * 4,
        out_specs=pl.BlockSpec(memory_space=pltpu.VMEM),
        scratch_shapes=[
            pltpu.VMEM((planes, 2, rows_per, width), jnp.float32),
            pltpu.VMEM((2, 2, rows_per, width), jnp.float32),
            pltpu.VMEM((refl_count, planes, rows_per, width), jnp.float32),
            pltpu.VMEM((planes, rows_per, width), jnp.float32),
            pltpu.SemaphoreType.DMA((2,)),
            pltpu.SemaphoreType.DMA((2,)),
            pltpu.SemaphoreType.DMA((refl_count,)),
            pltpu.SemaphoreType.DMA((refl_count,)),
        ],
        compiler_params=pltpu.CompilerParams(collective_id=0, has_side_effects=True),
    )(scalars, code_row, rows, kernels, obj)


def exchange_kernel(
    slot_ref, values_ref, ids_ref, data_out, code_out, data_buf, code_in, data_send, data_recv, code_send,
    code_recv,
    block_count,
):
    count, capacity = data_out.shape[0], data_out.shape[1]
    group = 8 if count >= 16 else count // 2
    groups = count // group
    rows = group * capacity
    me = lax.axis_index("slab")
    refl = lax.axis_index("refl")
    barrier = pltpu.get_barrier_semaphore()

    def greet(step, carry):
        peer = lax.rem(me + step, count)
        pl.semaphore_signal(barrier, 1, device_id=(refl, peer), device_id_type=MESH)
        return carry

    lax.fori_loop(1, count, greet, 0)

    def pack(g):
        target = lax.broadcasted_iota(jnp.int32, (rows, slot_ref.shape[1]), 0) + g * rows
        chosen = (slot_ref[...] == target).astype(jnp.bfloat16)
        sent = jnp.dot(chosen, values_ref[...], preferred_element_type=jnp.float32)
        data_buf[pl.ds(g * group, group)] = sent.astype(jnp.bfloat16).reshape(
            group, capacity, sent.shape[1]
        )
        codes = lax.dot_general(
            ids_ref[...], chosen, (((1,), (1,)), ((), ())), preferred_element_type=jnp.float32
        )
        codes = (codes[1:2] * float(block_count) + codes[0:1]).astype(jnp.int32)
        for part in range(group):
            window = (part * capacity) // 128
            code_in[g * group + part] = codes[:, window * 128 : (window + 1) * 128]

    def outgoing(d):
        data = pltpu.make_async_remote_copy(
            src_ref=data_buf.at[d], dst_ref=data_out.at[me], send_sem=data_send.at[d],
            recv_sem=data_recv.at[me], device_id=(refl, d), device_id_type=MESH,
        )
        code = pltpu.make_async_remote_copy(
            src_ref=code_in.at[d], dst_ref=code_out.at[me], send_sem=code_send.at[d],
            recv_sem=code_recv.at[me], device_id=(refl, d), device_id_type=MESH,
        )
        return data, code

    def incoming(s):
        data = pltpu.make_async_remote_copy(
            src_ref=data_buf.at[s], dst_ref=data_out.at[s], send_sem=data_send.at[s],
            recv_sem=data_recv.at[s], device_id=(refl, s), device_id_type=MESH,
        )
        code = pltpu.make_async_remote_copy(
            src_ref=code_in.at[s], dst_ref=code_out.at[s], send_sem=code_send.at[s],
            recv_sem=code_recv.at[s], device_id=(refl, s), device_id_type=MESH,
        )
        return data, code

    def send(g):
        for part in range(group):
            d = g * group + part

            @pl.when(d != me)
            def _():
                data, code = outgoing(d)
                code.start()
                data.start()

    home = me // group
    middle = groups // 2

    def order(j):
        return lax.rem(home + middle + (1 - 2 * lax.rem(j, 2)) * ((j + 1) // 2) + groups, groups)

    first = order(0)
    pack(first)
    pl.semaphore_wait(barrier, count - 1)
    send(first)

    def later(j, carry):
        g = order(j)
        pack(g)
        send(g)
        return carry

    lax.fori_loop(1, groups, later, 0)
    data_out[me] = data_buf[me]
    local = pltpu.make_async_copy(code_in.at[me], code_out.at[me], code_send.at[me])
    local.start()

    def finish(step, carry):
        data, code = outgoing(lax.rem(me + step, count))
        data.wait_send()
        code.wait_send()
        data, code = incoming(lax.rem(me + count - step, count))
        data.wait_recv()
        code.wait_recv()
        return carry

    lax.fori_loop(1, count, finish, 0)
    local.wait()


def exchange_slab(flat_slot, values, ids, count, capacity, block_count):
    data_shape = (count, capacity, values.shape[1])
    code_shape = (count, 1, 128)
    return pl.pallas_call(
        functools.partial(exchange_kernel, block_count=block_count),
        out_shape=(
            jax.ShapeDtypeStruct(data_shape, jnp.bfloat16),
            jax.ShapeDtypeStruct(code_shape, jnp.int32),
        ),
        in_specs=[pl.BlockSpec(memory_space=pltpu.VMEM)] * 3,
        out_specs=(pl.BlockSpec(memory_space=pltpu.VMEM), pl.BlockSpec(memory_space=pl.ANY)),
        scratch_shapes=[
            pltpu.VMEM(data_shape, jnp.bfloat16),
            pltpu.VMEM(code_shape, jnp.int32),
            pltpu.SemaphoreType.DMA((count,)),
            pltpu.SemaphoreType.DMA((count,)),
            pltpu.SemaphoreType.DMA((count,)),
            pltpu.SemaphoreType.DMA((count,)),
        ],
        compiler_params=pltpu.CompilerParams(collective_id=1, has_side_effects=True),
    )(flat_slot, values, ids)


def per_device(detector, owners, block_ids, kernel_ids, kernels, bragg_vectors, object_field):
    slab_count = lax.axis_size("slab")
    plane_count = object_field.shape[1]
    row_count = object_field.shape[2]
    block_count = plane_count * row_count
    kernel_count = kernels.shape[0]
    tile_count = detector.shape[1]
    tile_width = detector.shape[3]
    row_width = 2 * tile_width
    capacity = 2 * tile_count // slab_count
    values = detector[0].reshape(tile_count, row_width)
    owner = owners[0, :, 0]
    order = lax.broadcasted_iota(jnp.int32, (tile_count, tile_count), 1) < lax.broadcasted_iota(
        jnp.int32, (tile_count, tile_count), 0
    )
    same = (owner[:, None] == owner[None, :]) & order
    slots = jnp.sum(same.astype(jnp.int32), axis=1)
    flat_slot = owner * capacity + slots
    ids = jnp.concatenate(
        [block_ids, kernel_ids, jnp.zeros((6, tile_count), jnp.int32)], axis=0
    ).astype(jnp.bfloat16)
    got, got_code = exchange_slab(flat_slot[None, :], values, ids, slab_count, capacity, block_count)
    row_total = slab_count * capacity
    rows = got.reshape(row_total, row_width)
    offset = lax.rem(lax.axis_index("slab"), 4) * capacity
    got_codes = lax.dynamic_slice_in_dim(got_code[:, 0, :], offset, capacity, axis=1).reshape(row_total)
    code_row = got_codes[None, :]
    refl_count = bragg_vectors.shape[0]
    obj = object_field[0]
    updated = post_step(bragg_vectors, code_row, rows, kernels, obj, slab_count, refl_count)
    return updated[None]


def solution(mesh):
    in_specs = (
        P("refl", "slab", None, None),
        P("refl", "slab", None),
        P("refl", "slab"),
        P("refl", "slab"),
        P(),
        P(),
        P("refl", "slab", None, None, None),
    )
    out_specs = P("refl", "slab", None, None, None)
    return jax.shard_map(
        per_device, mesh=mesh, in_specs=in_specs, out_specs=out_specs, check_vma=False
    )
```

```python
import functools

import jax
import jax.numpy as jnp
from jax import lax
from jax.experimental import pallas as pl
from jax.experimental.pallas import tpu as pltpu
from jax.sharding import PartitionSpec as P

MESH = pl.DeviceIdType.MESH


def extended(block, sides, width):
    for axis, dim in sides:
        count = lax.axis_size(axis)
        forward = [(i, i + 1) for i in range(count - 1)]
        backward = [(target, source) for source, target in forward]
        low = lax.ppermute(
            lax.slice_in_dim(block, block.shape[dim] - width, None, axis=dim), axis, forward
        )
        high = lax.ppermute(lax.slice_in_dim(block, 0, width, axis=dim), axis, backward)
        block = jnp.concatenate([low, block, high], axis=dim)
    return block


def central(field, dimension):
    widths = [(0, 0)] * field.ndim
    widths[dimension] = (1, 1)
    padded = jnp.pad(field, widths)
    length = field.shape[dimension]
    return 0.5 * (
        lax.slice_in_dim(padded, 2, length + 2, axis=dimension)
        - lax.slice_in_dim(padded, 0, length, axis=dimension)
    )


def phase_term(obj_real, obj_imag, grad_x, grad_y, grad_z, qrow):
    term_x = obj_real * grad_x[:, :, 1] - obj_imag * grad_x[:, :, 0]
    term_y = obj_real * grad_y[:, :, 1] - obj_imag * grad_y[:, :, 0]
    term_z = obj_real * grad_z[:, :, 1] - obj_imag * grad_z[:, :, 0]
    return qrow[0] * term_x + qrow[1] * term_y + qrow[2] * term_z


def post_kernel(
    scalars, code_ref, rows_ref, kernels_ref, obj_ref, out_ref, grid_ref, halo, gathered, phase_buf,
    halo_send, halo_recv, send_sem, recv_sem, slab_count,
):
    refl_count = gathered.shape[0]
    planes, rows, width = grid_ref.shape[0], grid_ref.shape[2], grid_ref.shape[3]
    kernel_count = kernels_ref.shape[0]
    blocks = planes * rows
    me = lax.axis_index("slab")
    refl = lax.axis_index("refl")
    up = lax.rem(me + 1, slab_count)
    down = lax.rem(me + slab_count - 1, slab_count)
    barrier = pltpu.get_barrier_semaphore()
    pl.semaphore_signal(barrier, 1, device_id=(refl, up), device_id_type=MESH)
    pl.semaphore_signal(barrier, 1, device_id=(refl, down), device_id_type=MESH)
    for step in range(1, refl_count):
        peer = lax.rem(refl + step, refl_count)
        pl.semaphore_signal(barrier, 1, device_id=(peer, me), device_id_type=MESH)
    chosen = (
        code_ref[...] == lax.broadcasted_iota(jnp.int32, (kernel_count * blocks, code_ref.shape[1]), 0)
    ).astype(jnp.bfloat16)
    summed = jnp.dot(chosen, rows_ref[...], preferred_element_type=jnp.float32)
    for c in range(2):
        total = None
        for k in range(kernel_count):
            part = summed[k * blocks : (k + 1) * blocks, c * width : (c + 1) * width]
            weights = kernels_ref[k]
            for _ in range(3):
                piece = part.astype(jnp.bfloat16)
                term = jnp.dot(piece, weights, preferred_element_type=jnp.float32)
                total = term if total is None else total + term
                part = part - piece.astype(jnp.float32)
        for p in range(planes):
            grid_ref[p, c] = total[p * rows : (p + 1) * rows]
    pl.semaphore_wait(barrier, refl_count + 1)
    low_copy = pltpu.make_async_remote_copy(
        src_ref=grid_ref.at[planes - 1], dst_ref=halo.at[0], send_sem=halo_send.at[0],
        recv_sem=halo_recv.at[0], device_id=(refl, up), device_id_type=MESH,
    )
    high_copy = pltpu.make_async_remote_copy(
        src_ref=grid_ref.at[0], dst_ref=halo.at[1], send_sem=halo_send.at[1],
        recv_sem=halo_recv.at[1], device_id=(refl, down), device_id_type=MESH,
    )
    low_copy.start()
    high_copy.start()
    row_of = lax.broadcasted_iota(jnp.int32, (rows, width), 0)
    lane_of = lax.broadcasted_iota(jnp.int32, (rows, width), 1)

    def along_y(field):
        after = jnp.where(row_of == rows - 1, 0.0, pltpu.roll(field, rows - 1, 0))
        before = jnp.where(row_of == 0, 0.0, pltpu.roll(field, 1, 0))
        return 0.5 * (after - before)

    def along_w(field):
        after = jnp.where(lane_of == width - 1, 0.0, pltpu.roll(field, width - 1, 1))
        before = jnp.where(lane_of == 0, 0.0, pltpu.roll(field, 1, 1))
        return 0.5 * (after - before)

    mate = refl + 1 - 2 * lax.rem(refl, 2)
    q0, q1, q2 = scalars[0, refl], scalars[1, refl], scalars[2, refl]
    d0 = q0 - scalars[0, mate]
    d1 = q1 - scalars[1, mate]
    d2 = q2 - scalars[2, mate]
    partial = []
    for p in range(planes):
        obj_re, obj_im = obj_ref[p, :, 0, :], obj_ref[p, :, 1, :]
        term_y = obj_re * along_y(grid_ref[p, 1]) - obj_im * along_y(grid_ref[p, 0])
        term_z = obj_re * along_w(grid_ref[p, 1]) - obj_im * along_w(grid_ref[p, 0])
        partial.append((term_y, term_z))
    low_copy.wait_send()
    high_copy.wait_send()
    low_copy.wait_recv()
    high_copy.wait_recv()
    has_low = me > 0
    has_high = me < slab_count - 1
    for p in range(planes):
        obj_re, obj_im = obj_ref[p, :, 0, :], obj_ref[p, :, 1, :]
        grad = []
        for c in range(2):
            ahead = grid_ref[p + 1, c] if p + 1 < planes else jnp.where(has_high, halo[1, c], 0.0)
            behind = grid_ref[p - 1, c] if p > 0 else jnp.where(has_low, halo[0, c], 0.0)
            grad.append(0.5 * (ahead - behind))
        term_x = obj_re * grad[1] - obj_im * grad[0]
        term_y, term_z = partial[p]
        phase_buf[p] = q0 * term_x + q1 * term_y + q2 * term_z
    copies = []
    for step in range(1, refl_count):
        peer = lax.rem(refl + step, refl_count)
        copy = pltpu.make_async_remote_copy(
            src_ref=phase_buf, dst_ref=gathered.at[refl], send_sem=send_sem.at[step],
            recv_sem=recv_sem.at[step], device_id=(peer, me), device_id_type=MESH,
        )
        copy.start()
        copies.append(copy)
    gathered[refl] = phase_buf[...]
    for copy in copies:
        copy.wait_send()
    for step in range(1, refl_count):
        source = lax.rem(refl + refl_count - step, refl_count)
        pltpu.make_async_remote_copy(
            src_ref=phase_buf, dst_ref=gathered.at[source], send_sem=send_sem.at[step],
            recv_sem=recv_sem.at[step], device_id=(source, me), device_id_type=MESH,
        ).wait_recv()
    def weight(r):
        return scalars[0, r] * d0 + scalars[1, r] * d1 + scalars[2, r] * d2

    shift = weight(0) * gathered[0]
    for r in range(1, refl_count):
        shift = shift + weight(r) * gathered[r]
    for p in range(planes):
        obj_re, obj_im = obj_ref[p, :, 0, :], obj_ref[p, :, 1, :]
        new_re = obj_re - 0.5 * (grid_ref[p, 0] - obj_im * shift[p])
        new_im = obj_im - 0.5 * (grid_ref[p, 1] + obj_re * shift[p])
        out_ref[p] = jnp.stack([new_re, new_im], axis=1)


def post_step(scalars, code_row, rows, kernels, obj, slab_count, refl_count):
    planes, rows_per, _, width = obj.shape
    return pl.pallas_call(
        functools.partial(post_kernel, slab_count=slab_count),
        out_shape=jax.ShapeDtypeStruct(obj.shape, jnp.float32),
        in_specs=[pl.BlockSpec(memory_space=pltpu.SMEM)]
        + [pl.BlockSpec(memory_space=pltpu.VMEM)] * 4,
        out_specs=pl.BlockSpec(memory_space=pltpu.VMEM),
        scratch_shapes=[
            pltpu.VMEM((planes, 2, rows_per, width), jnp.float32),
            pltpu.VMEM((2, 2, rows_per, width), jnp.float32),
            pltpu.VMEM((refl_count, planes, rows_per, width), jnp.float32),
            pltpu.VMEM((planes, rows_per, width), jnp.float32),
            pltpu.SemaphoreType.DMA((2,)),
            pltpu.SemaphoreType.DMA((2,)),
            pltpu.SemaphoreType.DMA((refl_count,)),
            pltpu.SemaphoreType.DMA((refl_count,)),
        ],
        compiler_params=pltpu.CompilerParams(collective_id=0, has_side_effects=True),
    )(scalars, code_row, rows, kernels, obj)


def exchange_kernel(
    slot_ref, values_ref, ids_ref, data_out, code_out, data_buf, code_in, data_send, data_recv, code_send,
    code_recv,
    block_count,
):
    count, capacity = data_out.shape[0], data_out.shape[1]
    group = 8 if count >= 16 else count // 2
    groups = count // group
    rows = group * capacity
    me = lax.axis_index("slab")
    refl = lax.axis_index("refl")
    barrier = pltpu.get_barrier_semaphore()

    def greet(step, carry):
        peer = lax.rem(me + step, count)
        pl.semaphore_signal(barrier, 1, device_id=(refl, peer), device_id_type=MESH)
        return carry

    lax.fori_loop(1, count, greet, 0)

    def pack(g):
        target = lax.broadcasted_iota(jnp.int32, (rows, slot_ref.shape[1]), 0) + g * rows
        chosen = (slot_ref[...] == target).astype(jnp.bfloat16)
        sent = jnp.dot(chosen, values_ref[...], preferred_element_type=jnp.float32)
        data_buf[pl.ds(g * group, group)] = sent.astype(jnp.bfloat16).reshape(
            group, capacity, sent.shape[1]
        )
        codes = lax.dot_general(
            ids_ref[...], chosen, (((1,), (1,)), ((), ())), preferred_element_type=jnp.float32
        )
        codes = (codes[1:2] * float(block_count) + codes[0:1]).astype(jnp.int32)
        for part in range(group):
            window = (part * capacity) // 128
            code_in[g * group + part] = codes[:, window * 128 : (window + 1) * 128]

    def outgoing(d):
        data = pltpu.make_async_remote_copy(
            src_ref=data_buf.at[d], dst_ref=data_out.at[me], send_sem=data_send.at[d],
            recv_sem=data_recv.at[me], device_id=(refl, d), device_id_type=MESH,
        )
        code = pltpu.make_async_remote_copy(
            src_ref=code_in.at[d], dst_ref=code_out.at[me], send_sem=code_send.at[d],
            recv_sem=code_recv.at[me], device_id=(refl, d), device_id_type=MESH,
        )
        return data, code

    def incoming(s):
        data = pltpu.make_async_remote_copy(
            src_ref=data_buf.at[s], dst_ref=data_out.at[s], send_sem=data_send.at[s],
            recv_sem=data_recv.at[s], device_id=(refl, s), device_id_type=MESH,
        )
        code = pltpu.make_async_remote_copy(
            src_ref=code_in.at[s], dst_ref=code_out.at[s], send_sem=code_send.at[s],
            recv_sem=code_recv.at[s], device_id=(refl, s), device_id_type=MESH,
        )
        return data, code

    def send(g):
        for part in range(group):
            d = g * group + part

            @pl.when(d != me)
            def _():
                data, code = outgoing(d)
                code.start()
                data.start()

    home = me // group
    middle = groups // 2

    def order(j):
        return lax.rem(home + middle + (1 - 2 * lax.rem(j, 2)) * ((j + 1) // 2) + groups, groups)

    first = order(0)
    pack(first)
    pl.semaphore_wait(barrier, count - 1)
    send(first)

    def later(j, carry):
        g = order(j)
        pack(g)
        send(g)
        return carry

    lax.fori_loop(1, groups, later, 0)
    data_out[me] = data_buf[me]
    local = pltpu.make_async_copy(code_in.at[me], code_out.at[me], code_send.at[me])
    local.start()

    def finish(step, carry):
        data, code = outgoing(lax.rem(me + step, count))
        data.wait_send()
        code.wait_send()
        data, code = incoming(lax.rem(me + count - step, count))
        data.wait_recv()
        code.wait_recv()
        return carry

    lax.fori_loop(1, count, finish, 0)
    local.wait()


def exchange_slab(flat_slot, values, ids, count, capacity, block_count):
    data_shape = (count, capacity, values.shape[1])
    code_shape = (count, 1, 128)
    return pl.pallas_call(
        functools.partial(exchange_kernel, block_count=block_count),
        out_shape=(
            jax.ShapeDtypeStruct(data_shape, jnp.bfloat16),
            jax.ShapeDtypeStruct(code_shape, jnp.int32),
        ),
        in_specs=[pl.BlockSpec(memory_space=pltpu.VMEM)] * 3,
        out_specs=(pl.BlockSpec(memory_space=pltpu.VMEM), pl.BlockSpec(memory_space=pl.ANY)),
        scratch_shapes=[
            pltpu.VMEM(data_shape, jnp.bfloat16),
            pltpu.VMEM(code_shape, jnp.int32),
            pltpu.SemaphoreType.DMA((count,)),
            pltpu.SemaphoreType.DMA((count,)),
            pltpu.SemaphoreType.DMA((count,)),
            pltpu.SemaphoreType.DMA((count,)),
        ],
        compiler_params=pltpu.CompilerParams(collective_id=1, has_side_effects=True),
    )(flat_slot, values, ids)


def per_device(detector, owners, block_ids, kernel_ids, kernels, bragg_vectors, object_field):
    slab_count = lax.axis_size("slab")
    plane_count = object_field.shape[1]
    row_count = object_field.shape[2]
    block_count = plane_count * row_count
    kernel_count = kernels.shape[0]
    tile_count = detector.shape[1]
    tile_width = detector.shape[3]
    row_width = 2 * tile_width
    capacity = 2 * tile_count // slab_count
    values = detector[0].reshape(tile_count, row_width)
    owner = owners[0, :, 0]
    order = lax.broadcasted_iota(jnp.int32, (tile_count, tile_count), 1) < lax.broadcasted_iota(
        jnp.int32, (tile_count, tile_count), 0
    )
    same = (owner[:, None] == owner[None, :]) & order
    slots = jnp.sum(same.astype(jnp.int32), axis=1)
    flat_slot = owner * capacity + slots
    ids = jnp.concatenate(
        [block_ids, kernel_ids, jnp.zeros((6, tile_count), jnp.int32)], axis=0
    ).astype(jnp.bfloat16)
    got, got_code = exchange_slab(flat_slot[None, :], values, ids, slab_count, capacity, block_count)
    row_total = slab_count * capacity
    rows = got.reshape(row_total, row_width)
    offset = lax.rem(lax.axis_index("slab"), 4) * capacity
    got_codes = lax.dynamic_slice_in_dim(got_code[:, 0, :], offset, capacity, axis=1).reshape(row_total)
    code_row = got_codes[None, :]
    refl_count = bragg_vectors.shape[0]
    obj = object_field[0]
    updated = post_step(bragg_vectors.T, code_row, rows, kernels, obj, slab_count, refl_count)
    return updated[None]


def solution(mesh):
    in_specs = (
        P("refl", "slab", None, None),
        P("refl", "slab", None),
        P("refl", "slab"),
        P("refl", "slab"),
        P(),
        P(),
        P("refl", "slab", None, None, None),
    )
    out_specs = P("refl", "slab", None, None, None)
    return jax.shard_map(
        per_device, mesh=mesh, in_specs=in_specs, out_specs=out_specs, check_vma=False
    )
```

```python
import functools

import jax
import jax.numpy as jnp
from jax import lax
from jax.experimental import pallas as pl
from jax.experimental.pallas import tpu as pltpu
from jax.sharding import PartitionSpec as P

MESH = pl.DeviceIdType.MESH


def extended(block, sides, width):
    for axis, dim in sides:
        count = lax.axis_size(axis)
        forward = [(i, i + 1) for i in range(count - 1)]
        backward = [(target, source) for source, target in forward]
        low = lax.ppermute(
            lax.slice_in_dim(block, block.shape[dim] - width, None, axis=dim), axis, forward
        )
        high = lax.ppermute(lax.slice_in_dim(block, 0, width, axis=dim), axis, backward)
        block = jnp.concatenate([low, block, high], axis=dim)
    return block


def central(field, dimension):
    widths = [(0, 0)] * field.ndim
    widths[dimension] = (1, 1)
    padded = jnp.pad(field, widths)
    length = field.shape[dimension]
    return 0.5 * (
        lax.slice_in_dim(padded, 2, length + 2, axis=dimension)
        - lax.slice_in_dim(padded, 0, length, axis=dimension)
    )


def phase_term(obj_real, obj_imag, grad_x, grad_y, grad_z, qrow):
    term_x = obj_real * grad_x[:, :, 1] - obj_imag * grad_x[:, :, 0]
    term_y = obj_real * grad_y[:, :, 1] - obj_imag * grad_y[:, :, 0]
    term_z = obj_real * grad_z[:, :, 1] - obj_imag * grad_z[:, :, 0]
    return qrow[0] * term_x + qrow[1] * term_y + qrow[2] * term_z


def post_kernel(
    scalars, code_ref, rows_ref, kernels_ref, obj_ref, out_ref, grid_ref, halo, gathered, phase_buf,
    halo_send, halo_recv, send_sem, recv_sem, slab_count,
):
    refl_count = gathered.shape[0]
    planes, rows, width = grid_ref.shape[0], grid_ref.shape[2], grid_ref.shape[3]
    kernel_count = kernels_ref.shape[0]
    blocks = planes * rows
    me = lax.axis_index("slab")
    refl = lax.axis_index("refl")
    up = lax.rem(me + 1, slab_count)
    down = lax.rem(me + slab_count - 1, slab_count)
    barrier = pltpu.get_barrier_semaphore()
    pl.semaphore_signal(barrier, 1, device_id=(refl, up), device_id_type=MESH)
    pl.semaphore_signal(barrier, 1, device_id=(refl, down), device_id_type=MESH)
    for step in range(1, refl_count):
        peer = lax.rem(refl + step, refl_count)
        pl.semaphore_signal(barrier, 1, device_id=(peer, me), device_id_type=MESH)
    chosen = (
        code_ref[...] == lax.broadcasted_iota(jnp.int32, (kernel_count * blocks, code_ref.shape[1]), 0)
    ).astype(jnp.bfloat16)
    summed = jnp.dot(chosen, rows_ref[...], preferred_element_type=jnp.float32)

    def grid_plane(p):
        for c in range(2):
            total = None
            for k in range(kernel_count):
                start = k * blocks + p * rows
                part = summed[start : start + rows, c * width : (c + 1) * width]
                weights = kernels_ref[k]
                for _ in range(3):
                    piece = part.astype(jnp.bfloat16)
                    term = jnp.dot(piece, weights, preferred_element_type=jnp.float32)
                    total = term if total is None else total + term
                    part = part - piece.astype(jnp.float32)
            grid_ref[p, c] = total

    low_copy = pltpu.make_async_remote_copy(
        src_ref=grid_ref.at[planes - 1], dst_ref=halo.at[0], send_sem=halo_send.at[0],
        recv_sem=halo_recv.at[0], device_id=(refl, up), device_id_type=MESH,
    )
    high_copy = pltpu.make_async_remote_copy(
        src_ref=grid_ref.at[0], dst_ref=halo.at[1], send_sem=halo_send.at[1],
        recv_sem=halo_recv.at[1], device_id=(refl, down), device_id_type=MESH,
    )
    grid_plane(0)
    pl.semaphore_wait(barrier, refl_count + 1)
    high_copy.start()
    for p in range(1, planes):
        grid_plane(p)
    low_copy.start()
    row_of = lax.broadcasted_iota(jnp.int32, (rows, width), 0)
    lane_of = lax.broadcasted_iota(jnp.int32, (rows, width), 1)

    def along_y(field):
        after = jnp.where(row_of == rows - 1, 0.0, pltpu.roll(field, rows - 1, 0))
        before = jnp.where(row_of == 0, 0.0, pltpu.roll(field, 1, 0))
        return 0.5 * (after - before)

    def along_w(field):
        after = jnp.where(lane_of == width - 1, 0.0, pltpu.roll(field, width - 1, 1))
        before = jnp.where(lane_of == 0, 0.0, pltpu.roll(field, 1, 1))
        return 0.5 * (after - before)

    mate = refl + 1 - 2 * lax.rem(refl, 2)
    q0, q1, q2 = scalars[refl, 0], scalars[refl, 1], scalars[refl, 2]
    d0 = q0 - scalars[mate, 0]
    d1 = q1 - scalars[mate, 1]
    d2 = q2 - scalars[mate, 2]
    partial = []
    for p in range(planes):
        obj_re, obj_im = obj_ref[p, :, 0, :], obj_ref[p, :, 1, :]
        term_y = obj_re * along_y(grid_ref[p, 1]) - obj_im * along_y(grid_ref[p, 0])
        term_z = obj_re * along_w(grid_ref[p, 1]) - obj_im * along_w(grid_ref[p, 0])
        partial.append((term_y, term_z))
    low_copy.wait_send()
    high_copy.wait_send()
    low_copy.wait_recv()
    high_copy.wait_recv()
    has_low = me > 0
    has_high = me < slab_count - 1
    for p in range(planes):
        obj_re, obj_im = obj_ref[p, :, 0, :], obj_ref[p, :, 1, :]
        grad = []
        for c in range(2):
            ahead = grid_ref[p + 1, c] if p + 1 < planes else jnp.where(has_high, halo[1, c], 0.0)
            behind = grid_ref[p - 1, c] if p > 0 else jnp.where(has_low, halo[0, c], 0.0)
            grad.append(0.5 * (ahead - behind))
        term_x = obj_re * grad[1] - obj_im * grad[0]
        term_y, term_z = partial[p]
        phase_buf[p] = q0 * term_x + q1 * term_y + q2 * term_z
    copies = []
    for step in range(1, refl_count):
        peer = lax.rem(refl + step, refl_count)
        copy = pltpu.make_async_remote_copy(
            src_ref=phase_buf, dst_ref=gathered.at[refl], send_sem=send_sem.at[step],
            recv_sem=recv_sem.at[step], device_id=(peer, me), device_id_type=MESH,
        )
        copy.start()
        copies.append(copy)
    gathered[refl] = phase_buf[...]
    for copy in copies:
        copy.wait_send()
    for step in range(1, refl_count):
        source = lax.rem(refl + refl_count - step, refl_count)
        pltpu.make_async_remote_copy(
            src_ref=phase_buf, dst_ref=gathered.at[source], send_sem=send_sem.at[step],
            recv_sem=recv_sem.at[step], device_id=(source, me), device_id_type=MESH,
        ).wait_recv()
    def weight(r):
        return scalars[r, 0] * d0 + scalars[r, 1] * d1 + scalars[r, 2] * d2

    shift = weight(0) * gathered[0]
    for r in range(1, refl_count):
        shift = shift + weight(r) * gathered[r]
    for p in range(planes):
        obj_re, obj_im = obj_ref[p, :, 0, :], obj_ref[p, :, 1, :]
        new_re = obj_re - 0.5 * (grid_ref[p, 0] - obj_im * shift[p])
        new_im = obj_im - 0.5 * (grid_ref[p, 1] + obj_re * shift[p])
        out_ref[p] = jnp.stack([new_re, new_im], axis=1)


def post_step(scalars, code_row, rows, kernels, obj, slab_count, refl_count):
    planes, rows_per, _, width = obj.shape
    return pl.pallas_call(
        functools.partial(post_kernel, slab_count=slab_count),
        out_shape=jax.ShapeDtypeStruct(obj.shape, jnp.float32),
        in_specs=[pl.BlockSpec(memory_space=pltpu.SMEM)]
        + [pl.BlockSpec(memory_space=pltpu.VMEM)] * 4,
        out_specs=pl.BlockSpec(memory_space=pltpu.VMEM),
        scratch_shapes=[
            pltpu.VMEM((planes, 2, rows_per, width), jnp.float32),
            pltpu.VMEM((2, 2, rows_per, width), jnp.float32),
            pltpu.VMEM((refl_count, planes, rows_per, width), jnp.float32),
            pltpu.VMEM((planes, rows_per, width), jnp.float32),
            pltpu.SemaphoreType.DMA((2,)),
            pltpu.SemaphoreType.DMA((2,)),
            pltpu.SemaphoreType.DMA((refl_count,)),
            pltpu.SemaphoreType.DMA((refl_count,)),
        ],
        compiler_params=pltpu.CompilerParams(collective_id=0, has_side_effects=True),
    )(scalars, code_row, rows, kernels, obj)


def exchange_kernel(
    slot_ref, values_ref, ids_ref, data_out, code_out, data_buf, code_in, data_send, data_recv, code_send,
    code_recv,
):
    count, capacity = data_out.shape[0], data_out.shape[1]
    group = 8 if count >= 16 else count // 2
    groups = count // group
    rows = group * capacity
    me = lax.axis_index("slab")
    refl = lax.axis_index("refl")
    barrier = pltpu.get_barrier_semaphore()

    def greet(step, carry):
        peer = lax.rem(me + step, count)
        pl.semaphore_signal(barrier, 1, device_id=(refl, peer), device_id_type=MESH)
        return carry

    lax.fori_loop(1, count, greet, 0)

    def pack(g):
        target = lax.broadcasted_iota(jnp.int32, (rows, slot_ref.shape[1]), 0) + g * rows
        chosen = (slot_ref[...] == target).astype(jnp.bfloat16)
        sent = jnp.dot(chosen, values_ref[...], preferred_element_type=jnp.float32)
        data_buf[pl.ds(g * group, group)] = sent.astype(jnp.bfloat16).reshape(
            group, capacity, sent.shape[1]
        )
        codes = lax.dot_general(
            ids_ref[...], chosen, (((1,), (1,)), ((), ())), preferred_element_type=jnp.float32
        )
        codes = (codes[0:1] * 8.0 + codes[1:2]).astype(jnp.int32)
        for part in range(group):
            window = (part * capacity) // 128
            code_in[g * group + part] = codes[:, window * 128 : (window + 1) * 128]

    def outgoing(d):
        data = pltpu.make_async_remote_copy(
            src_ref=data_buf.at[d], dst_ref=data_out.at[me], send_sem=data_send.at[d],
            recv_sem=data_recv.at[me], device_id=(refl, d), device_id_type=MESH,
        )
        code = pltpu.make_async_remote_copy(
            src_ref=code_in.at[d], dst_ref=code_out.at[me], send_sem=code_send.at[d],
            recv_sem=code_recv.at[me], device_id=(refl, d), device_id_type=MESH,
        )
        return data, code

    def incoming(s):
        data = pltpu.make_async_remote_copy(
            src_ref=data_buf.at[s], dst_ref=data_out.at[s], send_sem=data_send.at[s],
            recv_sem=data_recv.at[s], device_id=(refl, s), device_id_type=MESH,
        )
        code = pltpu.make_async_remote_copy(
            src_ref=code_in.at[s], dst_ref=code_out.at[s], send_sem=code_send.at[s],
            recv_sem=code_recv.at[s], device_id=(refl, s), device_id_type=MESH,
        )
        return data, code

    def send(g):
        for part in range(group):
            d = g * group + part

            @pl.when(d != me)
            def _():
                data, code = outgoing(d)
                code.start()
                data.start()

    home = me // group
    middle = groups // 2

    def order(j):
        return lax.rem(home + middle + (1 - 2 * lax.rem(j, 2)) * ((j + 1) // 2) + groups, groups)

    first = order(0)
    pack(first)
    pl.semaphore_wait(barrier, count - 1)
    send(first)

    def later(j, carry):
        g = order(j)
        pack(g)
        send(g)
        return carry

    lax.fori_loop(1, groups, later, 0)
    data_out[me] = data_buf[me]
    local = pltpu.make_async_copy(code_in.at[me], code_out.at[me], code_send.at[me])
    local.start()

    def finish(step, carry):
        data, code = outgoing(lax.rem(me + step, count))
        data.wait_send()
        code.wait_send()
        data, code = incoming(lax.rem(me + count - step, count))
        data.wait_recv()
        code.wait_recv()
        return carry

    lax.fori_loop(1, count, finish, 0)
    local.wait()


def exchange_slab(flat_slot, values, ids, count, capacity):
    data_shape = (count, capacity, values.shape[1])
    code_shape = (count, 1, 128)
    return pl.pallas_call(
        exchange_kernel,
        out_shape=(
            jax.ShapeDtypeStruct(data_shape, jnp.bfloat16),
            jax.ShapeDtypeStruct(code_shape, jnp.int32),
        ),
        in_specs=[pl.BlockSpec(memory_space=pltpu.VMEM)] * 3,
        out_specs=(pl.BlockSpec(memory_space=pltpu.VMEM), pl.BlockSpec(memory_space=pl.ANY)),
        scratch_shapes=[
            pltpu.VMEM(data_shape, jnp.bfloat16),
            pltpu.VMEM(code_shape, jnp.int32),
            pltpu.SemaphoreType.DMA((count,)),
            pltpu.SemaphoreType.DMA((count,)),
            pltpu.SemaphoreType.DMA((count,)),
            pltpu.SemaphoreType.DMA((count,)),
        ],
        compiler_params=pltpu.CompilerParams(collective_id=1, has_side_effects=True),
    )(flat_slot, values, ids)


def per_device(detector, owners, block_ids, kernel_ids, kernels, bragg_vectors, object_field):
    slab_count = lax.axis_size("slab")
    plane_count = object_field.shape[1]
    row_count = object_field.shape[2]
    block_count = plane_count * row_count
    kernel_count = kernels.shape[0]
    tile_count = detector.shape[1]
    tile_width = detector.shape[3]
    row_width = 2 * tile_width
    capacity = 2 * tile_count // slab_count
    values = detector[0].reshape(tile_count, row_width)
    owner = owners[0, :, 0]
    order = lax.broadcasted_iota(jnp.int32, (tile_count, tile_count), 1) < lax.broadcasted_iota(
        jnp.int32, (tile_count, tile_count), 0
    )
    same = (owner[:, None] == owner[None, :]) & order
    slots = jnp.sum(same.astype(jnp.int32), axis=1)
    flat_slot = owner * capacity + slots
    ids = jnp.concatenate(
        [block_ids, kernel_ids, jnp.zeros((6, tile_count), jnp.int32)], axis=0
    ).astype(jnp.bfloat16)
    got, got_code = exchange_slab(flat_slot[None, :], values, ids, slab_count, capacity)
    row_total = slab_count * capacity
    rows = got.reshape(row_total, row_width)
    offset = lax.rem(lax.axis_index("slab"), 4) * capacity
    got_codes = lax.dynamic_slice_in_dim(got_code[:, 0, :], offset, capacity, axis=1).reshape(row_total)
    code_row = (lax.rem(got_codes, kernel_count) * block_count + got_codes // kernel_count)[None, :]
    refl_count = bragg_vectors.shape[0]
    obj = object_field[0]
    updated = post_step(bragg_vectors, code_row, rows, kernels, obj, slab_count, refl_count)
    return updated[None]


def solution(mesh):
    in_specs = (
        P("refl", "slab", None, None),
        P("refl", "slab", None),
        P("refl", "slab"),
        P("refl", "slab"),
        P(),
        P(),
        P("refl", "slab", None, None, None),
    )
    out_specs = P("refl", "slab", None, None, None)
    return jax.shard_map(
        per_device, mesh=mesh, in_specs=in_specs, out_specs=out_specs, check_vma=False
    )
```
